32 devices in a mesh: groups: 2 (over y), seq: 4 (over z), dp: 2 (over x), fsdp: 2 (over core).
Axes of the slice: x: 2, y: 2, z: 4, core: 2. Of those that a mesh axis runs over, the one named last changes fastest.
Arguments:
- tokens: bfloat16 [8, 4, 8, 16, 1024], P(('groups', 'dp', 'fsdp'), 'seq'), parts along dimension 0, may hold values from -6 to 6
- timesteps: int32 [8], P(('groups', 'dp', 'fsdp')), parts along dimension 0, may hold values from 0 to 999
- pxrd_mod: float32 [8, 3, 1024], P(('groups', 'dp', 'fsdp')), parts along dimension 0, may hold values from -3 to 3
- time_weight: bfloat16 [256, 3072], P('fsdp'), may hold values from -0.375 to 0.375
- conv_kernel: float32 [27, 1024], replicated, may hold values from -0.9 to 0.9
- qkv_weight: bfloat16 [1024, 1536], P('fsdp'), may hold values from -0.75 to 0.75
- out_weight: bfloat16 [512, 1024], P('fsdp'), may hold values from -1 to 1
- out_cot: bfloat16 [8, 4, 8, 16, 1024], P(('groups', 'dp', 'fsdp'), 'seq'), parts along dimension 0, may hold values from -6 to 6
Outputs:
- out_tokens: bfloat16 [8, 4, 8, 16, 1024], P(('groups', 'dp', 'fsdp'), 'seq'), parts along dimension 0
- d_tokens: bfloat16 [8, 4, 8, 16, 1024], P(('groups', 'dp', 'fsdp'), 'seq'), parts along dimension 0
- d_kernel: float32 [54, 1024], P('groups'), parts along dimension 0
The draws below stay inside these ranges and needn't reach their ends.
There are 2 independent parts, one for each index of `groups`. The reference program is written for one: setup_inputs(seed, part) draws one part's arguments, and reference() takes and returns one part's arrays. A program takes and returns all parts, laid end to end along the dimension named above; an argument that names none is the same for every part. Nothing has to cross between parts.
All inputs are finite; a program needn't handle non-finite values.
Results may differ from the reference program's by a relative error of at most 0.024.
Values may be sent and summed in bfloat16 or wider, within the bound.
No kernel may reach another device: no remote copies, remote signals or barrier semaphores. Data moves between devices by JAX's collectives and lax.ppermute only.
A program may use at most 64 MiB of HBM per device.

```python
import math
import jax
import jax.numpy as jnp
from jax import lax

D = 1024
H = 8
HD = 64
FREQ = 256
GY = 8
GX = 16
LZ = 4
SEQLEN = 512
CRYSTALS = 4


def touch_ends(values, stream_key, least, top_value):
    longest = values.shape.index(max(values.shape))
    spots = []
    for shift in (0, 1):
        where = [jax.random.randint(jax.random.fold_in(stream_key, axis), (), 0, length) for axis, length in enumerate(values.shape)]
        where[longest] = (where[longest] + shift) % values.shape[longest]
        spots.append(tuple(where))
    return values.at[spots[0]].set(least).at[spots[1]].set(top_value)


def block_levels(key, shape, split, low, largest):
    loudness = 1.0
    for dim, blocks in split:
        heights = jax.random.uniform(jax.random.fold_in(jax.random.fold_in(key, 6), dim), (blocks,), jnp.float32, low / len(split), largest / len(split))
        loudness = loudness * jnp.repeat(jnp.exp(heights), shape[dim] // blocks).reshape((-1,) + (1,) * (len(shape) - 1 - dim))
    return loudness


def noise(stream_key, dims, scale, limit, cuts=(), held_as=jnp.bfloat16):
    array = jax.random.normal(stream_key, dims, jnp.float32) * scale
    if len(cuts) > 0:
        array = block_levels(stream_key, dims, cuts, -0.22, 0.18) * array
    return jnp.clip(array, min=-limit, max=limit).astype(held_as)


def setup_inputs(seed: int = 0, part: int = 0) -> dict:
    splits = jax.random.split(jax.random.key(seed), 9)
    part_splits = jax.random.split(jax.random.fold_in(splits[8], part), 9)
    return {
        "tokens": noise(part_splits[0], (CRYSTALS, LZ, GY, GX, D), 1.0, 6.0, ((0, 4), (1, 4))),
        "timesteps": touch_ends(jax.random.randint(part_splits[1], (CRYSTALS,), 0, 1000), jax.random.fold_in(part_splits[1], 1), 0, 999).astype(jnp.int32),
        "pxrd_mod": noise(part_splits[2], (CRYSTALS, 3, D), 0.5, 3.0, ((0, 4),), jnp.float32),
        "time_weight": noise(splits[3], (FREQ, 3 * D), FREQ ** -0.5, 0.375, ((0, 2),)),
        "conv_kernel": noise(splits[4], (27, D), 0.15, 0.9, (), jnp.float32),
        "qkv_weight": noise(splits[5], (D, 3 * H * HD), (D // 16) ** -0.5, 0.75, ((0, 2),)),
        "out_weight": noise(splits[6], (H * HD, D), (H * HD // 16) ** -0.5, 1.0, ((0, 2),)),
        "out_cot": noise(part_splits[7], (CRYSTALS, LZ, GY, GX, D), 1.0, 6.0, ((0, 4), (1, 4))),
    }


def time_features(steps_int, freq_width):
    half_width = freq_width // 2
    freq_index = jnp.arange(half_width).astype(jnp.float32)
    frequency = jnp.exp(freq_index * (-math.log(10000.0) / half_width))
    angles = steps_int.astype(jnp.float32)[:, None] * frequency[None, :]
    return jnp.concatenate([jnp.cos(angles), jnp.sin(angles)], axis=1).astype(jnp.bfloat16)

def modulation(steps_int, pxrd_mod, time_weight):
    features = time_features(steps_int, time_weight.shape[0])
    projected = jnp.dot(features, time_weight, preferred_element_type=jnp.float32)
    return projected.reshape(steps_int.shape[0], 3, time_weight.shape[1] // 3) + pxrd_mod

def depthwise(padded_z, kernel_taps, plane_count):
    framed = jnp.pad(padded_z, ((0, 0), (1, 1), (1, 1), (0, 0)))
    side_y = framed.shape[1] - 2
    side_x = framed.shape[2] - 2
    result = jnp.zeros((plane_count, side_y, side_x, framed.shape[3]), jnp.float32)
    for tap_z in range(3):
        for tap_y in range(3):
            for tap_x in range(3):
                window = framed[tap_z:tap_z + plane_count, tap_y:tap_y + side_y, tap_x:tap_x + side_x]
                result = result + kernel_taps[9 * tap_z + 3 * tap_y + tap_x] * window.astype(jnp.float32)
    return result

def kernel_terms(padded_z, upstream, plane_count):
    framed = jnp.pad(padded_z, ((0, 0), (1, 1), (1, 1), (0, 0)))
    side_y = framed.shape[1] - 2
    side_x = framed.shape[2] - 2
    upstream_f = upstream.astype(jnp.float32)
    collected = []
    for tap_z in range(3):
        for tap_y in range(3):
            for tap_x in range(3):
                window = framed[tap_z:tap_z + plane_count, tap_y:tap_y + side_y, tap_x:tap_x + side_x]
                collected.append(lax.optimization_barrier(jnp.sum(window.astype(jnp.float32) * upstream_f, axis=(0, 1, 2))))
    return jnp.stack(collected)

def modulate(stream, shift_row, scale_row):
    centre = stream - lax.optimization_barrier(jnp.mean(stream, axis=-1, keepdims=True))
    spread = lax.optimization_barrier(jnp.mean(centre * centre, axis=-1, keepdims=True))
    return centre * lax.rsqrt(spread + 1e-06) * (1.0 + scale_row) + shift_row

def head_norms(projected):
    row_count = projected.shape[0]
    sections = projected.reshape(row_count, 3, H, HD)
    query_key = sections[:, :2]
    normed = query_key * lax.rsqrt(lax.optimization_barrier(jnp.mean(query_key * query_key, axis=-1, keepdims=True)) + 1e-06)
    return (normed[:, 0].reshape(row_count, H * HD), normed[:, 1].reshape(row_count, H * HD), sections[:, 2].reshape(row_count, H * HD))

def attend_both(queries, grads, key_rows, value_rows):
    count = queries.shape[0]
    heads = queries.shape[1]
    block = min(512, count)
    steps = count // block
    scale_dot = 1.0 / math.sqrt(HD)
    key_f = key_rows.astype(jnp.float32)
    value_f = value_rows.astype(jnp.float32)

    def one_block(carry, pieces):
        query_blk, grad_blk = pieces
        query_f = query_blk.astype(jnp.float32)
        grad_f = grad_blk.astype(jnp.float32)
        scores = jnp.einsum('qhd,khd->hqk', query_f, key_f) * scale_dot
        expo = jnp.exp(scores)
        totals = lax.optimization_barrier(jnp.sum(expo, axis=-1, keepdims=True))
        weights = expo / totals
        probs = lax.optimization_barrier(weights.astype(jnp.bfloat16)).astype(jnp.float32)
        attn_blk = jnp.einsum('hqk,khd->qhd', probs, value_f).astype(jnp.bfloat16)
        delta = lax.optimization_barrier(jnp.sum(grad_f * attn_blk.astype(jnp.float32), axis=-1)).T
        dprob = jnp.einsum('qhd,khd->hqk', grad_f, value_f)
        dscore = lax.optimization_barrier((weights * (dprob - delta[:, :, None]) * scale_dot).astype(jnp.bfloat16)).astype(jnp.float32)
        dquery = jnp.einsum('hqk,khd->qhd', dscore, key_f)
        dkey = carry[0] + jnp.einsum('hqk,qhd->khd', dscore, query_f)
        dvalue = carry[1] + jnp.einsum('hqk,qhd->khd', probs, grad_f)
        return ((dkey, dvalue), (attn_blk, dquery))
    zeros_kv = jnp.zeros(key_rows.shape, jnp.float32)
    (dkey, dvalue), (attn_all, dquery) = lax.scan(one_block, (zeros_kv, zeros_kv), (queries.reshape(steps, block, heads, HD), grads.reshape(steps, block, heads, HD)))
    return (attn_all.reshape(count, heads, HD), dquery.reshape(count, heads, HD), dkey, dvalue)

def reference(tokens, timesteps, pxrd_mod, time_weight, conv_kernel, qkv_weight, out_weight, out_cot):
    modul = modulation(timesteps, pxrd_mod, time_weight)
    kernel_total = jnp.zeros((27, D), jnp.float32)
    outputs = []
    gradients = []
    for crystal in range(CRYSTALS):
        grid = tokens[crystal]
        padded = jnp.pad(grid, ((1, 1), (0, 0), (0, 0), (0, 0)))
        mixed = depthwise(padded, conv_kernel, LZ)
        resid = (grid.astype(jnp.float32) + mixed).astype(jnp.bfloat16).reshape(SEQLEN, D)
        shift_row = modul[crystal, 0]
        scale_row = modul[crystal, 1]
        gate_row = modul[crystal, 2]
        resid_f = resid.astype(jnp.float32)
        normed = modulate(resid_f, shift_row, scale_row).astype(jnp.bfloat16)
        projected = jnp.dot(normed, qkv_weight, preferred_element_type=jnp.float32)
        query_f, key_f, value_f = head_norms(projected)
        cotangent = out_cot[crystal].reshape(SEQLEN, D).astype(jnp.float32)
        gated = (gate_row * cotangent).astype(jnp.bfloat16)
        grad_attn = lax.dot_general(gated, out_weight, (((1,), (1,)), ((), ())), preferred_element_type=jnp.float32).astype(jnp.bfloat16)
        attn_heads, dquery, dkey, dvalue = attend_both(query_f.astype(jnp.bfloat16).reshape(SEQLEN, H, HD), grad_attn.reshape(SEQLEN, H, HD), key_f.astype(jnp.bfloat16).reshape(SEQLEN, H, HD), value_f.astype(jnp.bfloat16).reshape(SEQLEN, H, HD))
        attn_tok = attn_heads.reshape(SEQLEN, H * HD)
        projected_out = jnp.dot(attn_tok, out_weight, preferred_element_type=jnp.float32)
        outputs.append((resid_f + gate_row * projected_out).astype(jnp.bfloat16).reshape(LZ, GY, GX, D))
        _, pullback = jax.vjp(head_norms, projected)
        grad_projected, = pullback((dquery.reshape(SEQLEN, H * HD), dkey.reshape(SEQLEN, H * HD), dvalue.reshape(SEQLEN, H * HD)))
        grad_proj_b = grad_projected.astype(jnp.bfloat16)
        grad_normed = lax.dot_general(grad_proj_b, qkv_weight, (((1,), (1,)), ((), ())), preferred_element_type=jnp.float32)
        _, pull_norm = jax.vjp(lambda stream: modulate(stream, shift_row, scale_row), resid_f)
        grad_stream, = pull_norm(grad_normed)
        grad_resid = (cotangent + grad_stream).astype(jnp.bfloat16).reshape(LZ, GY, GX, D)
        grad_padded = jnp.pad(grad_resid, ((1, 1), (0, 0), (0, 0), (0, 0)))
        gradients.append((grad_resid.astype(jnp.float32) + depthwise(grad_padded, conv_kernel[::-1], LZ)).astype(jnp.bfloat16))
        kernel_total = kernel_total + kernel_terms(padded, grad_resid, LZ)
    d_kernel = kernel_total * (1.0 / math.sqrt(CRYSTALS * SEQLEN))
    return (jnp.stack(outputs), jnp.stack(gradients), d_kernel)
```

```python
import functools
import math

import jax
import jax.numpy as jnp
from jax import lax
from jax.experimental import pallas as pl
from jax.experimental.pallas import tpu as pltpu
from jax.sharding import PartitionSpec as P

H = 8
HD = 64


def padded_2(value, sides, width):
    for axis, dim in sides:
        count, length = (lax.axis_size(axis), value.shape[dim])
        up = [(i, (i + 1) % count) for i in range(count - 1)]
        down = [(j, i) for i, j in up]
        last = lax.slice_in_dim(value, length - width, length, axis=dim)
        leading = lax.slice_in_dim(value, 0, width, axis=dim)
        before = lax.ppermute(last, axis, up)
        after = lax.ppermute(leading, axis, down)
        value = jnp.concatenate([before, value, after], axis=dim)
    return value


def time_features(steps_int, freq_width):
    half_width = freq_width // 2
    freq_index = jnp.arange(half_width).astype(jnp.float32)
    frequency = jnp.exp(freq_index * (-math.log(10000.0) / half_width))
    angles = steps_int.astype(jnp.float32)[:, None] * frequency[None, :]
    return jnp.concatenate([jnp.cos(angles), jnp.sin(angles)], axis=1).astype(jnp.bfloat16)


def modulation(steps_int, pxrd_mod, time_weight):
    features = time_features(steps_int, time_weight.shape[0])
    projected = jnp.dot(features, time_weight, preferred_element_type=jnp.float32)
    return projected.reshape(steps_int.shape[0], 3, time_weight.shape[1] // 3) + pxrd_mod


def depthwise(padded_z, kernel_taps, plane_count):
    framed = jnp.pad(padded_z, ((0, 0), (1, 1), (1, 1), (0, 0)))
    side_y = framed.shape[1] - 2
    side_x = framed.shape[2] - 2
    result = jnp.zeros((plane_count, side_y, side_x, framed.shape[3]), jnp.float32)
    for tap_z in range(3):
        for tap_y in range(3):
            for tap_x in range(3):
                window = framed[
                    tap_z : tap_z + plane_count, tap_y : tap_y + side_y, tap_x : tap_x + side_x
                ]
                result = result + kernel_taps[9 * tap_z + 3 * tap_y + tap_x] * window.astype(
                    jnp.float32
                )
    return result


def kernel_terms(padded_z, upstream, plane_count):
    framed = jnp.pad(padded_z, ((0, 0), (1, 1), (1, 1), (0, 0)))
    side_y = framed.shape[1] - 2
    side_x = framed.shape[2] - 2
    upstream_f = upstream.astype(jnp.float32)
    collected = []
    for tap_z in range(3):
        for tap_y in range(3):
            for tap_x in range(3):
                window = framed[
                    tap_z : tap_z + plane_count, tap_y : tap_y + side_y, tap_x : tap_x + side_x
                ]
                collected.append(jnp.sum(window.astype(jnp.float32) * upstream_f, axis=(0, 1, 2)))
    return jnp.stack(collected)


def modulate(stream, shift_row, scale_row):
    centre = stream - jnp.mean(stream, axis=-1, keepdims=True)
    spread = jnp.mean(centre * centre, axis=-1, keepdims=True)
    return centre * lax.rsqrt(spread + 1e-06) * (1.0 + scale_row) + shift_row


def head_norms(projected):
    row_count = projected.shape[0]
    sections = projected.reshape(row_count, 3, H, HD)
    query_key = sections[:, :2]
    normed = query_key * lax.rsqrt(jnp.mean(query_key * query_key, axis=-1, keepdims=True) + 1e-06)
    return (
        normed[:, 0].reshape(row_count, H * HD),
        normed[:, 1].reshape(row_count, H * HD),
        sections[:, 2].reshape(row_count, H * HD),
    )


def attend_both(queries, grads, key_rows, value_rows):
    count = queries.shape[0]
    heads = queries.shape[1]
    block = min(512, count)
    steps = count // block
    scale_dot = 1.0 / math.sqrt(HD)

    def one_block(carry, pieces):
        query_blk, grad_blk = pieces
        scores = (
            jnp.einsum("qhd,khd->hqk", query_blk, key_rows, preferred_element_type=jnp.float32)
            * scale_dot
        )
        expo = jnp.exp(scores)
        totals = jnp.sum(expo, axis=-1, keepdims=True)
        weights = expo / totals
        probs = weights.astype(jnp.bfloat16)
        attn_blk = jnp.einsum(
            "hqk,khd->qhd", probs, value_rows, preferred_element_type=jnp.float32
        ).astype(jnp.bfloat16)
        delta = jnp.sum(grad_blk.astype(jnp.float32) * attn_blk.astype(jnp.float32), axis=-1).T
        dprob = jnp.einsum("qhd,khd->hqk", grad_blk, value_rows, preferred_element_type=jnp.float32)
        dscore = (weights * (dprob - delta[:, :, None]) * scale_dot).astype(jnp.bfloat16)
        dquery = jnp.einsum("hqk,khd->qhd", dscore, key_rows, preferred_element_type=jnp.float32)
        dkey = carry[0] + jnp.einsum(
            "hqk,qhd->khd", dscore, query_blk, preferred_element_type=jnp.float32
        )
        dvalue = carry[1] + jnp.einsum(
            "hqk,qhd->khd", probs, grad_blk, preferred_element_type=jnp.float32
        )
        return ((dkey, dvalue), (attn_blk, dquery))

    zeros_kv = jnp.zeros(key_rows.shape, jnp.float32)
    (dkey, dvalue), (attn_all, dquery) = lax.scan(
        one_block,
        (zeros_kv, zeros_kv),
        (queries.reshape(steps, block, heads, HD), grads.reshape(steps, block, heads, HD)),
    )
    return (attn_all.reshape(count, heads, HD), dquery.reshape(count, heads, HD), dkey, dvalue)


def shards(tokens, timesteps, pxrd_mod, time_weight, conv_kernel, qkv_weight, out_weight, out_cot):
    w_qkv, w_out, w_time = (
        lax.all_gather(qkv_weight, "fsdp", axis=0, tiled=True),
        lax.all_gather(out_weight, "fsdp", axis=0, tiled=True),
        lax.all_gather(time_weight, "fsdp", axis=0, tiled=True),
    )
    plane_count = tokens.shape[1]
    side_y = tokens.shape[2]
    side_x = tokens.shape[3]
    width_model = tokens.shape[4]
    row_count = plane_count * side_y * side_x
    inner_width = H * HD
    seq_count = lax.axis_size("seq")
    head_groups = min(H, seq_count)
    per_device = H // head_groups
    row_split = seq_count // head_groups
    part_rows = row_count // row_split
    group_width = per_device * HD
    padded = padded_2(tokens, (("seq", 1),), 1)[0]
    mixed = depthwise(padded, conv_kernel, plane_count)
    resid = (
        (tokens[0].astype(jnp.float32) + mixed).astype(jnp.bfloat16).reshape(row_count, width_model)
    )
    modul = modulation(timesteps, pxrd_mod, w_time)
    shift_row = modul[0, 0]
    scale_row = modul[0, 1]
    gate_row = modul[0, 2]
    resid_f = resid.astype(jnp.float32)
    normed = modulate(resid_f, shift_row, scale_row).astype(jnp.bfloat16)
    projected = jnp.dot(normed, w_qkv, preferred_element_type=jnp.float32)
    query_f, key_f, value_f = head_norms(projected)
    cotangent = out_cot[0].reshape(row_count, width_model).astype(jnp.float32)
    gated = (gate_row * cotangent).astype(jnp.bfloat16)
    grad_attn = lax.dot_general(
        gated, w_out, (((1,), (1,)), ((), ())), preferred_element_type=jnp.float32
    ).astype(jnp.bfloat16)

    def to_heads(token_rows):
        shaped = token_rows.reshape(row_split, part_rows, head_groups, group_width)
        return shaped.transpose(2, 0, 1, 3).reshape(seq_count, part_rows, group_width)

    def from_heads(head_rows):
        shaped = head_rows.reshape(head_groups, row_split, part_rows, group_width)
        return shaped.transpose(1, 2, 0, 3).reshape(row_count, inner_width)

    query_heads, grad_heads = (
        lax.all_to_all(
            to_heads(query_f.astype(jnp.bfloat16)), "seq", split_axis=0, concat_axis=0, tiled=True
        ),
        lax.all_to_all(to_heads(grad_attn), "seq", split_axis=0, concat_axis=0, tiled=True),
    )
    query_count = seq_count * part_rows
    query_heads = query_heads.reshape(query_count, per_device, HD)
    grad_heads = grad_heads.reshape(query_count, per_device, HD)
    stacked = jnp.stack(
        [
            key_f.astype(jnp.bfloat16).reshape(row_count, head_groups, group_width),
            value_f.astype(jnp.bfloat16).reshape(row_count, head_groups, group_width),
        ],
        axis=2,
    )
    by_group = stacked.transpose(1, 0, 2, 3).reshape(head_groups, row_count, 2 * group_width)
    copies = jnp.broadcast_to(
        by_group[:, None], (head_groups, row_split, row_count, 2 * group_width)
    )
    arrived = lax.all_to_all(
        copies.reshape(seq_count, row_count, 2 * group_width),
        "seq",
        split_axis=0,
        concat_axis=0,
        tiled=True,
    )
    key_value = arrived.reshape(seq_count * row_count, 2, per_device, HD)
    attn_heads, dquery, dkey, dvalue = attend_both(
        query_heads, grad_heads, key_value[:, 0], key_value[:, 1]
    )
    attn_tok = from_heads(
        lax.all_to_all(
            attn_heads.reshape(seq_count, part_rows, group_width),
            "seq",
            split_axis=0,
            concat_axis=0,
            tiled=True,
        )
    )
    projected_out = jnp.dot(attn_tok, w_out, preferred_element_type=jnp.float32)
    out_rows = (resid_f + gate_row * projected_out).astype(jnp.bfloat16)
    dquery_tok = from_heads(
        lax.all_to_all(
            dquery.reshape(seq_count, part_rows, group_width),
            "seq",
            split_axis=0,
            concat_axis=0,
            tiled=True,
        )
    )
    grads_kv = jnp.stack([dkey, dvalue], axis=1)
    returned = lax.all_to_all(
        grads_kv.reshape(seq_count, row_count, 2 * group_width).astype(jnp.bfloat16),
        "seq",
        split_axis=0,
        concat_axis=0,
        tiled=True,
    ).astype(jnp.float32)
    summed = jnp.sum(returned.reshape(head_groups, row_split, row_count, 2 * group_width), axis=1)
    grads_tok = (
        summed.reshape(head_groups, row_count, 2, group_width)
        .transpose(2, 1, 0, 3)
        .reshape(2, row_count, inner_width)
    )
    _, pullback = jax.vjp(head_norms, projected)
    (grad_projected,) = pullback((dquery_tok, grads_tok[0], grads_tok[1]))
    grad_proj_b = grad_projected.astype(jnp.bfloat16)
    grad_normed = lax.dot_general(
        grad_proj_b, w_qkv, (((1,), (1,)), ((), ())), preferred_element_type=jnp.float32
    )
    _, pull_norm = jax.vjp(lambda stream: modulate(stream, shift_row, scale_row), resid_f)
    (grad_stream,) = pull_norm(grad_normed)
    grad_resid = (
        (cotangent + grad_stream)
        .astype(jnp.bfloat16)
        .reshape(1, plane_count, side_y, side_x, width_model)
    )
    grad_padded = padded_2(grad_resid, (("seq", 1),), 1)[0]
    grad_tokens = (
        grad_resid[0].astype(jnp.float32) + depthwise(grad_padded, conv_kernel[::-1], plane_count)
    ).astype(jnp.bfloat16)
    local_terms = kernel_terms(padded, grad_resid[0], plane_count)
    norm_factor = 1.0 / math.sqrt(
        lax.axis_size("dp") * lax.axis_size("fsdp") * seq_count * row_count
    )
    grad_kernel = lax.psum(local_terms, ("seq", "dp", "fsdp")) * norm_factor
    return (out_rows.reshape(tokens.shape), grad_tokens.reshape(tokens.shape), grad_kernel)


def as_f32(value):
    return value.astype(jnp.float32)


def row_shift(value, step, inner):
    rows = value.shape[0]
    moved = pltpu.roll(value, step % rows, axis=0)
    place = lax.rem(lax.broadcasted_iota(jnp.int32, value.shape, 0), inner)
    return jnp.where(place == (0 if step == 1 else inner - 1), 0.0, moved)


def slab_shift(value, step, inner):
    if step == 0:
        return value
    empty = jnp.zeros((inner, value.shape[1]), value.dtype)
    if step == 1:
        return jnp.concatenate([empty, value[:-inner]], axis=0)
    return jnp.concatenate([value[inner:], empty], axis=0)


def conv_lanes(planes, taps, flipped, inner):
    by_x = []
    for tap_x in range(3):
        total = None
        for tap_y in range(3):
            part = None
            for tap_z in range(3):
                index = 9 * tap_z + 3 * tap_y + tap_x
                index = 26 - index if flipped else index
                term = taps[index : index + 1] * planes[tap_z]
                part = term if part is None else part + term
            part = slab_shift(part, 1 - tap_y, inner)
            total = part if total is None else total + part
        by_x.append(total)
    return by_x[1] + row_shift(by_x[0], 1, inner) + row_shift(by_x[2], -1, inner)


def head_mean(value):
    width = value.shape[1]
    left = lax.broadcasted_iota(jnp.int32, (width, width), 0) // HD
    right = lax.broadcasted_iota(jnp.int32, (width, width), 1) // HD
    same = jnp.where(left == right, 1.0, 0.0).astype(jnp.bfloat16)
    high = value.astype(jnp.bfloat16)
    low = (value - as_f32(high)).astype(jnp.bfloat16)
    total = jnp.dot(high, same, preferred_element_type=jnp.float32)
    total = total + jnp.dot(low, same, preferred_element_type=jnp.float32)
    return total * (1.0 / HD)


def nt_dot(left, right):
    return lax.dot_general(
        left, right, (((1,), (1,)), ((), ())), preferred_element_type=jnp.float32
    )


def tn_dot(left, right):
    return lax.dot_general(
        left, right, (((0,), (0,)), ((), ())), preferred_element_type=jnp.float32
    )


def nn_dot(left, right):
    return jnp.dot(left, right, preferred_element_type=jnp.float32)


def front_body(slots, ids, feats, pxrd, wt_own, wt_oth, cot, wo_own, wo_oth, *rest):
    mod, sends, by_group = rest[0], rest[1 : 1 + slots], rest[1 + slots]
    me, half = ids[0], ids[1]
    width = pxrd.shape[1]
    projected = nn_dot(feats[0], wt_own[...]) + nn_dot(feats[1], wt_oth[...])
    for row in range(3):
        mod[row : row + 1, :] = projected[0:1, row * width : (row + 1) * width] + pxrd[row : row + 1, :]
    gated = (mod[2:3, :] * as_f32(cot[...])).astype(jnp.bfloat16)
    lanes = sends[0].shape[1]
    per_half = wo_own.shape[0] // lanes
    for weight, part in ((wo_own, half), (wo_oth, 1 - half)):
        grads = nt_dot(gated, weight[...]).astype(jnp.bfloat16)
        for j in range(per_half):
            by_group[part * per_half + j] = grads[:, j * lanes : (j + 1) * lanes]
    for k in range(slots):
        sends[k][...] = by_group[lax.bitwise_xor(me, k)]


def mix_body(slots, inner, ids, tok, up, down, taps, mod, w_own, w_oth, *rest):
    resid, sections = rest[0], rest[1]
    sends = rest[2 : 2 + slots]
    normed, by_group = rest[2 + slots :]
    me, half = ids[0], ids[1]
    rows, width = tok.shape
    step = 128
    sums = jnp.zeros((rows, step), jnp.float32)
    for start in range(0, width, step):
        cols = slice(start, start + step)
        planes = [as_f32(ref[:, cols]) for ref in (up, tok, down)]
        mixed = conv_lanes(planes, taps[:, cols], False, inner)
        rounded = (planes[1] + mixed).astype(jnp.bfloat16)
        resid[:, cols] = rounded
        sums = sums + as_f32(rounded)
    mean = jnp.sum(sums, axis=1, keepdims=True) * (1.0 / width)
    squares = jnp.zeros((rows, step), jnp.float32)
    for start in range(0, width, step):
        centre = as_f32(resid[:, start : start + step]) - mean
        squares = squares + centre * centre
    spread = jnp.sum(squares, axis=1, keepdims=True) * (1.0 / width)
    inverse = lax.rsqrt(spread + 1e-06)
    per_half = width // 2
    for start in range(0, width, step):
        cols = slice(start, start + step)
        centre = as_f32(resid[:, cols]) - mean
        value = centre * inverse * (1.0 + mod[1:2, cols]) + mod[0:1, cols]
        inside = start % per_half
        normed[start // per_half, :, inside : inside + step] = value.astype(jnp.bfloat16)
    projected = nn_dot(normed[half], w_own[...]) + nn_dot(normed[1 - half], w_oth[...])
    lanes = sends[0].shape[1] // 3
    inner_width = H * HD
    sections[...] = projected[:, : 2 * inner_width]
    for group in range(slots):
        for part in range(3):
            block = projected[:, part * inner_width + group * lanes :][:, :lanes]
            if part < 2:
                block = block * lax.rsqrt(head_mean(block * block) + 1e-06)
            by_group[group, :, part * lanes : (part + 1) * lanes] = block.astype(jnp.bfloat16)
    for k in range(slots):
        sends[k][...] = by_group[lax.bitwise_xor(me, k)]


def attend_body(slots, *refs):
    qkv_in, grads_in = refs[:slots], refs[slots : 2 * slots]
    backs, attns = refs[2 * slots : 3 * slots], refs[3 * slots : 4 * slots]
    keys, values, probs_all, dscore_all = refs[4 * slots :]
    rows, lanes = grads_in[0].shape
    heads = lanes // HD
    scale = 1.0 / math.sqrt(HD)
    for k in range(slots):
        keys[k * rows : (k + 1) * rows, :] = qkv_in[k][:, lanes : 2 * lanes]
        values[k * rows : (k + 1) * rows, :] = qkv_in[k][:, 2 * lanes :]
    owner = lax.broadcasted_iota(jnp.int32, (rows, lanes), 1) // HD
    for k in range(slots):
        query = qkv_in[k][:, :lanes]
        grad = grads_in[k][...]
        attn_total = None
        pieces = []
        for head in range(heads):
            mine = owner == head
            scores = nt_dot(jnp.where(mine, query, jnp.zeros_like(query)), keys[...]) * scale
            expo = jnp.exp(scores)
            weights = expo * (1.0 / jnp.sum(expo, axis=1, keepdims=True))
            probs = weights.astype(jnp.bfloat16)
            probs_all[head, k * rows : (k + 1) * rows, :] = probs
            attn = jnp.where(mine, nn_dot(probs, values[...]), 0.0)
            attn_total = attn if attn_total is None else attn_total + attn
            pieces.append(weights)
        attn_total = attn_total.astype(jnp.bfloat16)
        attns[k][...] = attn_total
        product = as_f32(attn_total) * as_f32(grad)
        dquery = None
        for head in range(heads):
            mine = owner == head
            delta = jnp.sum(jnp.where(mine, product, 0.0), axis=1, keepdims=True)
            dprob = nt_dot(jnp.where(mine, grad, jnp.zeros_like(grad)), values[...])
            dscore = (pieces[head] * (dprob - delta) * scale).astype(jnp.bfloat16)
            dscore_all[head, k * rows : (k + 1) * rows, :] = dscore
            part = jnp.where(mine, nn_dot(dscore, keys[...]), 0.0)
            dquery = part if dquery is None else dquery + part
        backs[k][:, :lanes] = dquery.astype(jnp.bfloat16)
    queries = jnp.concatenate([ref[:, :lanes] for ref in qkv_in], axis=0)
    grads = jnp.concatenate([ref[...] for ref in grads_in], axis=0)
    owner_all = lax.broadcasted_iota(jnp.int32, queries.shape, 1) // HD
    dkeys = None
    dvalues = None
    for head in range(heads):
        mine = owner_all == head
        dkey = jnp.where(mine, tn_dot(dscore_all[head], queries), 0.0)
        dvalue = jnp.where(mine, tn_dot(probs_all[head], grads), 0.0)
        dkeys = dkey if dkeys is None else dkeys + dkey
        dvalues = dvalue if dvalues is None else dvalues + dvalue
    for k in range(slots):
        backs[k][:, lanes : 2 * lanes] = dkeys[k * rows : (k + 1) * rows].astype(jnp.bfloat16)
        backs[k][:, 2 * lanes :] = dvalues[k * rows : (k + 1) * rows].astype(jnp.bfloat16)


def tail_body(slots, inner, ids, *refs):
    backs = refs[:slots]
    sections, resid, cot, mod, w_own, w_oth, tok, up, down = refs[slots : slots + 9]
    dresid, terms = refs[slots + 9 : slots + 11]
    by_group, dproj, dnormed, sums = refs[slots + 11 :]
    me, half = ids[0], ids[1]
    rows, width = resid.shape
    lanes = by_group.shape[3]
    inner_width = H * HD
    for k in range(slots):
        group = lax.bitwise_xor(me, k)
        for part in range(3):
            by_group[group, part] = backs[k][:, part * lanes : (part + 1) * lanes]
    for group in range(slots):
        for part in range(3):
            start = part * inner_width + group * lanes
            grad = by_group[group, part]
            if part < 2:
                grad = as_f32(grad)
                block = sections[:, start : start + lanes]
                inverse = lax.rsqrt(head_mean(block * block) + 1e-06)
                unit = block * inverse
                grad = (inverse * (grad - unit * head_mean(grad * unit))).astype(jnp.bfloat16)
            dproj[:, start : start + lanes] = grad
    dnormed[half] = nt_dot(dproj[...], w_own[...])
    dnormed[1 - half] = nt_dot(dproj[...], w_oth[...])
    step = 128
    per_half = width // 2
    total = jnp.zeros((rows, step), jnp.float32)
    for start in range(0, width, step):
        total = total + as_f32(resid[:, start : start + step])
    mean = jnp.sum(total, axis=1, keepdims=True) * (1.0 / width)
    total = jnp.zeros((rows, step), jnp.float32)
    for start in range(0, width, step):
        centre = as_f32(resid[:, start : start + step]) - mean
        total = total + centre * centre
    inverse = lax.rsqrt(jnp.sum(total, axis=1, keepdims=True) * (1.0 / width) + 1e-06)
    plain = jnp.zeros((rows, step), jnp.float32)
    crossed = jnp.zeros((rows, step), jnp.float32)
    for start in range(0, width, step):
        cols = slice(start, start + step)
        inside = start % per_half
        grad = dnormed[start // per_half, :, inside : inside + step] * (1.0 + mod[1:2, cols])
        unit = (as_f32(resid[:, cols]) - mean) * inverse
        plain = plain + grad
        crossed = crossed + grad * unit
    plain = jnp.sum(plain, axis=1, keepdims=True) * (1.0 / width)
    crossed = jnp.sum(crossed, axis=1, keepdims=True) * (1.0 / width)
    for start in range(0, width, step):
        cols = slice(start, start + step)
        inside = start % per_half
        grad = dnormed[start // per_half, :, inside : inside + step] * (1.0 + mod[1:2, cols])
        unit = (as_f32(resid[:, cols]) - mean) * inverse
        stream = as_f32(cot[:, cols]) + inverse * (grad - plain - unit * crossed)
        dresid[:, cols] = stream.astype(jnp.bfloat16)
    for start in range(0, width, step):
        cols = slice(start, start + step)
        grad = as_f32(dresid[:, cols])
        moved = [row_shift(grad, -1, inner), grad, row_shift(grad, 1, inner)]
        for tap_z, ref in enumerate((up, tok, down)):
            plane = as_f32(ref[:, cols])
            for tap_y in range(3):
                low, high = max(0, 1 - tap_y), max(0, tap_y - 1)
                for tap_x in range(3):
                    index = 9 * tap_z + 3 * tap_y + tap_x
                    prod = (
                        plane[high * inner : rows - low * inner]
                        * moved[tap_x][low * inner : rows - high * inner]
                    )
                    prod = jnp.sum(prod.reshape(-1, 8, step), axis=0)
                    terms[index : index + 1, cols] = jnp.sum(prod, axis=0, keepdims=True)


def out_body(slots, ids, *refs):
    attns = refs[:slots]
    resid, mod, wo_own, wo_oth, out, by_group = refs[slots:]
    me, half = ids[0], ids[1]
    lanes = attns[0].shape[1]
    per_half = wo_own.shape[0] // lanes
    for k in range(slots):
        by_group[lax.bitwise_xor(me, k)] = attns[k][...]
    total = None
    for weight, part in ((wo_own, half), (wo_oth, 1 - half)):
        for j in range(per_half):
            term = nn_dot(by_group[part * per_half + j], weight[j * lanes : (j + 1) * lanes, :])
            total = term if total is None else total + term
    out[...] = (as_f32(resid[...]) + mod[2:3, :] * total).astype(jnp.bfloat16)


def back_conv_body(inner, grad, up, down, taps, out):
    width = grad.shape[1]
    step = 128
    for start in range(0, width, step):
        cols = slice(start, start + step)
        planes = [as_f32(ref[:, cols]) for ref in (up, grad, down)]
        mixed = conv_lanes(planes, taps[:, cols], True, inner)
        out[:, cols] = (planes[1] + mixed).astype(jnp.bfloat16)


def pair_body(last, left, right, out):
    total = as_f32(left[...]) + as_f32(right[...])
    out[...] = total.astype(out.dtype)


def final_body(factor, slots, *refs):
    values = [as_f32(ref[...]) for ref in refs[:slots]]
    while len(values) > 1:
        values = [values[i] + values[i + 1] for i in range(0, len(values), 2)]
    refs[slots][...] = values[0] * factor


def call(body, name, outs, args, scratch=(), flops=0, scalars=False):
    whole = pl.BlockSpec(memory_space=pltpu.VMEM)
    specs = [whole] * len(args)
    if scalars:
        specs[0] = pl.BlockSpec(memory_space=pltpu.SMEM)
    sizes = [math.prod(a.shape) * a.dtype.itemsize for a in list(args) + list(outs)]
    return pl.pallas_call(
        body,
        out_shape=tuple(outs),
        in_specs=specs,
        out_specs=(whole,) * len(outs),
        scratch_shapes=list(scratch),
        compiler_params=pltpu.CompilerParams(vmem_limit_bytes=40 * 2**20),
        cost_estimate=pl.CostEstimate(flops=flops, bytes_accessed=sum(sizes), transcendentals=0),
        name=name,
    )(*args)


def swapped(value, axis, distance):
    count = lax.axis_size(axis)
    return lax.ppermute(value, axis, [(i, i ^ distance) for i in range(count)])


def exchanged(pieces):
    return [pieces[0]] + [swapped(pieces[k], "seq", k) for k in range(1, len(pieces))]


def neighbours(value):
    count = lax.axis_size("seq")
    up = [(i, i + 1) for i in range(count - 1)]
    down = [(i + 1, i) for i in range(count - 1)]
    return lax.ppermute(value, "seq", up), lax.ppermute(value, "seq", down)


def slab_shards(
    tokens, timesteps, pxrd_mod, time_weight, conv_kernel, qkv_weight, out_weight, out_cot
):
    bf16, f32 = jnp.bfloat16, jnp.float32
    side_y, inner, width = tokens.shape[2:]
    rows = side_y * inner
    slots = lax.axis_size("seq")
    lanes = H * HD // slots
    me = lax.axis_index("seq")
    half = lax.axis_index("fsdp")
    ids = jnp.stack([me, half]).astype(jnp.int32)
    tok = tokens.reshape(rows, width)
    cot = out_cot.reshape(rows, width)
    shape = jax.ShapeDtypeStruct

    wo_oth = swapped(out_weight, "fsdp", 1)
    wt_oth = swapped(time_weight, "fsdp", 1)
    up, down = neighbours(tok)
    wq_oth = swapped(qkv_weight, "fsdp", 1)

    freq = 2 * time_weight.shape[0]
    feats = time_features(timesteps, freq).reshape(2, freq // 2)
    own = lax.dynamic_slice_in_dim(feats, half, 1, axis=0)
    oth = lax.dynamic_slice_in_dim(feats, 1 - half, 1, axis=0)
    feats = jnp.broadcast_to(jnp.stack([own, oth]), (2, 8, freq // 2))
    front = call(
        functools.partial(front_body, slots),
        "front",
        [shape((3, width), f32)] + [shape((rows, lanes), bf16)] * slots,
        (ids, feats, pxrd_mod[0], time_weight, wt_oth, cot, out_weight, wo_oth),
        [pltpu.VMEM((slots, rows, lanes), bf16)],
        flops=2 * rows * width * H * HD,
        scalars=True,
    )
    mod = front[0]
    grads_in = exchanged(front[1:])

    mixed = call(
        functools.partial(mix_body, slots, inner),
        "mix",
        [shape((rows, width), bf16), shape((rows, 2 * H * HD), f32)]
        + [shape((rows, 3 * lanes), bf16)] * slots,
        (ids, tok, up, down, conv_kernel, mod, qkv_weight, wq_oth),
        [pltpu.VMEM((2, rows, width // 2), bf16), pltpu.VMEM((slots, rows, 3 * lanes), bf16)],
        flops=2 * rows * width * 3 * H * HD,
        scalars=True,
    )
    resid, sections = mixed[:2]
    qkv_in = exchanged(mixed[2:])
    count = slots * rows
    attended = call(
        functools.partial(attend_body, slots),
        "attend",
        [shape((rows, 3 * lanes), bf16)] * slots + [shape((rows, lanes), bf16)] * slots,
        (*qkv_in, *grads_in),
        [pltpu.VMEM((count, lanes), bf16)] * 2
        + [pltpu.VMEM((lanes // HD, count, count), bf16)] * 2,
        flops=12 * count * count * lanes,
    )
    backs = exchanged(attended[:slots])
    attns = exchanged(attended[slots:])
    dresid, terms = call(
        functools.partial(tail_body, slots, inner),
        "tail",
        [shape((rows, width), bf16), shape((27, width), f32)],
        (ids, *backs, sections, resid, cot, mod, qkv_weight, wq_oth, tok, up, down),
        [
            pltpu.VMEM((slots, 3, rows, lanes), bf16),
            pltpu.VMEM((rows, 3 * H * HD), bf16),
            pltpu.VMEM((2, rows, width // 2), f32),
            pltpu.VMEM((8, width), f32),
        ],
        flops=2 * rows * width * 3 * H * HD,
        scalars=True,
    )
    (out,) = call(
        functools.partial(out_body, slots),
        "out",
        [shape((rows, width), bf16)],
        (ids, *attns, resid, mod, out_weight, wo_oth),
        [pltpu.VMEM((slots, rows, lanes), bf16)],
        flops=2 * rows * width * H * HD,
        scalars=True,
    )
    (terms,) = call(
        functools.partial(pair_body, False),
        "add_fsdp",
        [shape((27, width), bf16)],
        (terms, swapped(terms, "fsdp", 1)),
    )
    (terms,) = call(
        functools.partial(pair_body, False),
        "add_dp",
        [shape((27, width), bf16)],
        (terms, swapped(terms, "dp", 1)),
    )
    factor = 1.0 / math.sqrt(lax.axis_size("dp") * lax.axis_size("fsdp") * slots * rows)
    (kernel_grad,) = call(
        functools.partial(final_body, factor, slots),
        "add_seq",
        [shape((27, width), f32)],
        exchanged([terms] * slots),
    )
    grad_up, grad_down = neighbours(dresid)
    (token_grad,) = call(
        functools.partial(back_conv_body, inner),
        "back_conv",
        [shape((rows, width), bf16)],
        (dresid, grad_up, grad_down, conv_kernel),
    )
    return out.reshape(tokens.shape), token_grad.reshape(tokens.shape), kernel_grad


def solution(mesh):
    count = mesh.shape["seq"]

    def pick(*args):
        tokens, time_weight = args[0], args[3]
        lanes = H * HD // count
        fits = (
            count in (2, 4)
            and tokens.shape[0] == 1
            and tokens.shape[1] == 1
            and tokens.shape[3] % 16 == 0
            and lanes % 128 == 0
            and mesh.shape["dp"] == 2
            and mesh.shape["fsdp"] == 2
        )
        return slab_shards(*args) if fits else shards(*args)

    placed = (
        P(("groups", "dp", "fsdp"), "seq", None, None, None),
        P(("groups", "dp", "fsdp")),
        P(("groups", "dp", "fsdp"), None, None),
        P("fsdp", None),
        P(),
        P("fsdp", None),
        P("fsdp", None),
        P(("groups", "dp", "fsdp"), "seq", None, None, None),
    )
    return jax.shard_map(
        pick,
        mesh=mesh,
        in_specs=placed,
        out_specs=(
            P(("groups", "dp", "fsdp"), "seq", None, None, None),
            P(("groups", "dp", "fsdp"), "seq", None, None, None),
            P("groups", None),
        ),
        check_vma=False,
    )
```

```python
import functools
import math

import jax
import jax.numpy as jnp
from jax import lax
from jax.experimental import pallas as pl
from jax.experimental.pallas import tpu as pltpu
from jax.sharding import PartitionSpec as P

H = 8
HD = 64


def padded_2(value, sides, width):
    for axis, dim in sides:
        count, length = (lax.axis_size(axis), value.shape[dim])
        up = [(i, (i + 1) % count) for i in range(count - 1)]
        down = [(j, i) for i, j in up]
        last = lax.slice_in_dim(value, length - width, length, axis=dim)
        leading = lax.slice_in_dim(value, 0, width, axis=dim)
        before = lax.ppermute(last, axis, up)
        after = lax.ppermute(leading, axis, down)
        value = jnp.concatenate([before, value, after], axis=dim)
    return value


def time_features(steps_int, freq_width):
    half_width = freq_width // 2
    freq_index = jnp.arange(half_width).astype(jnp.float32)
    frequency = jnp.exp(freq_index * (-math.log(10000.0) / half_width))
    angles = steps_int.astype(jnp.float32)[:, None] * frequency[None, :]
    return jnp.concatenate([jnp.cos(angles), jnp.sin(angles)], axis=1).astype(jnp.bfloat16)


def modulation(steps_int, pxrd_mod, time_weight):
    features = time_features(steps_int, time_weight.shape[0])
    projected = jnp.dot(features, time_weight, preferred_element_type=jnp.float32)
    return projected.reshape(steps_int.shape[0], 3, time_weight.shape[1] // 3) + pxrd_mod


def depthwise(padded_z, kernel_taps, plane_count):
    framed = jnp.pad(padded_z, ((0, 0), (1, 1), (1, 1), (0, 0)))
    side_y = framed.shape[1] - 2
    side_x = framed.shape[2] - 2
    result = jnp.zeros((plane_count, side_y, side_x, framed.shape[3]), jnp.float32)
    for tap_z in range(3):
        for tap_y in range(3):
            for tap_x in range(3):
                window = framed[
                    tap_z : tap_z + plane_count, tap_y : tap_y + side_y, tap_x : tap_x + side_x
                ]
                result = result + kernel_taps[9 * tap_z + 3 * tap_y + tap_x] * window.astype(
                    jnp.float32
                )
    return result


def kernel_terms(padded_z, upstream, plane_count):
    framed = jnp.pad(padded_z, ((0, 0), (1, 1), (1, 1), (0, 0)))
    side_y = framed.shape[1] - 2
    side_x = framed.shape[2] - 2
    upstream_f = upstream.astype(jnp.float32)
    collected = []
    for tap_z in range(3):
        for tap_y in range(3):
            for tap_x in range(3):
                window = framed[
                    tap_z : tap_z + plane_count, tap_y : tap_y + side_y, tap_x : tap_x + side_x
                ]
                collected.append(jnp.sum(window.astype(jnp.float32) * upstream_f, axis=(0, 1, 2)))
    return jnp.stack(collected)


def modulate(stream, shift_row, scale_row):
    centre = stream - jnp.mean(stream, axis=-1, keepdims=True)
    spread = jnp.mean(centre * centre, axis=-1, keepdims=True)
    return centre * lax.rsqrt(spread + 1e-06) * (1.0 + scale_row) + shift_row


def head_norms(projected):
    row_count = projected.shape[0]
    sections = projected.reshape(row_count, 3, H, HD)
    query_key = sections[:, :2]
    normed = query_key * lax.rsqrt(jnp.mean(query_key * query_key, axis=-1, keepdims=True) + 1e-06)
    return (
        normed[:, 0].reshape(row_count, H * HD),
        normed[:, 1].reshape(row_count, H * HD),
        sections[:, 2].reshape(row_count, H * HD),
    )


def attend_both(queries, grads, key_rows, value_rows):
    count = queries.shape[0]
    heads = queries.shape[1]
    block = min(512, count)
    steps = count // block
    scale_dot = 1.0 / math.sqrt(HD)

    def one_block(carry, pieces):
        query_blk, grad_blk = pieces
        scores = (
            jnp.einsum("qhd,khd->hqk", query_blk, key_rows, preferred_element_type=jnp.float32)
            * scale_dot
        )
        expo = jnp.exp(scores)
        totals = jnp.sum(expo, axis=-1, keepdims=True)
        weights = expo / totals
        probs = weights.astype(jnp.bfloat16)
        attn_blk = jnp.einsum(
            "hqk,khd->qhd", probs, value_rows, preferred_element_type=jnp.float32
        ).astype(jnp.bfloat16)
        delta = jnp.sum(grad_blk.astype(jnp.float32) * attn_blk.astype(jnp.float32), axis=-1).T
        dprob = jnp.einsum("qhd,khd->hqk", grad_blk, value_rows, preferred_element_type=jnp.float32)
        dscore = (weights * (dprob - delta[:, :, None]) * scale_dot).astype(jnp.bfloat16)
        dquery = jnp.einsum("hqk,khd->qhd", dscore, key_rows, preferred_element_type=jnp.float32)
        dkey = carry[0] + jnp.einsum(
            "hqk,qhd->khd", dscore, query_blk, preferred_element_type=jnp.float32
        )
        dvalue = carry[1] + jnp.einsum(
            "hqk,qhd->khd", probs, grad_blk, preferred_element_type=jnp.float32
        )
        return ((dkey, dvalue), (attn_blk, dquery))

    zeros_kv = jnp.zeros(key_rows.shape, jnp.float32)
    (dkey, dvalue), (attn_all, dquery) = lax.scan(
        one_block,
        (zeros_kv, zeros_kv),
        (queries.reshape(steps, block, heads, HD), grads.reshape(steps, block, heads, HD)),
    )
    return (attn_all.reshape(count, heads, HD), dquery.reshape(count, heads, HD), dkey, dvalue)


def shards(tokens, timesteps, pxrd_mod, time_weight, conv_kernel, qkv_weight, out_weight, out_cot):
    w_qkv, w_out, w_time = (
        lax.all_gather(qkv_weight, "fsdp", axis=0, tiled=True),
        lax.all_gather(out_weight, "fsdp", axis=0, tiled=True),
        lax.all_gather(time_weight, "fsdp", axis=0, tiled=True),
    )
    plane_count = tokens.shape[1]
    side_y = tokens.shape[2]
    side_x = tokens.shape[3]
    width_model = tokens.shape[4]
    row_count = plane_count * side_y * side_x
    inner_width = H * HD
    seq_count = lax.axis_size("seq")
    head_groups = min(H, seq_count)
    per_device = H // head_groups
    row_split = seq_count // head_groups
    part_rows = row_count // row_split
    group_width = per_device * HD
    padded = padded_2(tokens, (("seq", 1),), 1)[0]
    mixed = depthwise(padded, conv_kernel, plane_count)
    resid = (
        (tokens[0].astype(jnp.float32) + mixed).astype(jnp.bfloat16).reshape(row_count, width_model)
    )
    modul = modulation(timesteps, pxrd_mod, w_time)
    shift_row = modul[0, 0]
    scale_row = modul[0, 1]
    gate_row = modul[0, 2]
    resid_f = resid.astype(jnp.float32)
    normed = modulate(resid_f, shift_row, scale_row).astype(jnp.bfloat16)
    projected = jnp.dot(normed, w_qkv, preferred_element_type=jnp.float32)
    query_f, key_f, value_f = head_norms(projected)
    cotangent = out_cot[0].reshape(row_count, width_model).astype(jnp.float32)
    gated = (gate_row * cotangent).astype(jnp.bfloat16)
    grad_attn = lax.dot_general(
        gated, w_out, (((1,), (1,)), ((), ())), preferred_element_type=jnp.float32
    ).astype(jnp.bfloat16)

    def to_heads(token_rows):
        shaped = token_rows.reshape(row_split, part_rows, head_groups, group_width)
        return shaped.transpose(2, 0, 1, 3).reshape(seq_count, part_rows, group_width)

    def from_heads(head_rows):
        shaped = head_rows.reshape(head_groups, row_split, part_rows, group_width)
        return shaped.transpose(1, 2, 0, 3).reshape(row_count, inner_width)

    query_heads, grad_heads = (
        lax.all_to_all(
            to_heads(query_f.astype(jnp.bfloat16)), "seq", split_axis=0, concat_axis=0, tiled=True
        ),
        lax.all_to_all(to_heads(grad_attn), "seq", split_axis=0, concat_axis=0, tiled=True),
    )
    query_count = seq_count * part_rows
    query_heads = query_heads.reshape(query_count, per_device, HD)
    grad_heads = grad_heads.reshape(query_count, per_device, HD)
    stacked = jnp.stack(
        [
            key_f.astype(jnp.bfloat16).reshape(row_count, head_groups, group_width),
            value_f.astype(jnp.bfloat16).reshape(row_count, head_groups, group_width),
        ],
        axis=2,
    )
    by_group = stacked.transpose(1, 0, 2, 3).reshape(head_groups, row_count, 2 * group_width)
    copies = jnp.broadcast_to(
        by_group[:, None], (head_groups, row_split, row_count, 2 * group_width)
    )
    arrived = lax.all_to_all(
        copies.reshape(seq_count, row_count, 2 * group_width),
        "seq",
        split_axis=0,
        concat_axis=0,
        tiled=True,
    )
    key_value = arrived.reshape(seq_count * row_count, 2, per_device, HD)
    attn_heads, dquery, dkey, dvalue = attend_both(
        query_heads, grad_heads, key_value[:, 0], key_value[:, 1]
    )
    attn_tok = from_heads(
        lax.all_to_all(
            attn_heads.reshape(seq_count, part_rows, group_width),
            "seq",
            split_axis=0,
            concat_axis=0,
            tiled=True,
        )
    )
    projected_out = jnp.dot(attn_tok, w_out, preferred_element_type=jnp.float32)
    out_rows = (resid_f + gate_row * projected_out).astype(jnp.bfloat16)
    dquery_tok = from_heads(
        lax.all_to_all(
            dquery.reshape(seq_count, part_rows, group_width),
            "seq",
            split_axis=0,
            concat_axis=0,
            tiled=True,
        )
    )
    grads_kv = jnp.stack([dkey, dvalue], axis=1)
    returned = lax.all_to_all(
        grads_kv.reshape(seq_count, row_count, 2 * group_width).astype(jnp.bfloat16),
        "seq",
        split_axis=0,
        concat_axis=0,
        tiled=True,
    ).astype(jnp.float32)
    summed = jnp.sum(returned.reshape(head_groups, row_split, row_count, 2 * group_width), axis=1)
    grads_tok = (
        summed.reshape(head_groups, row_count, 2, group_width)
        .transpose(2, 1, 0, 3)
        .reshape(2, row_count, inner_width)
    )
    _, pullback = jax.vjp(head_norms, projected)
    (grad_projected,) = pullback((dquery_tok, grads_tok[0], grads_tok[1]))
    grad_proj_b = grad_projected.astype(jnp.bfloat16)
    grad_normed = lax.dot_general(
        grad_proj_b, w_qkv, (((1,), (1,)), ((), ())), preferred_element_type=jnp.float32
    )
    _, pull_norm = jax.vjp(lambda stream: modulate(stream, shift_row, scale_row), resid_f)
    (grad_stream,) = pull_norm(grad_normed)
    grad_resid = (
        (cotangent + grad_stream)
        .astype(jnp.bfloat16)
        .reshape(1, plane_count, side_y, side_x, width_model)
    )
    grad_padded = padded_2(grad_resid, (("seq", 1),), 1)[0]
    grad_tokens = (
        grad_resid[0].astype(jnp.float32) + depthwise(grad_padded, conv_kernel[::-1], plane_count)
    ).astype(jnp.bfloat16)
    local_terms = kernel_terms(padded, grad_resid[0], plane_count)
    norm_factor = 1.0 / math.sqrt(
        lax.axis_size("dp") * lax.axis_size("fsdp") * seq_count * row_count
    )
    grad_kernel = lax.psum(local_terms, ("seq", "dp", "fsdp")) * norm_factor
    return (out_rows.reshape(tokens.shape), grad_tokens.reshape(tokens.shape), grad_kernel)


def as_f32(value):
    return value.astype(jnp.float32)


def row_shift(value, step, inner):
    rows = value.shape[0]
    moved = pltpu.roll(value, step % rows, axis=0)
    place = lax.rem(lax.broadcasted_iota(jnp.int32, value.shape, 0), inner)
    return jnp.where(place == (0 if step == 1 else inner - 1), 0.0, moved)


def slab_shift(value, step, inner):
    if step == 0:
        return value
    empty = jnp.zeros((inner, value.shape[1]), value.dtype)
    if step == 1:
        return jnp.concatenate([empty, value[:-inner]], axis=0)
    return jnp.concatenate([value[inner:], empty], axis=0)


def sided_taps(taps, odd):
    before, after = taps[0:9], taps[18:27]
    return jnp.where(odd, before, after), taps[9:18], jnp.where(odd, after, before)


def conv_lanes(planes, taps, inner):
    by_x = []
    for tap_x in range(3):
        total = None
        for tap_y in range(3):
            part = None
            for tap_z in range(3):
                index = 3 * tap_y + tap_x
                term = taps[tap_z][index : index + 1] * planes[tap_z]
                part = term if part is None else part + term
            part = slab_shift(part, 1 - tap_y, inner)
            total = part if total is None else total + part
        by_x.append(total)
    return by_x[1] + row_shift(by_x[0], 1, inner) + row_shift(by_x[2], -1, inner)


def head_mean(value):
    width = value.shape[1]
    left = lax.broadcasted_iota(jnp.int32, (width, width), 0) // HD
    right = lax.broadcasted_iota(jnp.int32, (width, width), 1) // HD
    same = jnp.where(left == right, 1.0, 0.0).astype(jnp.bfloat16)
    high = value.astype(jnp.bfloat16)
    low = (value - as_f32(high)).astype(jnp.bfloat16)
    total = jnp.dot(high, same, preferred_element_type=jnp.float32)
    total = total + jnp.dot(low, same, preferred_element_type=jnp.float32)
    return total * (1.0 / HD)


def nt_dot(left, right):
    return lax.dot_general(
        left, right, (((1,), (1,)), ((), ())), preferred_element_type=jnp.float32
    )


def tn_dot(left, right):
    return lax.dot_general(
        left, right, (((0,), (0,)), ((), ())), preferred_element_type=jnp.float32
    )


def nn_dot(left, right):
    return jnp.dot(left, right, preferred_element_type=jnp.float32)


def front_body(slots, ids, feats, *rest):
    fetched = rest[:6]
    mod, sends, by_group = rest[6], rest[7 : 7 + slots], rest[7 + slots]
    wt_own, wt_oth, pxrd, wo_own, wo_oth, cot = held = rest[8 + slots : 14 + slots]
    arrive = rest[14 + slots]
    me, half = ids[0], ids[1]
    width = cot.shape[1]
    copies = [
        pltpu.make_async_copy(source, place, arrive.at[i])
        for i, (source, place) in enumerate(zip(fetched, held))
    ]
    for copy in copies:
        copy.start()
    for copy in copies[:3]:
        copy.wait()
    projected = nn_dot(feats[0], wt_own[...]) + nn_dot(feats[1], wt_oth[...])
    for row in range(3):
        cols = slice(row * width, (row + 1) * width)
        mod[row : row + 1, :] = projected[0:1, cols] + pxrd[row : row + 1, :]
    for copy in copies[3:]:
        copy.wait()
    gated = (mod[2:3, :] * as_f32(cot[...])).astype(jnp.bfloat16)
    lanes = sends[0].shape[1]
    per_half = wo_own.shape[0] // lanes
    for weight, part in ((wo_own, half), (wo_oth, 1 - half)):
        grads = nt_dot(gated, weight[...]).astype(jnp.bfloat16)
        for j in range(per_half):
            by_group[part * per_half + j] = grads[:, j * lanes : (j + 1) * lanes]
    for k, gap in enumerate(distances(slots)):
        sends[k][...] = by_group[lax.bitwise_xor(me, gap)]


def mix_body(slots, inner, ids, tok, near, far, taps, mod, w_own, w_oth, *rest):
    resid, sections = rest[0], rest[1]
    sends = rest[2 : 2 + slots]
    normed, by_group = rest[2 + slots :]
    me, half = ids[0], ids[1]
    odd = lax.rem(me, 2) == 1
    rows, width = tok.shape
    step = 128
    sums = jnp.zeros((rows, step), jnp.float32)
    for start in range(0, width, step):
        cols = slice(start, start + step)
        planes = [as_f32(ref[:, cols]) for ref in (near, tok, far)]
        mixed = conv_lanes(planes, sided_taps(taps[:, cols], odd), inner)
        rounded = (planes[1] + mixed).astype(jnp.bfloat16)
        resid[:, cols] = rounded
        sums = sums + as_f32(rounded)
    mean = jnp.sum(sums, axis=1, keepdims=True) * (1.0 / width)
    squares = jnp.zeros((rows, step), jnp.float32)
    for start in range(0, width, step):
        centre = as_f32(resid[:, start : start + step]) - mean
        squares = squares + centre * centre
    spread = jnp.sum(squares, axis=1, keepdims=True) * (1.0 / width)
    inverse = lax.rsqrt(spread + 1e-06)
    per_half = width // 2
    for start in range(0, width, step):
        cols = slice(start, start + step)
        centre = as_f32(resid[:, cols]) - mean
        value = centre * inverse * (1.0 + mod[1:2, cols]) + mod[0:1, cols]
        inside = start % per_half
        normed[start // per_half, :, inside : inside + step] = value.astype(jnp.bfloat16)
    projected = nn_dot(normed[half], w_own[...]) + nn_dot(normed[1 - half], w_oth[...])
    lanes = sends[0].shape[1] // 3
    inner_width = H * HD
    sections[...] = projected[:, : 2 * inner_width]
    for group in range(slots):
        for part in range(3):
            block = projected[:, part * inner_width + group * lanes :][:, :lanes]
            if part < 2:
                block = block * lax.rsqrt(head_mean(block * block) + 1e-06)
            by_group[group, :, part * lanes : (part + 1) * lanes] = block.astype(jnp.bfloat16)
    for k, gap in enumerate(distances(slots)):
        sends[k][...] = by_group[lax.bitwise_xor(me, gap)]


def attend_body(slots, *refs):
    qkv_in, grads_in = refs[:slots], refs[slots : 2 * slots]
    backs = refs[2 * slots : 3 * slots]
    keys, values, probs_all, dscore_all = refs[3 * slots :]
    rows, lanes = grads_in[0].shape
    heads = lanes // HD
    scale = 1.0 / math.sqrt(HD)
    for k in range(slots):
        keys[k * rows : (k + 1) * rows, :] = qkv_in[k][:, lanes : 2 * lanes]
        values[k * rows : (k + 1) * rows, :] = qkv_in[k][:, 2 * lanes :]
    owner = lax.broadcasted_iota(jnp.int32, (rows, lanes), 1) // HD
    for k in range(slots):
        query = qkv_in[k][:, :lanes]
        grad = grads_in[k][...]
        attn_total = None
        pieces = []
        for head in range(heads):
            mine = owner == head
            scores = nt_dot(jnp.where(mine, query, jnp.zeros_like(query)), keys[...]) * scale
            expo = jnp.exp(scores)
            weights = expo * (1.0 / jnp.sum(expo, axis=1, keepdims=True))
            probs = weights.astype(jnp.bfloat16)
            probs_all[head, k * rows : (k + 1) * rows, :] = probs
            attn = jnp.where(mine, nn_dot(probs, values[...]), 0.0)
            attn_total = attn if attn_total is None else attn_total + attn
            pieces.append(weights)
        attn_total = attn_total.astype(jnp.bfloat16)
        backs[k][:, 3 * lanes :] = attn_total
        product = as_f32(attn_total) * as_f32(grad)
        dquery = None
        for head in range(heads):
            mine = owner == head
            delta = jnp.sum(jnp.where(mine, product, 0.0), axis=1, keepdims=True)
            dprob = nt_dot(jnp.where(mine, grad, jnp.zeros_like(grad)), values[...])
            dscore = (pieces[head] * (dprob - delta) * scale).astype(jnp.bfloat16)
            dscore_all[head, k * rows : (k + 1) * rows, :] = dscore
            part = jnp.where(mine, nn_dot(dscore, keys[...]), 0.0)
            dquery = part if dquery is None else dquery + part
        backs[k][:, :lanes] = dquery.astype(jnp.bfloat16)
    queries = jnp.concatenate([ref[:, :lanes] for ref in qkv_in], axis=0)
    grads = jnp.concatenate([ref[...] for ref in grads_in], axis=0)
    owner_all = lax.broadcasted_iota(jnp.int32, queries.shape, 1) // HD
    dkeys = None
    dvalues = None
    for head in range(heads):
        mine = owner_all == head
        dkey = jnp.where(mine, tn_dot(dscore_all[head], queries), 0.0)
        dvalue = jnp.where(mine, tn_dot(probs_all[head], grads), 0.0)
        dkeys = dkey if dkeys is None else dkeys + dkey
        dvalues = dvalue if dvalues is None else dvalues + dvalue
    for k in range(slots):
        backs[k][:, lanes : 2 * lanes] = dkeys[k * rows : (k + 1) * rows].astype(jnp.bfloat16)
        backs[k][:, 2 * lanes : 3 * lanes] = dvalues[k * rows : (k + 1) * rows].astype(jnp.bfloat16)


def tail_body(slots, inner, ids, *refs):
    backs = refs[:slots]
    sections, resid, cot, mod, w_own, w_oth, tok, near, far = refs[slots : slots + 9]
    dresid, terms = refs[slots + 9 : slots + 11]
    by_group, dproj, dnormed = refs[slots + 11 :]
    me, half = ids[0], ids[1]
    odd = lax.rem(me, 2) == 1
    rows, width = resid.shape
    lanes = by_group.shape[3]
    inner_width = H * HD
    for k, gap in enumerate(distances(slots)):
        group = lax.bitwise_xor(me, gap)
        for part in range(3):
            by_group[group, part] = backs[k][:, part * lanes : (part + 1) * lanes]
    for group in range(slots):
        for part in range(3):
            start = part * inner_width + group * lanes
            grad = by_group[group, part]
            if part < 2:
                grad = as_f32(grad)
                block = sections[:, start : start + lanes]
                inverse = lax.rsqrt(head_mean(block * block) + 1e-06)
                unit = block * inverse
                grad = (inverse * (grad - unit * head_mean(grad * unit))).astype(jnp.bfloat16)
            dproj[:, start : start + lanes] = grad
    dnormed[half] = nt_dot(dproj[...], w_own[...])
    dnormed[1 - half] = nt_dot(dproj[...], w_oth[...])
    step = 128
    per_half = width // 2
    total = jnp.zeros((rows, step), jnp.float32)
    for start in range(0, width, step):
        total = total + as_f32(resid[:, start : start + step])
    mean = jnp.sum(total, axis=1, keepdims=True) * (1.0 / width)
    total = jnp.zeros((rows, step), jnp.float32)
    for start in range(0, width, step):
        centre = as_f32(resid[:, start : start + step]) - mean
        total = total + centre * centre
    inverse = lax.rsqrt(jnp.sum(total, axis=1, keepdims=True) * (1.0 / width) + 1e-06)
    plain = jnp.zeros((rows, step), jnp.float32)
    crossed = jnp.zeros((rows, step), jnp.float32)
    for start in range(0, width, step):
        cols = slice(start, start + step)
        inside = start % per_half
        grad = dnormed[start // per_half, :, inside : inside + step] * (1.0 + mod[1:2, cols])
        unit = (as_f32(resid[:, cols]) - mean) * inverse
        plain = plain + grad
        crossed = crossed + grad * unit
    plain = jnp.sum(plain, axis=1, keepdims=True) * (1.0 / width)
    crossed = jnp.sum(crossed, axis=1, keepdims=True) * (1.0 / width)
    for start in range(0, width, step):
        cols = slice(start, start + step)
        inside = start % per_half
        grad = dnormed[start // per_half, :, inside : inside + step] * (1.0 + mod[1:2, cols])
        unit = (as_f32(resid[:, cols]) - mean) * inverse
        stream = as_f32(cot[:, cols]) + inverse * (grad - plain - unit * crossed)
        dresid[:, cols] = stream.astype(jnp.bfloat16)
    for start in range(0, width, step):
        cols = slice(start, start + step)
        grad = as_f32(dresid[:, cols])
        moved = [row_shift(grad, -1, inner), grad, row_shift(grad, 1, inner)]
        found = []
        for ref in (near, tok, far):
            plane = as_f32(ref[:, cols])
            lines = []
            for tap_y in range(3):
                low, high = max(0, 1 - tap_y), max(0, tap_y - 1)
                for tap_x in range(3):
                    prod = (
                        plane[high * inner : rows - low * inner]
                        * moved[tap_x][low * inner : rows - high * inner]
                    )
                    prod = jnp.sum(prod.reshape(-1, 8, step), axis=0)
                    lines.append(jnp.sum(prod, axis=0, keepdims=True))
            found.append(lines)
        for i in range(9):
            by_near, by_far = found[0][i], found[2][i]
            terms[i : i + 1, cols] = jnp.where(odd, by_near, by_far)
            terms[9 + i : 10 + i, cols] = found[1][i]
            terms[18 + i : 19 + i, cols] = jnp.where(odd, by_far, by_near)


def out_body(slots, ids, *refs):
    backs = refs[:slots]
    resid, mod, wo_own, wo_oth, out, by_group = refs[slots:]
    me, half = ids[0], ids[1]
    lanes = backs[0].shape[1] // 4
    per_half = wo_own.shape[0] // lanes
    for k, gap in enumerate(distances(slots)):
        by_group[lax.bitwise_xor(me, gap)] = backs[k][:, 3 * lanes :]
    total = None
    for weight, part in ((wo_own, half), (wo_oth, 1 - half)):
        for j in range(per_half):
            term = nn_dot(by_group[part * per_half + j], weight[j * lanes : (j + 1) * lanes, :])
            total = term if total is None else total + term
    out[...] = (as_f32(resid[...]) + mod[2:3, :] * total).astype(jnp.bfloat16)


def back_conv_body(inner, ids, grad, near, far, taps, out):
    odd = lax.rem(ids[0], 2) == 1
    width = grad.shape[1]
    step = 128
    for start in range(0, width, step):
        cols = slice(start, start + step)
        planes = [as_f32(ref[:, cols]) for ref in (near, grad, far)]
        lines = taps[:, cols]
        turned = [jnp.concatenate([lines[r : r + 1] for r in range(26, -1, -1)], axis=0)]
        mixed = conv_lanes(planes, sided_taps(turned[0], odd), inner)
        out[:, cols] = (planes[1] + mixed).astype(jnp.bfloat16)


def pair_body(left, right, out):
    total = as_f32(left[...]) + as_f32(right[...])
    out[...] = total.astype(out.dtype)


def final_body(factor, slots, *refs):
    gaps = distances(slots)
    values = [as_f32(refs[gaps.index(gap)][...]) for gap in range(slots)]
    while len(values) > 1:
        values = [values[i] + values[i + 1] for i in range(0, len(values), 2)]
    refs[slots][...] = values[0] * factor


def call(body, name, outs, args, scratch=(), flops=0, scalars=False, far_args=(), vmem=16):
    whole = pl.BlockSpec(memory_space=pltpu.VMEM)
    specs = [whole] * len(args)
    if scalars:
        specs[0] = pl.BlockSpec(memory_space=pltpu.SMEM)
    for i in far_args:
        specs[i] = pl.BlockSpec(memory_space=pltpu.HBM)
    sizes = [math.prod(a.shape) * a.dtype.itemsize for a in list(args) + list(outs)]
    args = [
        pltpu.with_memory_space_constraint(a, pltpu.HBM) if i in far_args else a
        for i, a in enumerate(args)
    ]
    return pl.pallas_call(
        body,
        out_shape=tuple(outs),
        in_specs=specs,
        out_specs=(whole,) * len(outs),
        scratch_shapes=list(scratch),
        compiler_params=pltpu.CompilerParams(vmem_limit_bytes=vmem * 2**20),
        cost_estimate=pl.CostEstimate(flops=flops, bytes_accessed=sum(sizes), transcendentals=0),
        name=name,
    )(*args)


def swapped(value, axis, distance):
    count = lax.axis_size(axis)
    return lax.ppermute(value, axis, [(i, i ^ distance) for i in range(count)])


def distances(slots):
    return (0, 2, 3, 1) if slots == 4 else (0, 1)


def exchanged(pieces):
    pairs = list(zip(pieces, distances(len(pieces))))
    return [pieces[0]] + [swapped(piece, "seq", k) for piece, k in pairs[1:]]


def neighbours(value):
    count = lax.axis_size("seq")
    near = swapped(value, "seq", 1)
    if count == 2:
        return near, jnp.zeros_like(value)
    middle = [(i, i + 1) for i in range(1, count - 1, 2)]
    return near, lax.ppermute(value, "seq", middle + [(j, i) for i, j in middle])


def slab_shards(
    tokens, timesteps, pxrd_mod, time_weight, conv_kernel, qkv_weight, out_weight, out_cot
):
    bf16, f32 = jnp.bfloat16, jnp.float32
    side_y, inner, width = tokens.shape[2:]
    rows = side_y * inner
    slots = lax.axis_size("seq")
    lanes = H * HD // slots
    me = lax.axis_index("seq")
    half = lax.axis_index("fsdp")
    ids = jnp.stack([me, half]).astype(jnp.int32)
    tok = tokens.reshape(rows, width)
    cot = out_cot.reshape(rows, width)
    shape = jax.ShapeDtypeStruct

    wo_oth = swapped(out_weight, "fsdp", 1)
    wt_oth = swapped(time_weight, "fsdp", 1)
    near, far = neighbours(tok)
    wq_oth = swapped(qkv_weight, "fsdp", 1)

    freq = 2 * time_weight.shape[0]
    feats = time_features(timesteps, freq).reshape(2, freq // 2)
    own = lax.dynamic_slice_in_dim(feats, half, 1, axis=0)
    oth = lax.dynamic_slice_in_dim(feats, 1 - half, 1, axis=0)
    feats = jnp.broadcast_to(jnp.stack([own, oth]), (2, 8, freq // 2))
    front = call(
        functools.partial(front_body, slots),
        "front",
        [shape((3, width), f32)] + [shape((rows, lanes), bf16)] * slots,
        (ids, feats, time_weight, wt_oth, pxrd_mod[0], out_weight, wo_oth, cot),
        [pltpu.VMEM((slots, rows, lanes), bf16)]
        + [pltpu.VMEM(time_weight.shape, bf16)] * 2
        + [pltpu.VMEM(pxrd_mod.shape[1:], f32)]
        + [pltpu.VMEM(out_weight.shape, bf16)] * 2
        + [pltpu.VMEM((rows, width), bf16), pltpu.SemaphoreType.DMA((6,))],
        far_args=range(2, 8),
        flops=2 * rows * width * H * HD,
        scalars=True,
    )
    mod = front[0]
    grads_in = exchanged(front[1:])

    mixed = call(
        functools.partial(mix_body, slots, inner),
        "mix",
        [shape((rows, width), bf16), shape((rows, 2 * H * HD), f32)]
        + [shape((rows, 3 * lanes), bf16)] * slots,
        (ids, tok, near, far, conv_kernel, mod, qkv_weight, wq_oth),
        [pltpu.VMEM((2, rows, width // 2), bf16), pltpu.VMEM((slots, rows, 3 * lanes), bf16)],
        flops=2 * rows * width * 3 * H * HD,
        scalars=True,
    )
    resid, sections = mixed[:2]
    sends, grads_in = lax.optimization_barrier((mixed[2:], grads_in))
    qkv_in = exchanged(sends)
    count = slots * rows
    attended = call(
        functools.partial(attend_body, slots),
        "attend",
        [shape((rows, 4 * lanes), bf16)] * slots,
        (*qkv_in, *grads_in),
        [pltpu.VMEM((count, lanes), bf16)] * 2
        + [pltpu.VMEM((lanes // HD, count, count), bf16)] * 2,
        flops=12 * count * count * lanes,
    )
    backs = exchanged(attended)
    dresid, terms = call(
        functools.partial(tail_body, slots, inner),
        "tail",
        [shape((rows, width), bf16), shape((27, width), f32)],
        (ids, *backs, sections, resid, cot, mod, qkv_weight, wq_oth, tok, near, far),
        [
            pltpu.VMEM((slots, 3, rows, lanes), bf16),
            pltpu.VMEM((rows, 3 * H * HD), bf16),
            pltpu.VMEM((2, rows, width // 2), f32),
        ],
        flops=2 * rows * width * 3 * H * HD,
        scalars=True,
    )
    (out,) = call(
        functools.partial(out_body, slots),
        "out",
        [shape((rows, width), bf16)],
        (ids, *backs, resid, mod, out_weight, wo_oth),
        [pltpu.VMEM((slots, rows, lanes), bf16)],
        flops=2 * rows * width * H * HD,
        scalars=True,
    )
    shape_terms = [shape((27, width), bf16)]
    other = swapped(terms, "fsdp", 1)
    grad_near, grad_far = neighbours(dresid)
    (terms,) = call(pair_body, "add_fsdp", shape_terms, (terms, other))
    other = swapped(terms, "dp", 1)
    other, out = lax.optimization_barrier((other, out))
    (terms,) = call(pair_body, "add_dp", shape_terms, (terms, other))
    (token_grad,) = call(
        functools.partial(back_conv_body, inner),
        "back_conv",
        [shape((rows, width), bf16)],
        (ids, dresid, grad_near, grad_far, conv_kernel),
        scalars=True,
    )
    factor = 1.0 / math.sqrt(lax.axis_size("dp") * lax.axis_size("fsdp") * slots * rows)
    pieces = exchanged([terms] * slots)
    pieces[-1], token_grad = lax.optimization_barrier((pieces[-1], token_grad))
    (kernel_grad,) = call(
        functools.partial(final_body, factor, slots), "add_seq", [shape((27, width), f32)], pieces
    )
    return out.reshape(tokens.shape), token_grad.reshape(tokens.shape), kernel_grad


def solution(mesh):
    count = mesh.shape["seq"]

    def pick(*args):
        tokens, time_weight = args[0], args[3]
        lanes = H * HD // count
        fits = (
            count in (2, 4)
            and tokens.shape[0] == 1
            and tokens.shape[1] == 1
            and tokens.shape[3] % 16 == 0
            and lanes % 128 == 0
            and mesh.shape["dp"] == 2
            and mesh.shape["fsdp"] == 2
        )
        return slab_shards(*args) if fits else shards(*args)

    placed = (
        P(("groups", "dp", "fsdp"), "seq", None, None, None),
        P(("groups", "dp", "fsdp")),
        P(("groups", "dp", "fsdp"), None, None),
        P("fsdp", None),
        P(),
        P("fsdp", None),
        P("fsdp", None),
        P(("groups", "dp", "fsdp"), "seq", None, None, None),
    )
    return jax.shard_map(
        pick,
        mesh=mesh,
        in_specs=placed,
        out_specs=(
            P(("groups", "dp", "fsdp"), "seq", None, None, None),
            P(("groups", "dp", "fsdp"), "seq", None, None, None),
            P("groups", None),
        ),
        check_vma=False,
    )
```

```python
import functools
import math

import jax
import jax.numpy as jnp
from jax import lax
from jax.experimental import pallas as pl
from jax.experimental.pallas import tpu as pltpu
from jax.sharding import PartitionSpec as P

H = 8
HD = 64


def padded_2(value, sides, width):
    for axis, dim in sides:
        count, length = (lax.axis_size(axis), value.shape[dim])
        up = [(i, (i + 1) % count) for i in range(count - 1)]
        down = [(j, i) for i, j in up]
        last = lax.slice_in_dim(value, length - width, length, axis=dim)
        leading = lax.slice_in_dim(value, 0, width, axis=dim)
        before = lax.ppermute(last, axis, up)
        after = lax.ppermute(leading, axis, down)
        value = jnp.concatenate([before, value, after], axis=dim)
    return value


def time_features(steps_int, freq_width):
    half_width = freq_width // 2
    freq_index = jnp.arange(half_width).astype(jnp.float32)
    frequency = jnp.exp(freq_index * (-math.log(10000.0) / half_width))
    angles = steps_int.astype(jnp.float32)[:, None] * frequency[None, :]
    return jnp.concatenate([jnp.cos(angles), jnp.sin(angles)], axis=1).astype(jnp.bfloat16)


def modulation(steps_int, pxrd_mod, time_weight):
    features = time_features(steps_int, time_weight.shape[0])
    projected = jnp.dot(features, time_weight, preferred_element_type=jnp.float32)
    return projected.reshape(steps_int.shape[0], 3, time_weight.shape[1] // 3) + pxrd_mod


def depthwise(padded_z, kernel_taps, plane_count):
    framed = jnp.pad(padded_z, ((0, 0), (1, 1), (1, 1), (0, 0)))
    side_y = framed.shape[1] - 2
    side_x = framed.shape[2] - 2
    result = jnp.zeros((plane_count, side_y, side_x, framed.shape[3]), jnp.float32)
    for tap_z in range(3):
        for tap_y in range(3):
            for tap_x in range(3):
                window = framed[
                    tap_z : tap_z + plane_count, tap_y : tap_y + side_y, tap_x : tap_x + side_x
                ]
                result = result + kernel_taps[9 * tap_z + 3 * tap_y + tap_x] * window.astype(
                    jnp.float32
                )
    return result


def kernel_terms(padded_z, upstream, plane_count):
    framed = jnp.pad(padded_z, ((0, 0), (1, 1), (1, 1), (0, 0)))
    side_y = framed.shape[1] - 2
    side_x = framed.shape[2] - 2
    upstream_f = upstream.astype(jnp.float32)
    collected = []
    for tap_z in range(3):
        for tap_y in range(3):
            for tap_x in range(3):
                window = framed[
                    tap_z : tap_z + plane_count, tap_y : tap_y + side_y, tap_x : tap_x + side_x
                ]
                collected.append(jnp.sum(window.astype(jnp.float32) * upstream_f, axis=(0, 1, 2)))
    return jnp.stack(collected)


def modulate(stream, shift_row, scale_row):
    centre = stream - jnp.mean(stream, axis=-1, keepdims=True)
    spread = jnp.mean(centre * centre, axis=-1, keepdims=True)
    return centre * lax.rsqrt(spread + 1e-06) * (1.0 + scale_row) + shift_row


def head_norms(projected):
    row_count = projected.shape[0]
    sections = projected.reshape(row_count, 3, H, HD)
    query_key = sections[:, :2]
    normed = query_key * lax.rsqrt(jnp.mean(query_key * query_key, axis=-1, keepdims=True) + 1e-06)
    return (
        normed[:, 0].reshape(row_count, H * HD),
        normed[:, 1].reshape(row_count, H * HD),
        sections[:, 2].reshape(row_count, H * HD),
    )


def attend_both(queries, grads, key_rows, value_rows):
    count = queries.shape[0]
    heads = queries.shape[1]
    block = min(512, count)
    steps = count // block
    scale_dot = 1.0 / math.sqrt(HD)

    def one_block(carry, pieces):
        query_blk, grad_blk = pieces
        scores = (
            jnp.einsum("qhd,khd->hqk", query_blk, key_rows, preferred_element_type=jnp.float32)
            * scale_dot
        )
        expo = jnp.exp(scores)
        totals = jnp.sum(expo, axis=-1, keepdims=True)
        weights = expo / totals
        probs = weights.astype(jnp.bfloat16)
        attn_blk = jnp.einsum(
            "hqk,khd->qhd", probs, value_rows, preferred_element_type=jnp.float32
        ).astype(jnp.bfloat16)
        delta = jnp.sum(grad_blk.astype(jnp.float32) * attn_blk.astype(jnp.float32), axis=-1).T
        dprob = jnp.einsum("qhd,khd->hqk", grad_blk, value_rows, preferred_element_type=jnp.float32)
        dscore = (weights * (dprob - delta[:, :, None]) * scale_dot).astype(jnp.bfloat16)
        dquery = jnp.einsum("hqk,khd->qhd", dscore, key_rows, preferred_element_type=jnp.float32)
        dkey = carry[0] + jnp.einsum(
            "hqk,qhd->khd", dscore, query_blk, preferred_element_type=jnp.float32
        )
        dvalue = carry[1] + jnp.einsum(
            "hqk,qhd->khd", probs, grad_blk, preferred_element_type=jnp.float32
        )
        return ((dkey, dvalue), (attn_blk, dquery))

    zeros_kv = jnp.zeros(key_rows.shape, jnp.float32)
    (dkey, dvalue), (attn_all, dquery) = lax.scan(
        one_block,
        (zeros_kv, zeros_kv),
        (queries.reshape(steps, block, heads, HD), grads.reshape(steps, block, heads, HD)),
    )
    return (attn_all.reshape(count, heads, HD), dquery.reshape(count, heads, HD), dkey, dvalue)


def shards(tokens, timesteps, pxrd_mod, time_weight, conv_kernel, qkv_weight, out_weight, out_cot):
    w_qkv, w_out, w_time = (
        lax.all_gather(qkv_weight, "fsdp", axis=0, tiled=True),
        lax.all_gather(out_weight, "fsdp", axis=0, tiled=True),
        lax.all_gather(time_weight, "fsdp", axis=0, tiled=True),
    )
    plane_count = tokens.shape[1]
    side_y = tokens.shape[2]
    side_x = tokens.shape[3]
    width_model = tokens.shape[4]
    row_count = plane_count * side_y * side_x
    inner_width = H * HD
    seq_count = lax.axis_size("seq")
    head_groups = min(H, seq_count)
    per_device = H // head_groups
    row_split = seq_count // head_groups
    part_rows = row_count // row_split
    group_width = per_device * HD
    padded = padded_2(tokens, (("seq", 1),), 1)[0]
    mixed = depthwise(padded, conv_kernel, plane_count)
    resid = (
        (tokens[0].astype(jnp.float32) + mixed).astype(jnp.bfloat16).reshape(row_count, width_model)
    )
    modul = modulation(timesteps, pxrd_mod, w_time)
    shift_row = modul[0, 0]
    scale_row = modul[0, 1]
    gate_row = modul[0, 2]
    resid_f = resid.astype(jnp.float32)
    normed = modulate(resid_f, shift_row, scale_row).astype(jnp.bfloat16)
    projected = jnp.dot(normed, w_qkv, preferred_element_type=jnp.float32)
    query_f, key_f, value_f = head_norms(projected)
    cotangent = out_cot[0].reshape(row_count, width_model).astype(jnp.float32)
    gated = (gate_row * cotangent).astype(jnp.bfloat16)
    grad_attn = lax.dot_general(
        gated, w_out, (((1,), (1,)), ((), ())), preferred_element_type=jnp.float32
    ).astype(jnp.bfloat16)

    def to_heads(token_rows):
        shaped = token_rows.reshape(row_split, part_rows, head_groups, group_width)
        return shaped.transpose(2, 0, 1, 3).reshape(seq_count, part_rows, group_width)

    def from_heads(head_rows):
        shaped = head_rows.reshape(head_groups, row_split, part_rows, group_width)
        return shaped.transpose(1, 2, 0, 3).reshape(row_count, inner_width)

    query_heads, grad_heads = (
        lax.all_to_all(
            to_heads(query_f.astype(jnp.bfloat16)), "seq", split_axis=0, concat_axis=0, tiled=True
        ),
        lax.all_to_all(to_heads(grad_attn), "seq", split_axis=0, concat_axis=0, tiled=True),
    )
    query_count = seq_count * part_rows
    query_heads = query_heads.reshape(query_count, per_device, HD)
    grad_heads = grad_heads.reshape(query_count, per_device, HD)
    stacked = jnp.stack(
        [
            key_f.astype(jnp.bfloat16).reshape(row_count, head_groups, group_width),
            value_f.astype(jnp.bfloat16).reshape(row_count, head_groups, group_width),
        ],
        axis=2,
    )
    by_group = stacked.transpose(1, 0, 2, 3).reshape(head_groups, row_count, 2 * group_width)
    copies = jnp.broadcast_to(
        by_group[:, None], (head_groups, row_split, row_count, 2 * group_width)
    )
    arrived = lax.all_to_all(
        copies.reshape(seq_count, row_count, 2 * group_width),
        "seq",
        split_axis=0,
        concat_axis=0,
        tiled=True,
    )
    key_value = arrived.reshape(seq_count * row_count, 2, per_device, HD)
    attn_heads, dquery, dkey, dvalue = attend_both(
        query_heads, grad_heads, key_value[:, 0], key_value[:, 1]
    )
    attn_tok = from_heads(
        lax.all_to_all(
            attn_heads.reshape(seq_count, part_rows, group_width),
            "seq",
            split_axis=0,
            concat_axis=0,
            tiled=True,
        )
    )
    projected_out = jnp.dot(attn_tok, w_out, preferred_element_type=jnp.float32)
    out_rows = (resid_f + gate_row * projected_out).astype(jnp.bfloat16)
    dquery_tok = from_heads(
        lax.all_to_all(
            dquery.reshape(seq_count, part_rows, group_width),
            "seq",
            split_axis=0,
            concat_axis=0,
            tiled=True,
        )
    )
    grads_kv = jnp.stack([dkey, dvalue], axis=1)
    returned = lax.all_to_all(
        grads_kv.reshape(seq_count, row_count, 2 * group_width).astype(jnp.bfloat16),
        "seq",
        split_axis=0,
        concat_axis=0,
        tiled=True,
    ).astype(jnp.float32)
    summed = jnp.sum(returned.reshape(head_groups, row_split, row_count, 2 * group_width), axis=1)
    grads_tok = (
        summed.reshape(head_groups, row_count, 2, group_width)
        .transpose(2, 1, 0, 3)
        .reshape(2, row_count, inner_width)
    )
    _, pullback = jax.vjp(head_norms, projected)
    (grad_projected,) = pullback((dquery_tok, grads_tok[0], grads_tok[1]))
    grad_proj_b = grad_projected.astype(jnp.bfloat16)
    grad_normed = lax.dot_general(
        grad_proj_b, w_qkv, (((1,), (1,)), ((), ())), preferred_element_type=jnp.float32
    )
    _, pull_norm = jax.vjp(lambda stream: modulate(stream, shift_row, scale_row), resid_f)
    (grad_stream,) = pull_norm(grad_normed)
    grad_resid = (
        (cotangent + grad_stream)
        .astype(jnp.bfloat16)
        .reshape(1, plane_count, side_y, side_x, width_model)
    )
    grad_padded = padded_2(grad_resid, (("seq", 1),), 1)[0]
    grad_tokens = (
        grad_resid[0].astype(jnp.float32) + depthwise(grad_padded, conv_kernel[::-1], plane_count)
    ).astype(jnp.bfloat16)
    local_terms = kernel_terms(padded, grad_resid[0], plane_count)
    norm_factor = 1.0 / math.sqrt(
        lax.axis_size("dp") * lax.axis_size("fsdp") * seq_count * row_count
    )
    grad_kernel = lax.psum(local_terms, ("seq", "dp", "fsdp")) * norm_factor
    return (out_rows.reshape(tokens.shape), grad_tokens.reshape(tokens.shape), grad_kernel)


def as_f32(value):
    return value.astype(jnp.float32)


def row_shift(value, step, inner):
    rows = value.shape[0]
    moved = pltpu.roll(value, step % rows, axis=0)
    place = lax.rem(lax.broadcasted_iota(jnp.int32, value.shape, 0), inner)
    return jnp.where(place == (0 if step == 1 else inner - 1), 0.0, moved)


def slab_shift(value, step, inner):
    if step == 0:
        return value
    empty = jnp.zeros((inner, value.shape[1]), value.dtype)
    if step == 1:
        return jnp.concatenate([empty, value[:-inner]], axis=0)
    return jnp.concatenate([value[inner:], empty], axis=0)


def conv_lanes(planes, taps, odd, flipped, inner):
    before, after = (taps[18:27], taps[0:9]) if flipped else (taps[0:9], taps[18:27])
    sided = (jnp.where(odd, before, after), taps[9:18], jnp.where(odd, after, before))
    by_x = []
    for tap_x in range(3):
        total = None
        for tap_y in range(3):
            part = None
            index = 3 * tap_y + tap_x
            index = 8 - index if flipped else index
            for plane, lines in zip(planes, sided):
                term = lines[index : index + 1] * plane
                part = term if part is None else part + term
            part = slab_shift(part, 1 - tap_y, inner)
            total = part if total is None else total + part
        by_x.append(total)
    return by_x[1] + row_shift(by_x[0], 1, inner) + row_shift(by_x[2], -1, inner)


def head_mean(value):
    width = value.shape[1]
    left = lax.broadcasted_iota(jnp.int32, (width, width), 0) // HD
    right = lax.broadcasted_iota(jnp.int32, (width, width), 1) // HD
    same = jnp.where(left == right, 1.0, 0.0).astype(jnp.bfloat16)
    high = value.astype(jnp.bfloat16)
    low = (value - as_f32(high)).astype(jnp.bfloat16)
    total = jnp.dot(high, same, preferred_element_type=jnp.float32)
    total = total + jnp.dot(low, same, preferred_element_type=jnp.float32)
    return total * (1.0 / HD)


def nt_dot(left, right):
    return lax.dot_general(
        left, right, (((1,), (1,)), ((), ())), preferred_element_type=jnp.float32
    )


def tn_dot(left, right):
    return lax.dot_general(
        left, right, (((0,), (0,)), ((), ())), preferred_element_type=jnp.float32
    )


def nn_dot(left, right):
    return jnp.dot(left, right, preferred_element_type=jnp.float32)


def front_body(slots, ids, feats, *rest):
    fetched = rest[:6]
    mod, sends, by_group = rest[6], rest[7 : 7 + slots], rest[7 + slots]
    wt_own, wt_oth, pxrd, wo_own, wo_oth, cot = held = rest[8 + slots : 14 + slots]
    arrive = rest[14 + slots]
    me, half = ids[0], ids[1]
    width = cot.shape[1]
    copies = [
        pltpu.make_async_copy(source, place, arrive.at[i])
        for i, (source, place) in enumerate(zip(fetched, held))
    ]
    for copy in copies:
        copy.start()
    for copy in copies[:3]:
        copy.wait()
    projected = nn_dot(feats[0], wt_own[...]) + nn_dot(feats[1], wt_oth[...])
    for row in range(3):
        cols = slice(row * width, (row + 1) * width)
        mod[row : row + 1, :] = projected[0:1, cols] + pxrd[row]
    for copy in copies[3:]:
        copy.wait()
    gated = (mod[2:3, :] * as_f32(cot[...])).astype(jnp.bfloat16)
    lanes = sends[0].shape[1]
    per_half = wo_own.shape[0] // lanes
    for weight, part in ((wo_own, half), (wo_oth, 1 - half)):
        grads = nt_dot(gated, weight[...]).astype(jnp.bfloat16)
        for j in range(per_half):
            by_group[part * per_half + j] = grads[:, j * lanes : (j + 1) * lanes]
    for k, gap in enumerate(distances(slots)):
        sends[k][...] = by_group[lax.bitwise_xor(me, gap)]


def mix_body(slots, inner, ids, tok, near, far, taps, mod, w_own, w_oth, *rest):
    resid, sections = rest[0], rest[1]
    sends = rest[2 : 2 + slots]
    normed, by_group = rest[2 + slots :]
    me, half = ids[0], ids[1]
    odd = lax.rem(me, 2) == 1
    rows, width = tok.shape
    step = 128
    sums = jnp.zeros((rows, step), jnp.float32)
    for start in range(0, width, step):
        cols = slice(start, start + step)
        planes = [as_f32(ref[:, cols]) for ref in (near, tok, far)]
        mixed = conv_lanes(planes, taps[:, cols], odd, False, inner)
        rounded = (planes[1] + mixed).astype(jnp.bfloat16)
        resid[:, cols] = rounded
        sums = sums + as_f32(rounded)
    mean = jnp.sum(sums, axis=1, keepdims=True) * (1.0 / width)
    squares = jnp.zeros((rows, step), jnp.float32)
    for start in range(0, width, step):
        centre = as_f32(resid[:, start : start + step]) - mean
        squares = squares + centre * centre
    spread = jnp.sum(squares, axis=1, keepdims=True) * (1.0 / width)
    inverse = lax.rsqrt(spread + 1e-06)
    per_half = width // 2
    for start in range(0, width, step):
        cols = slice(start, start + step)
        centre = as_f32(resid[:, cols]) - mean
        value = centre * inverse * (1.0 + mod[1:2, cols]) + mod[0:1, cols]
        inside = start % per_half
        normed[start // per_half, :, inside : inside + step] = value.astype(jnp.bfloat16)
    projected = nn_dot(normed[half], w_own[...]) + nn_dot(normed[1 - half], w_oth[...])
    lanes = sends[0].shape[1] // 3
    inner_width = H * HD
    sections[...] = projected[:, : 2 * inner_width]
    for group in range(slots):
        for part in range(3):
            block = projected[:, part * inner_width + group * lanes :][:, :lanes]
            if part < 2:
                block = block * lax.rsqrt(head_mean(block * block) + 1e-06)
            by_group[group, :, part * lanes : (part + 1) * lanes] = block.astype(jnp.bfloat16)
    for k, gap in enumerate(distances(slots)):
        sends[k][...] = by_group[lax.bitwise_xor(me, gap)]


def attend_body(slots, *refs):
    qkv_in, grads_in = refs[:slots], refs[slots : 2 * slots]
    backs, attns = refs[2 * slots : 3 * slots], refs[3 * slots : 4 * slots]
    weights, probs, dscore = refs[4 * slots :]
    rows, lanes = grads_in[0].shape
    heads = lanes // HD
    count = slots * rows
    scale = 1.0 / math.sqrt(HD)
    step = 64
    zero = jnp.zeros((count, lanes), jnp.bfloat16)
    owner = lax.broadcasted_iota(jnp.int32, (count, lanes), 1) // HD
    masks = [owner == head for head in range(heads)]
    query = jnp.concatenate([ref[:, :lanes] for ref in qkv_in], axis=0)
    key = jnp.concatenate([ref[:, lanes : 2 * lanes] for ref in qkv_in], axis=0)
    value = jnp.concatenate([ref[:, 2 * lanes :] for ref in qkv_in], axis=0)
    grad = jnp.concatenate([ref[...] for ref in grads_in], axis=0)
    scaled = query * jnp.asarray(scale, jnp.bfloat16)
    for head in range(heads):
        weights[head] = nt_dot(jnp.where(masks[head], scaled, zero), key)
    for head in range(heads):
        for start in range(0, count, step):
            span = slice(start, start + step)
            expo = jnp.exp(weights[head, span, :])
            expo = expo * (1.0 / jnp.sum(expo, axis=1, keepdims=True))
            weights[head, span, :] = expo
            probs[span, head * count : (head + 1) * count] = expo.astype(jnp.bfloat16)
    values = jnp.concatenate([jnp.where(mask, value, zero) for mask in masks], axis=0)
    keys = jnp.concatenate([jnp.where(mask, key, zero) for mask in masks], axis=0)
    attn = nn_dot(probs[...], values).astype(jnp.bfloat16)
    for k in range(slots):
        attns[k][...] = attn[k * rows : (k + 1) * rows]
    product = as_f32(attn) * as_f32(grad)
    for head in range(heads):
        delta = jnp.sum(jnp.where(masks[head], product, 0.0), axis=1, keepdims=True)
        dprob = nt_dot(jnp.where(masks[head], grad, zero), value)
        for start in range(0, count, step):
            span = slice(start, start + step)
            part = weights[head, span, :] * (dprob[span] - delta[span])
            dscore[span, head * count : (head + 1) * count] = part.astype(jnp.bfloat16)
    dquery = nn_dot(dscore[...], keys) * scale
    dkeys, dvalues = None, None
    for head in range(heads):
        span = slice(head * count, (head + 1) * count)
        dkey = jnp.where(masks[head], tn_dot(dscore[:, span], scaled), 0.0)
        dvalue = jnp.where(masks[head], tn_dot(probs[:, span], grad), 0.0)
        dkeys = dkey if dkeys is None else dkeys + dkey
        dvalues = dvalue if dvalues is None else dvalues + dvalue
    for k in range(slots):
        span = slice(k * rows, (k + 1) * rows)
        for part, found in enumerate((dquery, dkeys, dvalues)):
            backs[k][:, part * lanes : (part + 1) * lanes] = found[span].astype(jnp.bfloat16)


def tail_body(slots, ids, *refs):
    backs = refs[:slots]
    sections, resid, cot, mod, w_own, w_oth, dresid = refs[slots : slots + 7]
    by_group, dproj, dnormed = refs[slots + 7 :]
    me, half = ids[0], ids[1]
    rows, width = resid.shape
    lanes = by_group.shape[3]
    inner_width = H * HD
    for k, gap in enumerate(distances(slots)):
        group = lax.bitwise_xor(me, gap)
        for part in range(3):
            by_group[group, part] = backs[k][:, part * lanes : (part + 1) * lanes]
    for group in range(slots):
        for part in range(3):
            start = part * inner_width + group * lanes
            grad = by_group[group, part]
            if part < 2:
                grad = as_f32(grad)
                block = sections[:, start : start + lanes]
                inverse = lax.rsqrt(head_mean(block * block) + 1e-06)
                unit = block * inverse
                grad = (inverse * (grad - unit * head_mean(grad * unit))).astype(jnp.bfloat16)
            dproj[:, start : start + lanes] = grad
    dnormed[half] = nt_dot(dproj[...], w_own[...])
    dnormed[1 - half] = nt_dot(dproj[...], w_oth[...])
    step = 128
    per_half = width // 2
    total = jnp.zeros((rows, step), jnp.float32)
    for start in range(0, width, step):
        total = total + as_f32(resid[:, start : start + step])
    mean = jnp.sum(total, axis=1, keepdims=True) * (1.0 / width)
    total = jnp.zeros((rows, step), jnp.float32)
    for start in range(0, width, step):
        centre = as_f32(resid[:, start : start + step]) - mean
        total = total + centre * centre
    inverse = lax.rsqrt(jnp.sum(total, axis=1, keepdims=True) * (1.0 / width) + 1e-06)
    plain = jnp.zeros((rows, step), jnp.float32)
    crossed = jnp.zeros((rows, step), jnp.float32)
    for start in range(0, width, step):
        cols = slice(start, start + step)
        inside = start % per_half
        grad = dnormed[start // per_half, :, inside : inside + step] * (1.0 + mod[1:2, cols])
        unit = (as_f32(resid[:, cols]) - mean) * inverse
        plain = plain + grad
        crossed = crossed + grad * unit
    plain = jnp.sum(plain, axis=1, keepdims=True) * (1.0 / width)
    crossed = jnp.sum(crossed, axis=1, keepdims=True) * (1.0 / width)
    for start in range(0, width, step):
        cols = slice(start, start + step)
        inside = start % per_half
        grad = dnormed[start // per_half, :, inside : inside + step] * (1.0 + mod[1:2, cols])
        unit = (as_f32(resid[:, cols]) - mean) * inverse
        stream = as_f32(cot[:, cols]) + inverse * (grad - plain - unit * crossed)
        dresid[:, cols] = stream.astype(jnp.bfloat16)


def terms_body(inner, ids, dresid, tok, near, far, terms, partial):
    odd = lax.rem(ids[0], 2) == 1
    rows, width = dresid.shape
    step = 128
    for start in range(0, width, step):
        cols = slice(start, start + step)
        grad = as_f32(dresid[:, cols])
        moved = [row_shift(grad, -1, inner), grad, row_shift(grad, 1, inner)]
        found = []
        for ref in (near, tok, far):
            plane = as_f32(ref[:, cols])
            lines = []
            for tap_y in range(3):
                low, high = max(0, 1 - tap_y), max(0, tap_y - 1)
                for tap_x in range(3):
                    prod = (
                        plane[high * inner : rows - low * inner]
                        * moved[tap_x][low * inner : rows - high * inner]
                    )
                    lines.append(jnp.sum(prod.reshape(-1, 8, step), axis=0))
            found.append(lines)
        base = 27 * (start // step)
        for i in range(9):
            by_near, by_far = found[0][i], found[2][i]
            lines = (jnp.where(odd, by_near, by_far), found[1][i], jnp.where(odd, by_far, by_near))
            for tap_z, line in enumerate(lines):
                row = 8 * (base + 9 * tap_z + i)
                partial[row : row + 8, :] = line
    count = terms.shape[0]
    total = partial[pl.ds(0, count, stride=8), :]
    for i in range(1, 8):
        total = total + partial[pl.ds(i, count, stride=8), :]
    terms[...] = total.astype(terms.dtype)


def out_body(slots, ids, *refs):
    attns = refs[:slots]
    resid, mod, wo_own, wo_oth, out, by_group = refs[slots:]
    me, half = ids[0], ids[1]
    lanes = attns[0].shape[1]
    per_half = wo_own.shape[0] // lanes
    for k, gap in enumerate(distances(slots)):
        by_group[lax.bitwise_xor(me, gap)] = attns[k][...]
    total = None
    for weight, part in ((wo_own, half), (wo_oth, 1 - half)):
        for j in range(per_half):
            term = nn_dot(by_group[part * per_half + j], weight[j * lanes : (j + 1) * lanes, :])
            total = term if total is None else total + term
    out[...] = (as_f32(resid[...]) + mod[2:3, :] * total).astype(jnp.bfloat16)


def back_conv_body(inner, ids, grad, near, far, taps, out):
    odd = lax.rem(ids[0], 2) == 1
    width = grad.shape[1]
    step = 128
    for start in range(0, width, step):
        cols = slice(start, start + step)
        planes = [as_f32(ref[:, cols]) for ref in (near, grad, far)]
        mixed = conv_lanes(planes, taps[:, cols], odd, True, inner)
        out[:, cols] = (planes[1] + mixed).astype(jnp.bfloat16)


def tree_sum(values):
    while len(values) > 1:
        values = [values[i] + values[i + 1] for i in range(0, len(values), 2)]
    return values[0]


def sum_body(*refs):
    out = refs[-1]
    out[...] = tree_sum([as_f32(ref[...]) for ref in refs[:-1]]).astype(out.dtype)


def final_body(factor, slots, *refs):
    gaps = distances(slots)
    out = refs[slots]
    total = tree_sum([as_f32(refs[gaps.index(gap)][...]) for gap in range(slots)]) * factor
    lanes = total.shape[1]
    for block in range(out.shape[1] // lanes):
        out[:, block * lanes : (block + 1) * lanes] = total[27 * block : 27 * (block + 1)]


def call(body, name, outs, args, scratch=(), flops=0, scalars=False, far_args=(), vmem=16):
    whole = pl.BlockSpec(memory_space=pltpu.VMEM)
    specs = [whole] * len(args)
    if scalars:
        specs[0] = pl.BlockSpec(memory_space=pltpu.SMEM)
    for i in far_args:
        specs[i] = pl.BlockSpec(memory_space=pltpu.HBM)
    sizes = [math.prod(a.shape) * a.dtype.itemsize for a in list(args) + list(outs)]
    args = [
        pltpu.with_memory_space_constraint(a, pltpu.HBM) if i in far_args else a
        for i, a in enumerate(args)
    ]
    return pl.pallas_call(
        body,
        out_shape=tuple(outs),
        in_specs=specs,
        out_specs=(whole,) * len(outs),
        scratch_shapes=list(scratch),
        compiler_params=pltpu.CompilerParams(vmem_limit_bytes=vmem * 2**20),
        cost_estimate=pl.CostEstimate(flops=flops, bytes_accessed=sum(sizes), transcendentals=0),
        name=name,
    )(*args)


def swapped(value, axis, distance):
    count = lax.axis_size(axis)
    return lax.ppermute(value, axis, [(i, i ^ distance) for i in range(count)])


def distances(slots):
    return (0, 2, 3, 1) if slots == 4 else (0, 1)


def exchanged(pieces):
    pairs = list(zip(pieces, distances(len(pieces))))
    return [pieces[0]] + [swapped(piece, "seq", k) for piece, k in pairs[1:]]


def neighbours(value):
    count = lax.axis_size("seq")
    near = swapped(value, "seq", 1)
    if count == 2:
        return near, jnp.zeros_like(value)
    middle = [(i, i + 1) for i in range(1, count - 1, 2)]
    return near, lax.ppermute(value, "seq", middle + [(j, i) for i, j in middle])


def slab_shards(
    tokens, timesteps, pxrd_mod, time_weight, conv_kernel, qkv_weight, out_weight, out_cot
):
    bf16, f32 = jnp.bfloat16, jnp.float32
    side_y, inner, width = tokens.shape[2:]
    rows = side_y * inner
    slots = lax.axis_size("seq")
    lanes = H * HD // slots
    me = lax.axis_index("seq")
    half = lax.axis_index("fsdp")
    ids = jnp.stack([me, half]).astype(jnp.int32)
    tok = tokens.reshape(rows, width)
    cot = out_cot.reshape(rows, width)
    shape = jax.ShapeDtypeStruct

    wo_oth = swapped(out_weight, "fsdp", 1)
    wt_oth = swapped(time_weight, "fsdp", 1)
    near, far = (pltpu.with_memory_space_constraint(v, pltpu.VMEM) for v in neighbours(tok))
    wq_oth = swapped(qkv_weight, "fsdp", 1)

    freq = 2 * time_weight.shape[0]
    feats = time_features(timesteps, freq).reshape(2, freq // 2)
    own = lax.dynamic_slice_in_dim(feats, half, 1, axis=0)
    oth = lax.dynamic_slice_in_dim(feats, 1 - half, 1, axis=0)
    feats = jnp.broadcast_to(jnp.stack([own, oth]), (2, 8, freq // 2))
    pxrd_rows = pxrd_mod.transpose(1, 0, 2)
    front = call(
        functools.partial(front_body, slots),
        "front",
        [shape((3, width), f32)] + [shape((rows, lanes), bf16)] * slots,
        (ids, feats, time_weight, wt_oth, pxrd_rows, out_weight, wo_oth, cot),
        [pltpu.VMEM((slots, rows, lanes), bf16)]
        + [pltpu.VMEM(time_weight.shape, bf16)] * 2
        + [pltpu.VMEM(pxrd_rows.shape, f32)]
        + [pltpu.VMEM(out_weight.shape, bf16)] * 2
        + [pltpu.VMEM((rows, width), bf16), pltpu.SemaphoreType.DMA((6,))],
        far_args=range(2, 8),
        flops=2 * rows * width * H * HD,
        scalars=True,
    )
    mod = front[0]
    grads_in = exchanged(front[1:])

    mixed = call(
        functools.partial(mix_body, slots, inner),
        "mix",
        [shape((rows, width), bf16), shape((rows, 2 * H * HD), f32)]
        + [shape((rows, 3 * lanes), bf16)] * slots,
        (ids, tok, near, far, conv_kernel, mod, qkv_weight, wq_oth),
        [pltpu.VMEM((2, rows, width // 2), bf16), pltpu.VMEM((slots, rows, 3 * lanes), bf16)],
        flops=2 * rows * width * 3 * H * HD,
        scalars=True,
    )
    resid, sections = mixed[:2]
    sends, grads_in = lax.optimization_barrier((mixed[2:], grads_in))
    qkv_in = exchanged(sends)
    count = slots * rows
    attended = call(
        functools.partial(attend_body, slots),
        "attend",
        [shape((rows, 3 * lanes), bf16)] * slots + [shape((rows, lanes), bf16)] * slots,
        (*qkv_in, *grads_in),
        [
            pltpu.VMEM((lanes // HD, count, count), f32),
            pltpu.VMEM((count, lanes // HD * count), bf16),
            pltpu.VMEM((count, lanes // HD * count), bf16),
        ],
        flops=12 * count * count * lanes,
    )
    backs = exchanged(attended[:slots])
    attns = exchanged(attended[slots:])
    (dresid,) = call(
        functools.partial(tail_body, slots),
        "tail",
        [shape((rows, width), bf16)],
        (ids, *backs, sections, resid, cot, mod, qkv_weight, wq_oth),
        [
            pltpu.VMEM((slots, 3, rows, lanes), bf16),
            pltpu.VMEM((rows, 3 * H * HD), bf16),
            pltpu.VMEM((2, rows, width // 2), f32),
        ],
        flops=2 * rows * width * 3 * H * HD,
        scalars=True,
    )
    dresid, attns = lax.optimization_barrier((dresid, attns))
    (terms,) = call(
        functools.partial(terms_body, inner),
        "terms",
        [shape((27 * width // 128, 128), bf16)],
        (ids, dresid, tok, near, far),
        [pltpu.VMEM((8 * 27 * width // 128, 128), f32)],
        scalars=True,
    )
    (out,) = call(
        functools.partial(out_body, slots),
        "out",
        [shape((rows, width), bf16)],
        (ids, *attns, resid, mod, out_weight, wo_oth),
        [pltpu.VMEM((slots, rows, lanes), bf16)],
        flops=2 * rows * width * H * HD,
        scalars=True,
    )
    grad_near, grad_far = neighbours(dresid)
    pair = ("dp", "fsdp")
    others = [lax.ppermute(terms, pair, [(i, i ^ gap) for i in range(4)]) for gap in (1, 2, 3)]
    others[-1], out = lax.optimization_barrier((others[-1], out))
    (terms,) = call(
        sum_body, "add_dp", [shape((27 * width // 128, 128), bf16)], (terms, *others)
    )
    (token_grad,) = call(
        functools.partial(back_conv_body, inner),
        "back_conv",
        [shape((rows, width), bf16)],
        (ids, dresid, grad_near, grad_far, conv_kernel),
        scalars=True,
    )
    factor = 1.0 / math.sqrt(lax.axis_size("dp") * lax.axis_size("fsdp") * slots * rows)
    pieces = exchanged([terms] * slots)
    pieces[-1], token_grad = lax.optimization_barrier((pieces[-1], token_grad))
    (kernel_grad,) = call(
        functools.partial(final_body, factor, slots), "add_seq", [shape((27, width), f32)], pieces
    )
    return out.reshape(tokens.shape), token_grad.reshape(tokens.shape), kernel_grad


def solution(mesh):
    count = mesh.shape["seq"]

    def pick(*args):
        tokens, time_weight = args[0], args[3]
        lanes = H * HD // count
        fits = (
            count in (2, 4)
            and tokens.shape[0] == 1
            and tokens.shape[1] == 1
            and tokens.shape[3] % 16 == 0
            and lanes % 128 == 0
            and mesh.shape["dp"] == 2
            and mesh.shape["fsdp"] == 2
        )
        return slab_shards(*args) if fits else shards(*args)

    placed = (
        P(("groups", "dp", "fsdp"), "seq", None, None, None),
        P(("groups", "dp", "fsdp")),
        P(("groups", "dp", "fsdp"), None, None),
        P("fsdp", None),
        P(),
        P("fsdp", None),
        P("fsdp", None),
        P(("groups", "dp", "fsdp"), "seq", None, None, None),
    )
    return jax.shard_map(
        pick,
        mesh=mesh,
        in_specs=placed,
        out_specs=(
            P(("groups", "dp", "fsdp"), "seq", None, None, None),
            P(("groups", "dp", "fsdp"), "seq", None, None, None),
            P("groups", None),
        ),
        check_vma=False,
    )
```

```python
import functools
import math

import jax
import jax.numpy as jnp
from jax import lax
from jax.experimental import pallas as pl
from jax.experimental.pallas import tpu as pltpu
from jax.sharding import PartitionSpec as P

H = 8
HD = 64


def padded_2(value, sides, width):
    for axis, dim in sides:
        count, length = (lax.axis_size(axis), value.shape[dim])
        up = [(i, (i + 1) % count) for i in range(count - 1)]
        down = [(j, i) for i, j in up]
        last = lax.slice_in_dim(value, length - width, length, axis=dim)
        leading = lax.slice_in_dim(value, 0, width, axis=dim)
        before = lax.ppermute(last, axis, up)
        after = lax.ppermute(leading, axis, down)
        value = jnp.concatenate([before, value, after], axis=dim)
    return value


def time_features(steps_int, freq_width):
    half_width = freq_width // 2
    freq_index = jnp.arange(half_width).astype(jnp.float32)
    frequency = jnp.exp(freq_index * (-math.log(10000.0) / half_width))
    angles = steps_int.astype(jnp.float32)[:, None] * frequency[None, :]
    return jnp.concatenate([jnp.cos(angles), jnp.sin(angles)], axis=1).astype(jnp.bfloat16)


def modulation(steps_int, pxrd_mod, time_weight):
    features = time_features(steps_int, time_weight.shape[0])
    projected = jnp.dot(features, time_weight, preferred_element_type=jnp.float32)
    return projected.reshape(steps_int.shape[0], 3, time_weight.shape[1] // 3) + pxrd_mod


def depthwise(padded_z, kernel_taps, plane_count):
    framed = jnp.pad(padded_z, ((0, 0), (1, 1), (1, 1), (0, 0)))
    side_y = framed.shape[1] - 2
    side_x = framed.shape[2] - 2
    result = jnp.zeros((plane_count, side_y, side_x, framed.shape[3]), jnp.float32)
    for tap_z in range(3):
        for tap_y in range(3):
            for tap_x in range(3):
                window = framed[
                    tap_z : tap_z + plane_count, tap_y : tap_y + side_y, tap_x : tap_x + side_x
                ]
                result = result + kernel_taps[9 * tap_z + 3 * tap_y + tap_x] * window.astype(
                    jnp.float32
                )
    return result


def kernel_terms(padded_z, upstream, plane_count):
    framed = jnp.pad(padded_z, ((0, 0), (1, 1), (1, 1), (0, 0)))
    side_y = framed.shape[1] - 2
    side_x = framed.shape[2] - 2
    upstream_f = upstream.astype(jnp.float32)
    collected = []
    for tap_z in range(3):
        for tap_y in range(3):
            for tap_x in range(3):
                window = framed[
                    tap_z : tap_z + plane_count, tap_y : tap_y + side_y, tap_x : tap_x + side_x
                ]
                collected.append(jnp.sum(window.astype(jnp.float32) * upstream_f, axis=(0, 1, 2)))
    return jnp.stack(collected)


def modulate(stream, shift_row, scale_row):
    centre = stream - jnp.mean(stream, axis=-1, keepdims=True)
    spread = jnp.mean(centre * centre, axis=-1, keepdims=True)
    return centre * lax.rsqrt(spread + 1e-06) * (1.0 + scale_row) + shift_row


def head_norms(projected):
    row_count = projected.shape[0]
    sections = projected.reshape(row_count, 3, H, HD)
    query_key = sections[:, :2]
    normed = query_key * lax.rsqrt(jnp.mean(query_key * query_key, axis=-1, keepdims=True) + 1e-06)
    return (
        normed[:, 0].reshape(row_count, H * HD),
        normed[:, 1].reshape(row_count, H * HD),
        sections[:, 2].reshape(row_count, H * HD),
    )


def attend_both(queries, grads, key_rows, value_rows):
    count = queries.shape[0]
    heads = queries.shape[1]
    block = min(512, count)
    steps = count // block
    scale_dot = 1.0 / math.sqrt(HD)

    def one_block(carry, pieces):
        query_blk, grad_blk = pieces
        scores = (
            jnp.einsum("qhd,khd->hqk", query_blk, key_rows, preferred_element_type=jnp.float32)
            * scale_dot
        )
        expo = jnp.exp(scores)
        totals = jnp.sum(expo, axis=-1, keepdims=True)
        weights = expo / totals
        probs = weights.astype(jnp.bfloat16)
        attn_blk = jnp.einsum(
            "hqk,khd->qhd", probs, value_rows, preferred_element_type=jnp.float32
        ).astype(jnp.bfloat16)
        delta = jnp.sum(grad_blk.astype(jnp.float32) * attn_blk.astype(jnp.float32), axis=-1).T
        dprob = jnp.einsum("qhd,khd->hqk", grad_blk, value_rows, preferred_element_type=jnp.float32)
        dscore = (weights * (dprob - delta[:, :, None]) * scale_dot).astype(jnp.bfloat16)
        dquery = jnp.einsum("hqk,khd->qhd", dscore, key_rows, preferred_element_type=jnp.float32)
        dkey = carry[0] + jnp.einsum(
            "hqk,qhd->khd", dscore, query_blk, preferred_element_type=jnp.float32
        )
        dvalue = carry[1] + jnp.einsum(
            "hqk,qhd->khd", probs, grad_blk, preferred_element_type=jnp.float32
        )
        return ((dkey, dvalue), (attn_blk, dquery))

    zeros_kv = jnp.zeros(key_rows.shape, jnp.float32)
    (dkey, dvalue), (attn_all, dquery) = lax.scan(
        one_block,
        (zeros_kv, zeros_kv),
        (queries.reshape(steps, block, heads, HD), grads.reshape(steps, block, heads, HD)),
    )
    return (attn_all.reshape(count, heads, HD), dquery.reshape(count, heads, HD), dkey, dvalue)


def shards(tokens, timesteps, pxrd_mod, time_weight, conv_kernel, qkv_weight, out_weight, out_cot):
    w_qkv, w_out, w_time = (
        lax.all_gather(qkv_weight, "fsdp", axis=0, tiled=True),
        lax.all_gather(out_weight, "fsdp", axis=0, tiled=True),
        lax.all_gather(time_weight, "fsdp", axis=0, tiled=True),
    )
    plane_count = tokens.shape[1]
    side_y = tokens.shape[2]
    side_x = tokens.shape[3]
    width_model = tokens.shape[4]
    row_count = plane_count * side_y * side_x
    inner_width = H * HD
    seq_count = lax.axis_size("seq")
    head_groups = min(H, seq_count)
    per_device = H // head_groups
    row_split = seq_count // head_groups
    part_rows = row_count // row_split
    group_width = per_device * HD
    padded = padded_2(tokens, (("seq", 1),), 1)[0]
    mixed = depthwise(padded, conv_kernel, plane_count)
    resid = (
        (tokens[0].astype(jnp.float32) + mixed).astype(jnp.bfloat16).reshape(row_count, width_model)
    )
    modul = modulation(timesteps, pxrd_mod, w_time)
    shift_row = modul[0, 0]
    scale_row = modul[0, 1]
    gate_row = modul[0, 2]
    resid_f = resid.astype(jnp.float32)
    normed = modulate(resid_f, shift_row, scale_row).astype(jnp.bfloat16)
    projected = jnp.dot(normed, w_qkv, preferred_element_type=jnp.float32)
    query_f, key_f, value_f = head_norms(projected)
    cotangent = out_cot[0].reshape(row_count, width_model).astype(jnp.float32)
    gated = (gate_row * cotangent).astype(jnp.bfloat16)
    grad_attn = lax.dot_general(
        gated, w_out, (((1,), (1,)), ((), ())), preferred_element_type=jnp.float32
    ).astype(jnp.bfloat16)

    def to_heads(token_rows):
        shaped = token_rows.reshape(row_split, part_rows, head_groups, group_width)
        return shaped.transpose(2, 0, 1, 3).reshape(seq_count, part_rows, group_width)

    def from_heads(head_rows):
        shaped = head_rows.reshape(head_groups, row_split, part_rows, group_width)
        return shaped.transpose(1, 2, 0, 3).reshape(row_count, inner_width)

    query_heads, grad_heads = (
        lax.all_to_all(
            to_heads(query_f.astype(jnp.bfloat16)), "seq", split_axis=0, concat_axis=0, tiled=True
        ),
        lax.all_to_all(to_heads(grad_attn), "seq", split_axis=0, concat_axis=0, tiled=True),
    )
    query_count = seq_count * part_rows
    query_heads = query_heads.reshape(query_count, per_device, HD)
    grad_heads = grad_heads.reshape(query_count, per_device, HD)
    stacked = jnp.stack(
        [
            key_f.astype(jnp.bfloat16).reshape(row_count, head_groups, group_width),
            value_f.astype(jnp.bfloat16).reshape(row_count, head_groups, group_width),
        ],
        axis=2,
    )
    by_group = stacked.transpose(1, 0, 2, 3).reshape(head_groups, row_count, 2 * group_width)
    copies = jnp.broadcast_to(
        by_group[:, None], (head_groups, row_split, row_count, 2 * group_width)
    )
    arrived = lax.all_to_all(
        copies.reshape(seq_count, row_count, 2 * group_width),
        "seq",
        split_axis=0,
        concat_axis=0,
        tiled=True,
    )
    key_value = arrived.reshape(seq_count * row_count, 2, per_device, HD)
    attn_heads, dquery, dkey, dvalue = attend_both(
        query_heads, grad_heads, key_value[:, 0], key_value[:, 1]
    )
    attn_tok = from_heads(
        lax.all_to_all(
            attn_heads.reshape(seq_count, part_rows, group_width),
            "seq",
            split_axis=0,
            concat_axis=0,
            tiled=True,
        )
    )
    projected_out = jnp.dot(attn_tok, w_out, preferred_element_type=jnp.float32)
    out_rows = (resid_f + gate_row * projected_out).astype(jnp.bfloat16)
    dquery_tok = from_heads(
        lax.all_to_all(
            dquery.reshape(seq_count, part_rows, group_width),
            "seq",
            split_axis=0,
            concat_axis=0,
            tiled=True,
        )
    )
    grads_kv = jnp.stack([dkey, dvalue], axis=1)
    returned = lax.all_to_all(
        grads_kv.reshape(seq_count, row_count, 2 * group_width).astype(jnp.bfloat16),
        "seq",
        split_axis=0,
        concat_axis=0,
        tiled=True,
    ).astype(jnp.float32)
    summed = jnp.sum(returned.reshape(head_groups, row_split, row_count, 2 * group_width), axis=1)
    grads_tok = (
        summed.reshape(head_groups, row_count, 2, group_width)
        .transpose(2, 1, 0, 3)
        .reshape(2, row_count, inner_width)
    )
    _, pullback = jax.vjp(head_norms, projected)
    (grad_projected,) = pullback((dquery_tok, grads_tok[0], grads_tok[1]))
    grad_proj_b = grad_projected.astype(jnp.bfloat16)
    grad_normed = lax.dot_general(
        grad_proj_b, w_qkv, (((1,), (1,)), ((), ())), preferred_element_type=jnp.float32
    )
    _, pull_norm = jax.vjp(lambda stream: modulate(stream, shift_row, scale_row), resid_f)
    (grad_stream,) = pull_norm(grad_normed)
    grad_resid = (
        (cotangent + grad_stream)
        .astype(jnp.bfloat16)
        .reshape(1, plane_count, side_y, side_x, width_model)
    )
    grad_padded = padded_2(grad_resid, (("seq", 1),), 1)[0]
    grad_tokens = (
        grad_resid[0].astype(jnp.float32) + depthwise(grad_padded, conv_kernel[::-1], plane_count)
    ).astype(jnp.bfloat16)
    local_terms = kernel_terms(padded, grad_resid[0], plane_count)
    norm_factor = 1.0 / math.sqrt(
        lax.axis_size("dp") * lax.axis_size("fsdp") * seq_count * row_count
    )
    grad_kernel = lax.psum(local_terms, ("seq", "dp", "fsdp")) * norm_factor
    return (out_rows.reshape(tokens.shape), grad_tokens.reshape(tokens.shape), grad_kernel)


def as_f32(value):
    return value.astype(jnp.float32)


def row_shift(value, step, inner):
    rows = value.shape[0]
    moved = pltpu.roll(value, step % rows, axis=0)
    place = lax.rem(lax.broadcasted_iota(jnp.int32, value.shape, 0), inner)
    return jnp.where(place == (0 if step == 1 else inner - 1), 0.0, moved)


def slab_shift(value, step, inner):
    if step == 0:
        return value
    empty = jnp.zeros((inner, value.shape[1]), value.dtype)
    if step == 1:
        return jnp.concatenate([empty, value[:-inner]], axis=0)
    return jnp.concatenate([value[inner:], empty], axis=0)


def conv_lanes(planes, taps, flipped, inner):
    by_x = []
    for tap_x in range(3):
        total = None
        for tap_y in range(3):
            part = None
            for tap_z, plane in planes.items():
                index = 9 * tap_z + 3 * tap_y + tap_x
                index = 26 - index if flipped else index
                term = taps[index : index + 1] * plane
                part = term if part is None else part + term
            part = slab_shift(part, 1 - tap_y, inner)
            total = part if total is None else total + part
        by_x.append(total)
    return by_x[1] + row_shift(by_x[0], 1, inner) + row_shift(by_x[2], -1, inner)


def sided(odd, near, far, body):
    pl.when(odd)(lambda: body(near, far))
    pl.when(jnp.logical_not(odd))(lambda: body(far, near))


def head_mean(value):
    width = value.shape[1]
    left = lax.broadcasted_iota(jnp.int32, (width, width), 0) // HD
    right = lax.broadcasted_iota(jnp.int32, (width, width), 1) // HD
    same = jnp.where(left == right, 1.0, 0.0).astype(jnp.bfloat16)
    high = value.astype(jnp.bfloat16)
    low = (value - as_f32(high)).astype(jnp.bfloat16)
    total = jnp.dot(high, same, preferred_element_type=jnp.float32)
    total = total + jnp.dot(low, same, preferred_element_type=jnp.float32)
    return total * (1.0 / HD)


def nt_dot(left, right):
    return lax.dot_general(
        left, right, (((1,), (1,)), ((), ())), preferred_element_type=jnp.float32
    )


def tn_dot(left, right):
    return lax.dot_general(
        left, right, (((0,), (0,)), ((), ())), preferred_element_type=jnp.float32
    )


def nn_dot(left, right):
    return jnp.dot(left, right, preferred_element_type=jnp.float32)


def front_body(slots, ids, feats, *rest):
    fetched = rest[:6]
    mod, wo_oth, sends = rest[6], rest[7], rest[8 : 8 + slots]
    by_group, wt_own, wt_oth, pxrd, wo_own, cot, arrive = rest[8 + slots :]
    held = (wt_own, wt_oth, pxrd, wo_own, wo_oth, cot)
    me, half = ids[0], ids[1]
    width = cot.shape[1]
    copies = [
        pltpu.make_async_copy(source, place, arrive.at[i])
        for i, (source, place) in enumerate(zip(fetched, held))
    ]
    for copy in copies:
        copy.start()
    for copy in copies[:3]:
        copy.wait()
    projected = nn_dot(feats[0], wt_own[...]) + nn_dot(feats[1], wt_oth[...])
    for row in range(3):
        cols = slice(row * width, (row + 1) * width)
        mod[row : row + 1, :] = projected[0:1, cols] + pxrd[row]
    for copy in copies[3:]:
        copy.wait()
    gated = (mod[2:3, :] * as_f32(cot[...])).astype(jnp.bfloat16)
    lanes = sends[0].shape[1]
    per_half = wo_own.shape[0] // lanes
    for weight, part in ((wo_own, half), (wo_oth, 1 - half)):
        grads = nt_dot(gated, weight[...]).astype(jnp.bfloat16)
        for j in range(per_half):
            by_group[part * per_half + j] = grads[:, j * lanes : (j + 1) * lanes]
    for k, gap in enumerate(distances(slots)):
        sends[k][...] = by_group[lax.bitwise_xor(me, gap)]


def mix_body(slots, inner, ids, tok, near, far, taps, mod, w_own, w_oth, *rest):
    resid, sections = rest[0], rest[1]
    sends = rest[2 : 2 + slots]
    normed, by_group, sums_ref = rest[2 + slots :]
    me, half = ids[0], ids[1]
    rows, width = tok.shape
    step = 128

    def all_planes(before, after):
        sums = jnp.zeros((rows, step), jnp.float32)
        for start in range(0, width, step):
            cols = slice(start, start + step)
            planes = {i: as_f32(ref[:, cols]) for i, ref in enumerate((before, tok, after))}
            rounded = planes[1] + conv_lanes(planes, taps[:, cols], False, inner)
            rounded = rounded.astype(jnp.bfloat16)
            resid[:, cols] = rounded
            sums = sums + as_f32(rounded)
        sums_ref[...] = sums

    sided(lax.rem(me, 2) == 1, near, far, all_planes)
    sums = sums_ref[...]
    mean = jnp.sum(sums, axis=1, keepdims=True) * (1.0 / width)
    squares = jnp.zeros((rows, step), jnp.float32)
    for start in range(0, width, step):
        centre = as_f32(resid[:, start : start + step]) - mean
        squares = squares + centre * centre
    spread = jnp.sum(squares, axis=1, keepdims=True) * (1.0 / width)
    inverse = lax.rsqrt(spread + 1e-06)
    per_half = width // 2
    for start in range(0, width, step):
        cols = slice(start, start + step)
        centre = as_f32(resid[:, cols]) - mean
        value = centre * inverse * (1.0 + mod[1:2, cols]) + mod[0:1, cols]
        inside = start % per_half
        normed[start // per_half, :, inside : inside + step] = value.astype(jnp.bfloat16)
    projected = nn_dot(normed[half], w_own[...]) + nn_dot(normed[1 - half], w_oth[...])
    lanes = sends[0].shape[1] // 3
    inner_width = H * HD
    sections[...] = projected[:, : 2 * inner_width]
    for group in range(slots):
        for part in range(3):
            block = projected[:, part * inner_width + group * lanes :][:, :lanes]
            if part < 2:
                block = block * lax.rsqrt(head_mean(block * block) + 1e-06)
            by_group[group, :, part * lanes : (part + 1) * lanes] = block.astype(jnp.bfloat16)
    for k, gap in enumerate(distances(slots)):
        sends[k][...] = by_group[lax.bitwise_xor(me, gap)]


def attend_body(slots, *refs):
    qkv_in, grads_in = refs[:slots], refs[slots : 2 * slots]
    backs, attns = refs[2 * slots : 3 * slots], refs[3 * slots : 4 * slots]
    weights, probs, dscore = refs[4 * slots :]
    rows, lanes = grads_in[0].shape
    heads = lanes // HD
    count = slots * rows
    scale = 1.0 / math.sqrt(HD)
    step = 64
    zero = jnp.zeros((count, lanes), jnp.bfloat16)
    owner = lax.broadcasted_iota(jnp.int32, (count, lanes), 1) // HD
    masks = [owner == head for head in range(heads)]
    query = jnp.concatenate([ref[:, :lanes] for ref in qkv_in], axis=0)
    key = jnp.concatenate([ref[:, lanes : 2 * lanes] for ref in qkv_in], axis=0)
    value = jnp.concatenate([ref[:, 2 * lanes :] for ref in qkv_in], axis=0)
    grad = jnp.concatenate([ref[...] for ref in grads_in], axis=0)
    scaled = query * jnp.asarray(scale, jnp.bfloat16)
    for head in range(heads):
        weights[head] = nt_dot(jnp.where(masks[head], scaled, zero), key)
    for head in range(heads):
        for start in range(0, count, step):
            span = slice(start, start + step)
            expo = jnp.exp(weights[head, span, :])
            expo = expo * (1.0 / jnp.sum(expo, axis=1, keepdims=True))
            weights[head, span, :] = expo
            probs[span, head * count : (head + 1) * count] = expo.astype(jnp.bfloat16)
    values = jnp.concatenate([jnp.where(mask, value, zero) for mask in masks], axis=0)
    keys = jnp.concatenate([jnp.where(mask, key, zero) for mask in masks], axis=0)
    attn = nn_dot(probs[...], values).astype(jnp.bfloat16)
    for k in range(slots):
        attns[k][...] = attn[k * rows : (k + 1) * rows]
    product = as_f32(attn) * as_f32(grad)
    for head in range(heads):
        delta = jnp.sum(jnp.where(masks[head], product, 0.0), axis=1, keepdims=True)
        dprob = nt_dot(jnp.where(masks[head], grad, zero), value)
        for start in range(0, count, step):
            span = slice(start, start + step)
            part = weights[head, span, :] * (dprob[span] - delta[span])
            dscore[span, head * count : (head + 1) * count] = part.astype(jnp.bfloat16)
    dquery = nn_dot(dscore[...], keys) * scale
    dkeys, dvalues = None, None
    for head in range(heads):
        span = slice(head * count, (head + 1) * count)
        dkey = jnp.where(masks[head], tn_dot(dscore[:, span], scaled), 0.0)
        dvalue = jnp.where(masks[head], tn_dot(probs[:, span], grad), 0.0)
        dkeys = dkey if dkeys is None else dkeys + dkey
        dvalues = dvalue if dvalues is None else dvalues + dvalue
    for k in range(slots):
        span = slice(k * rows, (k + 1) * rows)
        for part, found in enumerate((dquery, dkeys, dvalues)):
            backs[k][:, part * lanes : (part + 1) * lanes] = found[span].astype(jnp.bfloat16)


def tail_body(slots, inner, ids, *refs):
    backs = refs[:slots]
    sections, resid, cot, mod, w_own, w_oth, tok, near_far, far_far = refs[slots : slots + 9]
    dresid, terms, by_group, dproj, dnormed, partial, near, far, arrive = refs[slots + 9 :]
    me, half = ids[0], ids[1]
    copies = [
        pltpu.make_async_copy(near_far, near, arrive.at[0]),
        pltpu.make_async_copy(far_far, far, arrive.at[1]),
    ]
    for copy in copies:
        copy.start()
    rows, width = resid.shape
    lanes = by_group.shape[3]
    inner_width = H * HD
    for k, gap in enumerate(distances(slots)):
        group = lax.bitwise_xor(me, gap)
        for part in range(3):
            by_group[group, part] = backs[k][:, part * lanes : (part + 1) * lanes]
    for group in range(slots):
        for part in range(3):
            start = part * inner_width + group * lanes
            grad = by_group[group, part]
            if part < 2:
                grad = as_f32(grad)
                block = sections[:, start : start + lanes]
                inverse = lax.rsqrt(head_mean(block * block) + 1e-06)
                unit = block * inverse
                grad = (inverse * (grad - unit * head_mean(grad * unit))).astype(jnp.bfloat16)
            dproj[:, start : start + lanes] = grad
    dnormed[half] = nt_dot(dproj[...], w_own[...])
    dnormed[1 - half] = nt_dot(dproj[...], w_oth[...])
    step = 128
    per_half = width // 2
    total = jnp.zeros((rows, step), jnp.float32)
    for start in range(0, width, step):
        total = total + as_f32(resid[:, start : start + step])
    mean = jnp.sum(total, axis=1, keepdims=True) * (1.0 / width)
    total = jnp.zeros((rows, step), jnp.float32)
    for start in range(0, width, step):
        centre = as_f32(resid[:, start : start + step]) - mean
        total = total + centre * centre
    inverse = lax.rsqrt(jnp.sum(total, axis=1, keepdims=True) * (1.0 / width) + 1e-06)
    plain = jnp.zeros((rows, step), jnp.float32)
    crossed = jnp.zeros((rows, step), jnp.float32)
    for start in range(0, width, step):
        cols = slice(start, start + step)
        inside = start % per_half
        grad = dnormed[start // per_half, :, inside : inside + step] * (1.0 + mod[1:2, cols])
        unit = (as_f32(resid[:, cols]) - mean) * inverse
        plain = plain + grad
        crossed = crossed + grad * unit
    plain = jnp.sum(plain, axis=1, keepdims=True) * (1.0 / width)
    crossed = jnp.sum(crossed, axis=1, keepdims=True) * (1.0 / width)
    for start in range(0, width, step):
        cols = slice(start, start + step)
        inside = start % per_half
        grad = dnormed[start // per_half, :, inside : inside + step] * (1.0 + mod[1:2, cols])
        unit = (as_f32(resid[:, cols]) - mean) * inverse
        stream = as_f32(cot[:, cols]) + inverse * (grad - plain - unit * crossed)
        dresid[:, cols] = stream.astype(jnp.bfloat16)
    for copy in copies:
        copy.wait()
    outer = functools.partial(tap_terms, inner, dresid, tok, partial)
    sided(lax.rem(me, 2) == 1, near, far, outer)
    count = terms.shape[0]
    total = partial[pl.ds(0, count, stride=8), :]
    for i in range(1, 8):
        total = total + partial[pl.ds(i, count, stride=8), :]
    terms[...] = total.astype(terms.dtype)


def tap_terms(inner, dresid, tok, partial, before, after):
    rows, width = dresid.shape
    step = 128
    for start in range(0, width, step):
        cols = slice(start, start + step)
        grad = as_f32(dresid[:, cols])
        moved = [row_shift(grad, -1, inner), grad, row_shift(grad, 1, inner)]
        base = 27 * (start // step)
        for tap_z, ref in enumerate((before, tok, after)):
            plane = as_f32(ref[:, cols])
            for tap_y in range(3):
                low, high = max(0, 1 - tap_y), max(0, tap_y - 1)
                for tap_x in range(3):
                    prod = (
                        plane[high * inner : rows - low * inner]
                        * moved[tap_x][low * inner : rows - high * inner]
                    )
                    row = 8 * (base + 9 * tap_z + 3 * tap_y + tap_x)
                    partial[row : row + 8, :] = jnp.sum(prod.reshape(-1, 8, step), axis=0)


def out_body(slots, ids, *refs):
    attns = refs[:slots]
    resid, mod, wo_own, wo_oth, out, by_group = refs[slots:]
    me, half = ids[0], ids[1]
    lanes = attns[0].shape[1]
    per_half = wo_own.shape[0] // lanes
    for k, gap in enumerate(distances(slots)):
        by_group[lax.bitwise_xor(me, gap)] = attns[k][...]
    total = None
    for weight, part in ((wo_own, half), (wo_oth, 1 - half)):
        for j in range(per_half):
            term = nn_dot(by_group[part * per_half + j], weight[j * lanes : (j + 1) * lanes, :])
            total = term if total is None else total + term
    out[...] = (as_f32(resid[...]) + mod[2:3, :] * total).astype(jnp.bfloat16)


def back_conv_body(inner, ids, grad, near, far, taps, out):
    width = grad.shape[1]
    step = 128

    def all_planes(before, after):
        for start in range(0, width, step):
            cols = slice(start, start + step)
            planes = {i: as_f32(ref[:, cols]) for i, ref in enumerate((before, grad, after))}
            mixed = conv_lanes(planes, taps[:, cols], True, inner)
            out[:, cols] = (planes[1] + mixed).astype(jnp.bfloat16)

    sided(lax.rem(ids[0], 2) == 1, near, far, all_planes)


def tree_sum(values):
    while len(values) > 1:
        values = [values[i] + values[i + 1] for i in range(0, len(values), 2)]
    return values[0]


def sum_body(*refs):
    out = refs[-1]
    out[...] = tree_sum([as_f32(ref[...]) for ref in refs[:-1]]).astype(out.dtype)


def final_body(factor, slots, *refs):
    gaps = distances(slots)
    out = refs[slots]
    total = tree_sum([as_f32(refs[gaps.index(gap)][...]) for gap in range(slots)]) * factor
    lanes = total.shape[1]
    for block in range(out.shape[1] // lanes):
        out[:, block * lanes : (block + 1) * lanes] = total[27 * block : 27 * (block + 1)]


def call(body, name, outs, args, scratch=(), flops=0, scalars=False, far_args=(), vmem=16):
    whole = pl.BlockSpec(memory_space=pltpu.VMEM)
    specs = [whole] * len(args)
    if scalars:
        specs[0] = pl.BlockSpec(memory_space=pltpu.SMEM)
    for i in far_args:
        specs[i] = pl.BlockSpec(memory_space=pltpu.HBM)
    sizes = [math.prod(a.shape) * a.dtype.itemsize for a in list(args) + list(outs)]
    args = [
        pltpu.with_memory_space_constraint(a, pltpu.HBM) if i in far_args else a
        for i, a in enumerate(args)
    ]
    return pl.pallas_call(
        body,
        out_shape=tuple(outs),
        in_specs=specs,
        out_specs=(whole,) * len(outs),
        scratch_shapes=list(scratch),
        compiler_params=pltpu.CompilerParams(vmem_limit_bytes=vmem * 2**20),
        cost_estimate=pl.CostEstimate(flops=flops, bytes_accessed=sum(sizes), transcendentals=0),
        name=name,
    )(*args)


def swapped(value, axis, distance):
    count = lax.axis_size(axis)
    return lax.ppermute(value, axis, [(i, i ^ distance) for i in range(count)])


def distances(slots):
    return (0, 2, 3, 1)[:slots]


def exchanged(pieces):
    pairs = list(zip(pieces, distances(len(pieces))))
    return [pieces[0]] + [swapped(piece, "seq", k) for piece, k in pairs[1:]]


def neighbours(value):
    count = lax.axis_size("seq")
    near = swapped(value, "seq", 1)
    middle = [(i, i + 1) for i in range(1, count - 1, 2)]
    return near, lax.ppermute(value, "seq", middle + [(j, i) for i, j in middle])


def slab_shards(
    tokens, timesteps, pxrd_mod, time_weight, conv_kernel, qkv_weight, out_weight, out_cot
):
    bf16, f32 = jnp.bfloat16, jnp.float32
    side_y, inner, width = tokens.shape[2:]
    rows = side_y * inner
    slots = lax.axis_size("seq")
    lanes = H * HD // slots
    me = lax.axis_index("seq")
    half = lax.axis_index("fsdp")
    ids = jnp.stack([me, half]).astype(jnp.int32)
    tok = tokens.reshape(rows, width)
    cot = out_cot.reshape(rows, width)
    shape = jax.ShapeDtypeStruct

    wo_oth = swapped(out_weight, "fsdp", 1)
    wt_oth = swapped(time_weight, "fsdp", 1)
    near, far = neighbours(tok)
    wq_oth = swapped(qkv_weight, "fsdp", 1)

    freq = 2 * time_weight.shape[0]
    feats = time_features(timesteps, freq).reshape(2, freq // 2)
    own = lax.dynamic_slice_in_dim(feats, half, 1, axis=0)
    oth = lax.dynamic_slice_in_dim(feats, 1 - half, 1, axis=0)
    feats = jnp.broadcast_to(jnp.stack([own, oth]), (2, 8, freq // 2))
    pxrd_rows = pxrd_mod.transpose(1, 0, 2)
    front = call(
        functools.partial(front_body, slots),
        "front",
        [shape((3, width), f32), shape(out_weight.shape, bf16)]
        + [shape((rows, lanes), bf16)] * slots,
        (ids, feats, time_weight, wt_oth, pxrd_rows, out_weight, wo_oth, cot),
        [pltpu.VMEM((slots, rows, lanes), bf16)]
        + [pltpu.VMEM(time_weight.shape, bf16)] * 2
        + [pltpu.VMEM(pxrd_rows.shape, f32)]
        + [pltpu.VMEM(out_weight.shape, bf16)]
        + [pltpu.VMEM((rows, width), bf16), pltpu.SemaphoreType.DMA((6,))],
        far_args=range(2, 8),
        flops=2 * rows * width * H * HD,
        scalars=True,
    )
    mod, wo_held = front[:2]
    grads_in = exchanged(front[2:])

    mixed = call(
        functools.partial(mix_body, slots, inner),
        "mix",
        [shape((rows, width), bf16), shape((rows, 2 * H * HD), f32)]
        + [shape((rows, 3 * lanes), bf16)] * slots,
        (ids, tok, near, far, conv_kernel, mod, qkv_weight, wq_oth),
        [
            pltpu.VMEM((2, rows, width // 2), bf16),
            pltpu.VMEM((slots, rows, 3 * lanes), bf16),
            pltpu.VMEM((rows, 128), f32),
        ],
        flops=2 * rows * width * 3 * H * HD,
        scalars=True,
    )
    resid, sections = mixed[:2]
    sends, grads_in = lax.optimization_barrier((mixed[2:], grads_in))
    qkv_in = exchanged(sends)
    count = slots * rows
    attended = call(
        functools.partial(attend_body, slots),
        "attend",
        [shape((rows, 3 * lanes), bf16)] * slots + [shape((rows, lanes), bf16)] * slots,
        (*qkv_in, *grads_in),
        [
            pltpu.VMEM((lanes // HD, count, count), f32),
            pltpu.VMEM((count, lanes // HD * count), bf16),
            pltpu.VMEM((count, lanes // HD * count), bf16),
        ],
        flops=12 * count * count * lanes,
    )
    backs = exchanged(attended[:slots])
    attns = exchanged(attended[slots:])
    dresid, terms = call(
        functools.partial(tail_body, slots, inner),
        "tail",
        [shape((rows, width), bf16), shape((27 * width // 128, 128), bf16)],
        (ids, *backs, sections, resid, cot, mod, qkv_weight, wq_oth, tok, near, far),
        [
            pltpu.VMEM((slots, 3, rows, lanes), bf16),
            pltpu.VMEM((rows, 3 * H * HD), bf16),
            pltpu.VMEM((2, rows, width // 2), f32),
            pltpu.VMEM((8 * 27 * width // 128, 128), f32),
            pltpu.VMEM((rows, width), bf16),
            pltpu.VMEM((rows, width), bf16),
            pltpu.SemaphoreType.DMA((2,)),
        ],
        flops=2 * rows * width * 3 * H * HD,
        scalars=True,
        far_args=(slots + 8, slots + 9),
    )
    dresid, attns = lax.optimization_barrier((dresid, attns))
    (out,) = call(
        functools.partial(out_body, slots),
        "out",
        [shape((rows, width), bf16)],
        (ids, *attns, resid, mod, out_weight, wo_held),
        [pltpu.VMEM((slots, rows, lanes), bf16)],
        flops=2 * rows * width * H * HD,
        scalars=True,
    )
    grad_near, grad_far = neighbours(dresid)
    pair = ("dp", "fsdp")
    others = [lax.ppermute(terms, pair, [(i, i ^ gap) for i in range(4)]) for gap in (1, 2, 3)]
    others[-1], out = lax.optimization_barrier((others[-1], out))
    (terms,) = call(
        sum_body, "add_dp", [shape((27 * width // 128, 128), bf16)], (terms, *others)
    )
    (token_grad,) = call(
        functools.partial(back_conv_body, inner),
        "back_conv",
        [shape((rows, width), bf16)],
        (ids, dresid, grad_near, grad_far, conv_kernel),
        scalars=True,
    )
    factor = 1.0 / math.sqrt(lax.axis_size("dp") * lax.axis_size("fsdp") * slots * rows)
    pieces = exchanged([terms] * slots)
    pieces[-1], token_grad = lax.optimization_barrier((pieces[-1], token_grad))
    (kernel_grad,) = call(
        functools.partial(final_body, factor, slots), "add_seq", [shape((27, width), f32)], pieces
    )
    return out.reshape(tokens.shape), token_grad.reshape(tokens.shape), kernel_grad


def solution(mesh):
    count = mesh.shape["seq"]

    def pick(*args):
        tokens, time_weight = args[0], args[3]
        lanes = H * HD // count
        fits = (
            count == 4
            and tokens.shape[0] == 1
            and tokens.shape[1] == 1
            and tokens.shape[3] % 16 == 0
            and lanes % 128 == 0
            and mesh.shape["dp"] == 2
            and mesh.shape["fsdp"] == 2
        )
        return slab_shards(*args) if fits else shards(*args)

    placed = (
        P(("groups", "dp", "fsdp"), "seq", None, None, None),
        P(("groups", "dp", "fsdp")),
        P(("groups", "dp", "fsdp"), None, None),
        P("fsdp", None),
        P(),
        P("fsdp", None),
        P("fsdp", None),
        P(("groups", "dp", "fsdp"), "seq", None, None, None),
    )
    return jax.shard_map(
        pick,
        mesh=mesh,
        in_specs=placed,
        out_specs=(
            P(("groups", "dp", "fsdp"), "seq", None, None, None),
            P(("groups", "dp", "fsdp"), "seq", None, None, None),
            P("groups", None),
        ),
        check_vma=False,
    )
```

```python
import functools
import math

import jax
import jax.numpy as jnp
from jax import lax
from jax.experimental import pallas as pl
from jax.experimental.pallas import tpu as pltpu
from jax.sharding import PartitionSpec as P

H = 8
HD = 64


def padded_2(value, sides, width):
    for axis, dim in sides:
        count, length = (lax.axis_size(axis), value.shape[dim])
        up = [(i, (i + 1) % count) for i in range(count - 1)]
        down = [(j, i) for i, j in up]
        last = lax.slice_in_dim(value, length - width, length, axis=dim)
        leading = lax.slice_in_dim(value, 0, width, axis=dim)
        before = lax.ppermute(last, axis, up)
        after = lax.ppermute(leading, axis, down)
        value = jnp.concatenate([before, value, after], axis=dim)
    return value


def time_features(steps_int, freq_width):
    half_width = freq_width // 2
    freq_index = jnp.arange(half_width).astype(jnp.float32)
    frequency = jnp.exp(freq_index * (-math.log(10000.0) / half_width))
    angles = steps_int.astype(jnp.float32)[:, None] * frequency[None, :]
    return jnp.concatenate([jnp.cos(angles), jnp.sin(angles)], axis=1).astype(jnp.bfloat16)


def modulation(steps_int, pxrd_mod, time_weight):
    features = time_features(steps_int, time_weight.shape[0])
    projected = jnp.dot(features, time_weight, preferred_element_type=jnp.float32)
    return projected.reshape(steps_int.shape[0], 3, time_weight.shape[1] // 3) + pxrd_mod


def depthwise(padded_z, kernel_taps, plane_count):
    framed = jnp.pad(padded_z, ((0, 0), (1, 1), (1, 1), (0, 0)))
    side_y = framed.shape[1] - 2
    side_x = framed.shape[2] - 2
    result = jnp.zeros((plane_count, side_y, side_x, framed.shape[3]), jnp.float32)
    for tap_z in range(3):
        for tap_y in range(3):
            for tap_x in range(3):
                window = framed[
                    tap_z : tap_z + plane_count, tap_y : tap_y + side_y, tap_x : tap_x + side_x
                ]
                result = result + kernel_taps[9 * tap_z + 3 * tap_y + tap_x] * window.astype(
                    jnp.float32
                )
    return result


def kernel_terms(padded_z, upstream, plane_count):
    framed = jnp.pad(padded_z, ((0, 0), (1, 1), (1, 1), (0, 0)))
    side_y = framed.shape[1] - 2
    side_x = framed.shape[2] - 2
    upstream_f = upstream.astype(jnp.float32)
    collected = []
    for tap_z in range(3):
        for tap_y in range(3):
            for tap_x in range(3):
                window = framed[
                    tap_z : tap_z + plane_count, tap_y : tap_y + side_y, tap_x : tap_x + side_x
                ]
                collected.append(jnp.sum(window.astype(jnp.float32) * upstream_f, axis=(0, 1, 2)))
    return jnp.stack(collected)


def modulate(stream, shift_row, scale_row):
    centre = stream - jnp.mean(stream, axis=-1, keepdims=True)
    spread = jnp.mean(centre * centre, axis=-1, keepdims=True)
    return centre * lax.rsqrt(spread + 1e-06) * (1.0 + scale_row) + shift_row


def head_norms(projected):
    row_count = projected.shape[0]
    sections = projected.reshape(row_count, 3, H, HD)
    query_key = sections[:, :2]
    normed = query_key * lax.rsqrt(jnp.mean(query_key * query_key, axis=-1, keepdims=True) + 1e-06)
    return (
        normed[:, 0].reshape(row_count, H * HD),
        normed[:, 1].reshape(row_count, H * HD),
        sections[:, 2].reshape(row_count, H * HD),
    )


def attend_both(queries, grads, key_rows, value_rows):
    count = queries.shape[0]
    heads = queries.shape[1]
    block = min(512, count)
    steps = count // block
    scale_dot = 1.0 / math.sqrt(HD)

    def one_block(carry, pieces):
        query_blk, grad_blk = pieces
        scores = (
            jnp.einsum("qhd,khd->hqk", query_blk, key_rows, preferred_element_type=jnp.float32)
            * scale_dot
        )
        expo = jnp.exp(scores)
        totals = jnp.sum(expo, axis=-1, keepdims=True)
        weights = expo / totals
        probs = weights.astype(jnp.bfloat16)
        attn_blk = jnp.einsum(
            "hqk,khd->qhd", probs, value_rows, preferred_element_type=jnp.float32
        ).astype(jnp.bfloat16)
        delta = jnp.sum(grad_blk.astype(jnp.float32) * attn_blk.astype(jnp.float32), axis=-1).T
        dprob = jnp.einsum("qhd,khd->hqk", grad_blk, value_rows, preferred_element_type=jnp.float32)
        dscore = (weights * (dprob - delta[:, :, None]) * scale_dot).astype(jnp.bfloat16)
        dquery = jnp.einsum("hqk,khd->qhd", dscore, key_rows, preferred_element_type=jnp.float32)
        dkey = carry[0] + jnp.einsum(
            "hqk,qhd->khd", dscore, query_blk, preferred_element_type=jnp.float32
        )
        dvalue = carry[1] + jnp.einsum(
            "hqk,qhd->khd", probs, grad_blk, preferred_element_type=jnp.float32
        )
        return ((dkey, dvalue), (attn_blk, dquery))

    zeros_kv = jnp.zeros(key_rows.shape, jnp.float32)
    (dkey, dvalue), (attn_all, dquery) = lax.scan(
        one_block,
        (zeros_kv, zeros_kv),
        (queries.reshape(steps, block, heads, HD), grads.reshape(steps, block, heads, HD)),
    )
    return (attn_all.reshape(count, heads, HD), dquery.reshape(count, heads, HD), dkey, dvalue)


def shards(tokens, timesteps, pxrd_mod, time_weight, conv_kernel, qkv_weight, out_weight, out_cot):
    w_qkv, w_out, w_time = (
        lax.all_gather(qkv_weight, "fsdp", axis=0, tiled=True),
        lax.all_gather(out_weight, "fsdp", axis=0, tiled=True),
        lax.all_gather(time_weight, "fsdp", axis=0, tiled=True),
    )
    plane_count = tokens.shape[1]
    side_y = tokens.shape[2]
    side_x = tokens.shape[3]
    width_model = tokens.shape[4]
    row_count = plane_count * side_y * side_x
    inner_width = H * HD
    seq_count = lax.axis_size("seq")
    head_groups = min(H, seq_count)
    per_device = H // head_groups
    row_split = seq_count // head_groups
    part_rows = row_count // row_split
    group_width = per_device * HD
    padded = padded_2(tokens, (("seq", 1),), 1)[0]
    mixed = depthwise(padded, conv_kernel, plane_count)
    resid = (
        (tokens[0].astype(jnp.float32) + mixed).astype(jnp.bfloat16).reshape(row_count, width_model)
    )
    modul = modulation(timesteps, pxrd_mod, w_time)
    shift_row = modul[0, 0]
    scale_row = modul[0, 1]
    gate_row = modul[0, 2]
    resid_f = resid.astype(jnp.float32)
    normed = modulate(resid_f, shift_row, scale_row).astype(jnp.bfloat16)
    projected = jnp.dot(normed, w_qkv, preferred_element_type=jnp.float32)
    query_f, key_f, value_f = head_norms(projected)
    cotangent = out_cot[0].reshape(row_count, width_model).astype(jnp.float32)
    gated = (gate_row * cotangent).astype(jnp.bfloat16)
    grad_attn = lax.dot_general(
        gated, w_out, (((1,), (1,)), ((), ())), preferred_element_type=jnp.float32
    ).astype(jnp.bfloat16)

    def to_heads(token_rows):
        shaped = token_rows.reshape(row_split, part_rows, head_groups, group_width)
        return shaped.transpose(2, 0, 1, 3).reshape(seq_count, part_rows, group_width)

    def from_heads(head_rows):
        shaped = head_rows.reshape(head_groups, row_split, part_rows, group_width)
        return shaped.transpose(1, 2, 0, 3).reshape(row_count, inner_width)

    query_heads, grad_heads = (
        lax.all_to_all(
            to_heads(query_f.astype(jnp.bfloat16)), "seq", split_axis=0, concat_axis=0, tiled=True
        ),
        lax.all_to_all(to_heads(grad_attn), "seq", split_axis=0, concat_axis=0, tiled=True),
    )
    query_count = seq_count * part_rows
    query_heads = query_heads.reshape(query_count, per_device, HD)
    grad_heads = grad_heads.reshape(query_count, per_device, HD)
    stacked = jnp.stack(
        [
            key_f.astype(jnp.bfloat16).reshape(row_count, head_groups, group_width),
            value_f.astype(jnp.bfloat16).reshape(row_count, head_groups, group_width),
        ],
        axis=2,
    )
    by_group = stacked.transpose(1, 0, 2, 3).reshape(head_groups, row_count, 2 * group_width)
    copies = jnp.broadcast_to(
        by_group[:, None], (head_groups, row_split, row_count, 2 * group_width)
    )
    arrived = lax.all_to_all(
        copies.reshape(seq_count, row_count, 2 * group_width),
        "seq",
        split_axis=0,
        concat_axis=0,
        tiled=True,
    )
    key_value = arrived.reshape(seq_count * row_count, 2, per_device, HD)
    attn_heads, dquery, dkey, dvalue = attend_both(
        query_heads, grad_heads, key_value[:, 0], key_value[:, 1]
    )
    attn_tok = from_heads(
        lax.all_to_all(
            attn_heads.reshape(seq_count, part_rows, group_width),
            "seq",
            split_axis=0,
            concat_axis=0,
            tiled=True,
        )
    )
    projected_out = jnp.dot(attn_tok, w_out, preferred_element_type=jnp.float32)
    out_rows = (resid_f + gate_row * projected_out).astype(jnp.bfloat16)
    dquery_tok = from_heads(
        lax.all_to_all(
            dquery.reshape(seq_count, part_rows, group_width),
            "seq",
            split_axis=0,
            concat_axis=0,
            tiled=True,
        )
    )
    grads_kv = jnp.stack([dkey, dvalue], axis=1)
    returned = lax.all_to_all(
        grads_kv.reshape(seq_count, row_count, 2 * group_width).astype(jnp.bfloat16),
        "seq",
        split_axis=0,
        concat_axis=0,
        tiled=True,
    ).astype(jnp.float32)
    summed = jnp.sum(returned.reshape(head_groups, row_split, row_count, 2 * group_width), axis=1)
    grads_tok = (
        summed.reshape(head_groups, row_count, 2, group_width)
        .transpose(2, 1, 0, 3)
        .reshape(2, row_count, inner_width)
    )
    _, pullback = jax.vjp(head_norms, projected)
    (grad_projected,) = pullback((dquery_tok, grads_tok[0], grads_tok[1]))
    grad_proj_b = grad_projected.astype(jnp.bfloat16)
    grad_normed = lax.dot_general(
        grad_proj_b, w_qkv, (((1,), (1,)), ((), ())), preferred_element_type=jnp.float32
    )
    _, pull_norm = jax.vjp(lambda stream: modulate(stream, shift_row, scale_row), resid_f)
    (grad_stream,) = pull_norm(grad_normed)
    grad_resid = (
        (cotangent + grad_stream)
        .astype(jnp.bfloat16)
        .reshape(1, plane_count, side_y, side_x, width_model)
    )
    grad_padded = padded_2(grad_resid, (("seq", 1),), 1)[0]
    grad_tokens = (
        grad_resid[0].astype(jnp.float32) + depthwise(grad_padded, conv_kernel[::-1], plane_count)
    ).astype(jnp.bfloat16)
    local_terms = kernel_terms(padded, grad_resid[0], plane_count)
    norm_factor = 1.0 / math.sqrt(
        lax.axis_size("dp") * lax.axis_size("fsdp") * seq_count * row_count
    )
    grad_kernel = lax.psum(local_terms, ("seq", "dp", "fsdp")) * norm_factor
    return (out_rows.reshape(tokens.shape), grad_tokens.reshape(tokens.shape), grad_kernel)


def as_f32(value):
    return value.astype(jnp.float32)


def row_shift(value, step, inner):
    rows = value.shape[0]
    moved = pltpu.roll(value, step % rows, axis=0)
    place = lax.rem(lax.broadcasted_iota(jnp.int32, value.shape, 0), inner)
    return jnp.where(place == (0 if step == 1 else inner - 1), 0.0, moved)


def slab_shift(value, step, inner):
    if step == 0:
        return value
    empty = jnp.zeros((inner, value.shape[1]), value.dtype)
    if step == 1:
        return jnp.concatenate([empty, value[:-inner]], axis=0)
    return jnp.concatenate([value[inner:], empty], axis=0)


def conv_lanes(planes, taps, flipped, inner):
    by_x = []
    for tap_x in range(3):
        total = None
        for tap_y in range(3):
            part = None
            for tap_z, plane in planes.items():
                index = 9 * tap_z + 3 * tap_y + tap_x
                index = 26 - index if flipped else index
                term = taps[index : index + 1] * plane
                part = term if part is None else part + term
            part = slab_shift(part, 1 - tap_y, inner)
            total = part if total is None else total + part
        by_x.append(total)
    return by_x[1] + row_shift(by_x[0], 1, inner) + row_shift(by_x[2], -1, inner)


def sided(odd, near, far, body):
    pl.when(odd)(lambda: body(near, far))
    pl.when(jnp.logical_not(odd))(lambda: body(far, near))


def head_mean(value):
    width = value.shape[1]
    left = lax.broadcasted_iota(jnp.int32, (width, width), 0) // HD
    right = lax.broadcasted_iota(jnp.int32, (width, width), 1) // HD
    same = jnp.where(left == right, 1.0, 0.0).astype(jnp.bfloat16)
    high = value.astype(jnp.bfloat16)
    low = (value - as_f32(high)).astype(jnp.bfloat16)
    total = jnp.dot(high, same, preferred_element_type=jnp.float32)
    total = total + jnp.dot(low, same, preferred_element_type=jnp.float32)
    return total * (1.0 / HD)


def nt_dot(left, right):
    return lax.dot_general(
        left, right, (((1,), (1,)), ((), ())), preferred_element_type=jnp.float32
    )


def tn_dot(left, right):
    return lax.dot_general(
        left, right, (((0,), (0,)), ((), ())), preferred_element_type=jnp.float32
    )


def nn_dot(left, right):
    return jnp.dot(left, right, preferred_element_type=jnp.float32)


def front_body(slots, ids, feats, *rest):
    fetched = rest[:6]
    mod, wo_oth, sends = rest[6], rest[7], rest[8 : 8 + slots]
    by_group, wt_own, wt_oth, pxrd, wo_own, cot, arrive = rest[8 + slots :]
    held = (wt_own, wt_oth, pxrd, wo_own, wo_oth, cot)
    me, half = ids[0], ids[1]
    width = cot.shape[1]
    copies = [
        pltpu.make_async_copy(source, place, arrive.at[i])
        for i, (source, place) in enumerate(zip(fetched, held))
    ]
    for copy in copies:
        copy.start()
    for copy in copies[:3]:
        copy.wait()
    projected = nn_dot(feats[0], wt_own[...]) + nn_dot(feats[1], wt_oth[...])
    for row in range(3):
        cols = slice(row * width, (row + 1) * width)
        mod[row : row + 1, :] = projected[0:1, cols] + pxrd[row]
    for copy in copies[3:]:
        copy.wait()
    gated = (mod[2:3, :] * as_f32(cot[...])).astype(jnp.bfloat16)
    lanes = sends[0].shape[1]
    per_half = wo_own.shape[0] // lanes
    for weight, part in ((wo_own, half), (wo_oth, 1 - half)):
        grads = nt_dot(gated, weight[...]).astype(jnp.bfloat16)
        for j in range(per_half):
            by_group[part * per_half + j] = grads[:, j * lanes : (j + 1) * lanes]
    for k, gap in enumerate(distances(slots)):
        sends[k][...] = by_group[lax.bitwise_xor(me, gap)]


def mix_body(slots, inner, ids, tok, near, far, taps, mod, w_own, w_oth, *rest):
    resid, sections = rest[0], rest[1]
    sends = rest[2 : 2 + slots]
    normed, by_group, sums_ref = rest[2 + slots :]
    me, half = ids[0], ids[1]
    rows, width = tok.shape
    step = 128

    def all_planes(before, after):
        sums = jnp.zeros((rows, step), jnp.float32)
        for start in range(0, width, step):
            cols = slice(start, start + step)
            planes = {i: as_f32(ref[:, cols]) for i, ref in enumerate((before, tok, after))}
            rounded = planes[1] + conv_lanes(planes, taps[:, cols], False, inner)
            rounded = rounded.astype(jnp.bfloat16)
            resid[:, cols] = rounded
            sums = sums + as_f32(rounded)
        sums_ref[...] = sums

    sided(lax.rem(me, 2) == 1, near, far, all_planes)
    sums = sums_ref[...]
    mean = jnp.sum(sums, axis=1, keepdims=True) * (1.0 / width)
    squares = jnp.zeros((rows, step), jnp.float32)
    for start in range(0, width, step):
        centre = as_f32(resid[:, start : start + step]) - mean
        squares = squares + centre * centre
    spread = jnp.sum(squares, axis=1, keepdims=True) * (1.0 / width)
    inverse = lax.rsqrt(spread + 1e-06)
    per_half = width // 2
    for start in range(0, width, step):
        cols = slice(start, start + step)
        centre = as_f32(resid[:, cols]) - mean
        value = centre * inverse * (1.0 + mod[1:2, cols]) + mod[0:1, cols]
        inside = start % per_half
        normed[start // per_half, :, inside : inside + step] = value.astype(jnp.bfloat16)
    projected = nn_dot(normed[half], w_own[...]) + nn_dot(normed[1 - half], w_oth[...])
    lanes = sends[0].shape[1] // 3
    inner_width = H * HD
    sections[...] = projected[:, : 2 * inner_width]
    for group in range(slots):
        for part in range(3):
            block = projected[:, part * inner_width + group * lanes :][:, :lanes]
            if part < 2:
                block = block * lax.rsqrt(head_mean(block * block) + 1e-06)
            by_group[group, :, part * lanes : (part + 1) * lanes] = block.astype(jnp.bfloat16)
    for k, gap in enumerate(distances(slots)):
        sends[k][...] = by_group[lax.bitwise_xor(me, gap)]


def attend_body(slots, *refs):
    qkv_in, grads_in = refs[:slots], refs[slots : 2 * slots]
    backs, attns = refs[2 * slots : 3 * slots], refs[3 * slots : 4 * slots]
    weights, probs, dscore = refs[4 * slots :]
    rows, lanes = grads_in[0].shape
    heads = lanes // HD
    count = slots * rows
    scale = 1.0 / math.sqrt(HD)
    step = 64
    zero = jnp.zeros((count, lanes), jnp.bfloat16)
    owner = lax.broadcasted_iota(jnp.int32, (count, lanes), 1) // HD
    masks = [owner == head for head in range(heads)]
    query = jnp.concatenate([ref[:, :lanes] for ref in qkv_in], axis=0)
    key = jnp.concatenate([ref[:, lanes : 2 * lanes] for ref in qkv_in], axis=0)
    value = jnp.concatenate([ref[:, 2 * lanes :] for ref in qkv_in], axis=0)
    grad = jnp.concatenate([ref[...] for ref in grads_in], axis=0)
    scaled = query * jnp.asarray(scale, jnp.bfloat16)
    for head in range(heads):
        weights[head] = nt_dot(jnp.where(masks[head], scaled, zero), key)
    for head in range(heads):
        for start in range(0, count, step):
            span = slice(start, start + step)
            expo = jnp.exp(weights[head, span, :])
            expo = expo * (1.0 / jnp.sum(expo, axis=1, keepdims=True))
            weights[head, span, :] = expo
            probs[span, head * count : (head + 1) * count] = expo.astype(jnp.bfloat16)
    values = jnp.concatenate([jnp.where(mask, value, zero) for mask in masks], axis=0)
    keys = jnp.concatenate([jnp.where(mask, key, zero) for mask in masks], axis=0)
    attn = nn_dot(probs[...], values).astype(jnp.bfloat16)
    for k in range(slots):
        attns[k][...] = attn[k * rows : (k + 1) * rows]
    product = as_f32(attn) * as_f32(grad)
    for head in range(heads):
        delta = jnp.sum(jnp.where(masks[head], product, 0.0), axis=1, keepdims=True)
        dprob = nt_dot(jnp.where(masks[head], grad, zero), value)
        for start in range(0, count, step):
            span = slice(start, start + step)
            part = weights[head, span, :] * (dprob[span] - delta[span])
            dscore[span, head * count : (head + 1) * count] = part.astype(jnp.bfloat16)
    dquery = nn_dot(dscore[...], keys) * scale
    dkeys, dvalues = None, None
    for head in range(heads):
        span = slice(head * count, (head + 1) * count)
        dkey = jnp.where(masks[head], tn_dot(dscore[:, span], scaled), 0.0)
        dvalue = jnp.where(masks[head], tn_dot(probs[:, span], grad), 0.0)
        dkeys = dkey if dkeys is None else dkeys + dkey
        dvalues = dvalue if dvalues is None else dvalues + dvalue
    for k in range(slots):
        span = slice(k * rows, (k + 1) * rows)
        for part, found in enumerate((dquery, dkeys, dvalues)):
            backs[k][:, part * lanes : (part + 1) * lanes] = found[span].astype(jnp.bfloat16)


def tail_body(slots, inner, ids, *refs):
    backs = refs[:slots]
    sections, resid, cot, mod, w_own, w_oth, tok, near_far, far_far = refs[slots : slots + 9]
    dresid, terms, by_group, dproj, dnormed, partial, near, far, arrive = refs[slots + 9 :]
    me, half = ids[0], ids[1]
    copies = [
        pltpu.make_async_copy(near_far, near, arrive.at[0]),
        pltpu.make_async_copy(far_far, far, arrive.at[1]),
    ]
    for copy in copies:
        copy.start()
    rows, width = resid.shape
    lanes = by_group.shape[3]
    inner_width = H * HD
    for k, gap in enumerate(distances(slots)):
        group = lax.bitwise_xor(me, gap)
        for part in range(3):
            by_group[group, part] = backs[k][:, part * lanes : (part + 1) * lanes]
    for group in range(slots):
        for part in range(3):
            start = part * inner_width + group * lanes
            grad = by_group[group, part]
            if part < 2:
                grad = as_f32(grad)
                block = sections[:, start : start + lanes]
                inverse = lax.rsqrt(head_mean(block * block) + 1e-06)
                unit = block * inverse
                grad = (inverse * (grad - unit * head_mean(grad * unit))).astype(jnp.bfloat16)
            dproj[:, start : start + lanes] = grad
    dnormed[half] = nt_dot(dproj[...], w_own[...])
    dnormed[1 - half] = nt_dot(dproj[...], w_oth[...])
    step = 128
    per_half = width // 2
    total = jnp.zeros((rows, step), jnp.float32)
    for start in range(0, width, step):
        total = total + as_f32(resid[:, start : start + step])
    mean = jnp.sum(total, axis=1, keepdims=True) * (1.0 / width)
    total = jnp.zeros((rows, step), jnp.float32)
    for start in range(0, width, step):
        centre = as_f32(resid[:, start : start + step]) - mean
        total = total + centre * centre
    inverse = lax.rsqrt(jnp.sum(total, axis=1, keepdims=True) * (1.0 / width) + 1e-06)
    plain = jnp.zeros((rows, step), jnp.float32)
    crossed = jnp.zeros((rows, step), jnp.float32)
    for start in range(0, width, step):
        cols = slice(start, start + step)
        inside = start % per_half
        grad = dnormed[start // per_half, :, inside : inside + step] * (1.0 + mod[1:2, cols])
        unit = (as_f32(resid[:, cols]) - mean) * inverse
        plain = plain + grad
        crossed = crossed + grad * unit
    plain = jnp.sum(plain, axis=1, keepdims=True) * (1.0 / width)
    crossed = jnp.sum(crossed, axis=1, keepdims=True) * (1.0 / width)
    for start in range(0, width, step):
        cols = slice(start, start + step)
        inside = start % per_half
        grad = dnormed[start // per_half, :, inside : inside + step] * (1.0 + mod[1:2, cols])
        unit = (as_f32(resid[:, cols]) - mean) * inverse
        stream = as_f32(cot[:, cols]) + inverse * (grad - plain - unit * crossed)
        dresid[:, cols] = stream.astype(jnp.bfloat16)
    for copy in copies:
        copy.wait()
    outer = functools.partial(tap_terms, inner, dresid, tok, partial)
    sided(lax.rem(me, 2) == 1, near, far, outer)
    count = terms.shape[0]
    total = partial[pl.ds(0, count, stride=8), :]
    for i in range(1, 8):
        total = total + partial[pl.ds(i, count, stride=8), :]
    terms[...] = total.astype(terms.dtype)


def tap_terms(inner, dresid, tok, partial, before, after):
    rows, width = dresid.shape
    step = 128
    for start in range(0, width, step):
        cols = slice(start, start + step)
        grad = as_f32(dresid[:, cols])
        moved = [row_shift(grad, -1, inner), grad, row_shift(grad, 1, inner)]
        base = 27 * (start // step)
        for tap_z, ref in enumerate((before, tok, after)):
            plane = as_f32(ref[:, cols])
            for tap_y in range(3):
                low, high = max(0, 1 - tap_y), max(0, tap_y - 1)
                for tap_x in range(3):
                    prod = (
                        plane[high * inner : rows - low * inner]
                        * moved[tap_x][low * inner : rows - high * inner]
                    )
                    row = 8 * (base + 9 * tap_z + 3 * tap_y + tap_x)
                    partial[row : row + 8, :] = jnp.sum(prod.reshape(-1, 8, step), axis=0)


def out_body(slots, ids, *refs):
    attns = refs[:slots]
    resid, mod, wo_own, wo_oth, out, by_group = refs[slots:]
    me, half = ids[0], ids[1]
    lanes = attns[0].shape[1]
    per_half = wo_own.shape[0] // lanes
    for k, gap in enumerate(distances(slots)):
        by_group[lax.bitwise_xor(me, gap)] = attns[k][...]
    total = None
    for weight, part in ((wo_own, half), (wo_oth, 1 - half)):
        for j in range(per_half):
            term = nn_dot(by_group[part * per_half + j], weight[j * lanes : (j + 1) * lanes, :])
            total = term if total is None else total + term
    out[...] = (as_f32(resid[...]) + mod[2:3, :] * total).astype(jnp.bfloat16)


def back_conv_body(inner, ids, grad, near, far, taps, out):
    width = grad.shape[1]
    step = 128

    def all_planes(before, after):
        for start in range(0, width, step):
            cols = slice(start, start + step)
            planes = {i: as_f32(ref[:, cols]) for i, ref in enumerate((before, grad, after))}
            mixed = conv_lanes(planes, taps[:, cols], True, inner)
            out[:, cols] = (planes[1] + mixed).astype(jnp.bfloat16)

    sided(lax.rem(ids[0], 2) == 1, near, far, all_planes)


def tree_sum(values):
    while len(values) > 1:
        values = [values[i] + values[i + 1] for i in range(0, len(values), 2)]
    return values[0]


def sum_body(*refs):
    out = refs[-1]
    out[...] = tree_sum([as_f32(ref[...]) for ref in refs[:-1]]).astype(out.dtype)


def seq_sum_body(slots, *refs):
    gaps = distances(slots)
    refs[slots][...] = tree_sum([refs[gaps.index(gap)][...].astype(jnp.float32) for gap in range(slots)])


def final_body(factor, left, right, out):
    total = (left[...] + right[...]) * factor
    lanes = total.shape[1]
    for block in range(out.shape[1] // lanes):
        out[:, block * lanes : (block + 1) * lanes] = total[27 * block : 27 * (block + 1)]


def call(body, name, outs, args, scratch=(), flops=0, scalars=False, far_args=(), vmem=16):
    whole = pl.BlockSpec(memory_space=pltpu.VMEM)
    specs = [whole] * len(args)
    if scalars:
        specs[0] = pl.BlockSpec(memory_space=pltpu.SMEM)
    for i in far_args:
        specs[i] = pl.BlockSpec(memory_space=pltpu.HBM)
    sizes = [math.prod(a.shape) * a.dtype.itemsize for a in list(args) + list(outs)]
    args = [
        pltpu.with_memory_space_constraint(a, pltpu.HBM) if i in far_args else a
        for i, a in enumerate(args)
    ]
    return pl.pallas_call(
        body,
        out_shape=tuple(outs),
        in_specs=specs,
        out_specs=(whole,) * len(outs),
        scratch_shapes=list(scratch),
        compiler_params=pltpu.CompilerParams(vmem_limit_bytes=vmem * 2**20),
        cost_estimate=pl.CostEstimate(flops=flops, bytes_accessed=sum(sizes), transcendentals=0),
        name=name,
    )(*args)


def swapped(value, axis, distance):
    count = lax.axis_size(axis)
    return lax.ppermute(value, axis, [(i, i ^ distance) for i in range(count)])


def distances(slots):
    return (0, 2, 3, 1)[:slots]


def exchanged(pieces):
    pairs = list(zip(pieces, distances(len(pieces))))
    return [pieces[0]] + [swapped(piece, "seq", k) for piece, k in pairs[1:]]


def neighbours(value):
    count = lax.axis_size("seq")
    near = swapped(value, "seq", 1)
    middle = [(i, i + 1) for i in range(1, count - 1, 2)]
    return near, lax.ppermute(value, "seq", middle + [(j, i) for i, j in middle])


def slab_shards(
    tokens, timesteps, pxrd_mod, time_weight, conv_kernel, qkv_weight, out_weight, out_cot
):
    bf16, f32 = jnp.bfloat16, jnp.float32
    side_y, inner, width = tokens.shape[2:]
    rows = side_y * inner
    slots = lax.axis_size("seq")
    lanes = H * HD // slots
    me = lax.axis_index("seq")
    half = lax.axis_index("fsdp")
    ids = jnp.stack([me, half]).astype(jnp.int32)
    tok = tokens.reshape(rows, width)
    cot = out_cot.reshape(rows, width)
    shape = jax.ShapeDtypeStruct

    wo_oth = swapped(out_weight, "fsdp", 1)
    wt_oth = swapped(time_weight, "fsdp", 1)
    near, far = neighbours(tok)
    wq_oth = swapped(qkv_weight, "fsdp", 1)

    freq = 2 * time_weight.shape[0]
    feats = time_features(timesteps, freq).reshape(2, freq // 2)
    own = lax.dynamic_slice_in_dim(feats, half, 1, axis=0)
    oth = lax.dynamic_slice_in_dim(feats, 1 - half, 1, axis=0)
    feats = jnp.broadcast_to(jnp.stack([own, oth]), (2, 8, freq // 2))
    pxrd_rows = pxrd_mod.transpose(1, 0, 2)
    front = call(
        functools.partial(front_body, slots),
        "front",
        [shape((3, width), f32), shape(out_weight.shape, bf16)]
        + [shape((rows, lanes), bf16)] * slots,
        (ids, feats, time_weight, wt_oth, pxrd_rows, out_weight, wo_oth, cot),
        [pltpu.VMEM((slots, rows, lanes), bf16)]
        + [pltpu.VMEM(time_weight.shape, bf16)] * 2
        + [pltpu.VMEM(pxrd_rows.shape, f32)]
        + [pltpu.VMEM(out_weight.shape, bf16)]
        + [pltpu.VMEM((rows, width), bf16), pltpu.SemaphoreType.DMA((6,))],
        far_args=range(2, 8),
        flops=2 * rows * width * H * HD,
        scalars=True,
    )
    mod, wo_held = front[:2]
    grads_in = exchanged(front[2:])

    mixed = call(
        functools.partial(mix_body, slots, inner),
        "mix",
        [shape((rows, width), bf16), shape((rows, 2 * H * HD), f32)]
        + [shape((rows, 3 * lanes), bf16)] * slots,
        (ids, tok, near, far, conv_kernel, mod, qkv_weight, wq_oth),
        [
            pltpu.VMEM((2, rows, width // 2), bf16),
            pltpu.VMEM((slots, rows, 3 * lanes), bf16),
            pltpu.VMEM((rows, 128), f32),
        ],
        flops=2 * rows * width * 3 * H * HD,
        scalars=True,
    )
    resid, sections = mixed[:2]
    sends, grads_in = lax.optimization_barrier((mixed[2:], grads_in))
    qkv_in = exchanged(sends)
    count = slots * rows
    attended = call(
        functools.partial(attend_body, slots),
        "attend",
        [shape((rows, 3 * lanes), bf16)] * slots + [shape((rows, lanes), bf16)] * slots,
        (*qkv_in, *grads_in),
        [
            pltpu.VMEM((lanes // HD, count, count), f32),
            pltpu.VMEM((count, lanes // HD * count), bf16),
            pltpu.VMEM((count, lanes // HD * count), bf16),
        ],
        flops=12 * count * count * lanes,
    )
    backs = exchanged(attended[:slots])
    attns = exchanged(attended[slots:])
    dresid, terms = call(
        functools.partial(tail_body, slots, inner),
        "tail",
        [shape((rows, width), bf16), shape((27 * width // 128, 128), bf16)],
        (ids, *backs, sections, resid, cot, mod, qkv_weight, wq_oth, tok, near, far),
        [
            pltpu.VMEM((slots, 3, rows, lanes), bf16),
            pltpu.VMEM((rows, 3 * H * HD), bf16),
            pltpu.VMEM((2, rows, width // 2), f32),
            pltpu.VMEM((8 * 27 * width // 128, 128), f32),
            pltpu.VMEM((rows, width), bf16),
            pltpu.VMEM((rows, width), bf16),
            pltpu.SemaphoreType.DMA((2,)),
        ],
        flops=2 * rows * width * 3 * H * HD,
        scalars=True,
        far_args=(slots + 8, slots + 9),
    )
    dresid, attns = lax.optimization_barrier((dresid, attns))
    (out,) = call(
        functools.partial(out_body, slots),
        "out",
        [shape((rows, width), bf16)],
        (ids, *attns, resid, mod, out_weight, wo_held),
        [pltpu.VMEM((slots, rows, lanes), bf16)],
        flops=2 * rows * width * H * HD,
        scalars=True,
    )
    grad_near, grad_far = neighbours(dresid)
    other = swapped(terms, "dp", 1)
    other, out = lax.optimization_barrier((other, out))
    (terms,) = call(sum_body, "add_dp", [shape(terms.shape, bf16)], (terms, other))
    (token_grad,) = call(
        functools.partial(back_conv_body, inner),
        "back_conv",
        [shape((rows, width), bf16)],
        (ids, dresid, grad_near, grad_far, conv_kernel),
        scalars=True,
    )
    factor = 1.0 / math.sqrt(lax.axis_size("dp") * lax.axis_size("fsdp") * slots * rows)
    pieces = exchanged([terms] * slots)
    pieces[-1], token_grad = lax.optimization_barrier((pieces[-1], token_grad))
    (summed,) = call(
        functools.partial(seq_sum_body, slots), "add_seq", [shape(terms.shape, f32)], pieces
    )
    (kernel_grad,) = call(
        functools.partial(final_body, factor),
        "final",
        [shape((27, width), f32)],
        (summed, swapped(summed, "fsdp", 1)),
    )
    return out.reshape(tokens.shape), token_grad.reshape(tokens.shape), kernel_grad


def solution(mesh):
    count = mesh.shape["seq"]

    def pick(*args):
        tokens, time_weight = args[0], args[3]
        lanes = H * HD // count
        fits = (
            count == 4
            and tokens.shape[0] == 1
            and tokens.shape[1] == 1
            and tokens.shape[3] % 16 == 0
            and lanes % 128 == 0
            and mesh.shape["dp"] == 2
            and mesh.shape["fsdp"] == 2
        )
        return slab_shards(*args) if fits else shards(*args)

    placed = (
        P(("groups", "dp", "fsdp"), "seq", None, None, None),
        P(("groups", "dp", "fsdp")),
        P(("groups", "dp", "fsdp"), None, None),
        P("fsdp", None),
        P(),
        P("fsdp", None),
        P("fsdp", None),
        P(("groups", "dp", "fsdp"), "seq", None, None, None),
    )
    return jax.shard_map(
        pick,
        mesh=mesh,
        in_specs=placed,
        out_specs=(
            P(("groups", "dp", "fsdp"), "seq", None, None, None),
            P(("groups", "dp", "fsdp"), "seq", None, None, None),
            P("groups", None),
        ),
        check_vma=False,
    )
```

```python
import functools
import math

import jax
import jax.numpy as jnp
from jax import lax
from jax.experimental import pallas as pl
from jax.experimental.pallas import tpu as pltpu
from jax.sharding import PartitionSpec as P

H = 8
HD = 64


def padded_2(value, sides, width):
    for axis, dim in sides:
        count, length = (lax.axis_size(axis), value.shape[dim])
        up = [(i, (i + 1) % count) for i in range(count - 1)]
        down = [(j, i) for i, j in up]
        last = lax.slice_in_dim(value, length - width, length, axis=dim)
        leading = lax.slice_in_dim(value, 0, width, axis=dim)
        before = lax.ppermute(last, axis, up)
        after = lax.ppermute(leading, axis, down)
        value = jnp.concatenate([before, value, after], axis=dim)
    return value


def time_features(steps_int, freq_width):
    half_width = freq_width // 2
    freq_index = jnp.arange(half_width).astype(jnp.float32)
    frequency = jnp.exp(freq_index * (-math.log(10000.0) / half_width))
    angles = steps_int.astype(jnp.float32)[:, None] * frequency[None, :]
    return jnp.concatenate([jnp.cos(angles), jnp.sin(angles)], axis=1).astype(jnp.bfloat16)


def modulation(steps_int, pxrd_mod, time_weight):
    features = time_features(steps_int, time_weight.shape[0])
    projected = jnp.dot(features, time_weight, preferred_element_type=jnp.float32)
    return projected.reshape(steps_int.shape[0], 3, time_weight.shape[1] // 3) + pxrd_mod


def depthwise(padded_z, kernel_taps, plane_count):
    framed = jnp.pad(padded_z, ((0, 0), (1, 1), (1, 1), (0, 0)))
    side_y = framed.shape[1] - 2
    side_x = framed.shape[2] - 2
    result = jnp.zeros((plane_count, side_y, side_x, framed.shape[3]), jnp.float32)
    for tap_z in range(3):
        for tap_y in range(3):
            for tap_x in range(3):
                window = framed[
                    tap_z : tap_z + plane_count, tap_y : tap_y + side_y, tap_x : tap_x + side_x
                ]
                result = result + kernel_taps[9 * tap_z + 3 * tap_y + tap_x] * window.astype(
                    jnp.float32
                )
    return result


def kernel_terms(padded_z, upstream, plane_count):
    framed = jnp.pad(padded_z, ((0, 0), (1, 1), (1, 1), (0, 0)))
    side_y = framed.shape[1] - 2
    side_x = framed.shape[2] - 2
    upstream_f = upstream.astype(jnp.float32)
    collected = []
    for tap_z in range(3):
        for tap_y in range(3):
            for tap_x in range(3):
                window = framed[
                    tap_z : tap_z + plane_count, tap_y : tap_y + side_y, tap_x : tap_x + side_x
                ]
                collected.append(jnp.sum(window.astype(jnp.float32) * upstream_f, axis=(0, 1, 2)))
    return jnp.stack(collected)


def modulate(stream, shift_row, scale_row):
    centre = stream - jnp.mean(stream, axis=-1, keepdims=True)
    spread = jnp.mean(centre * centre, axis=-1, keepdims=True)
    return centre * lax.rsqrt(spread + 1e-06) * (1.0 + scale_row) + shift_row


def head_norms(projected):
    row_count = projected.shape[0]
    sections = projected.reshape(row_count, 3, H, HD)
    query_key = sections[:, :2]
    normed = query_key * lax.rsqrt(jnp.mean(query_key * query_key, axis=-1, keepdims=True) + 1e-06)
    return (
        normed[:, 0].reshape(row_count, H * HD),
        normed[:, 1].reshape(row_count, H * HD),
        sections[:, 2].reshape(row_count, H * HD),
    )


def attend_both(queries, grads, key_rows, value_rows):
    count = queries.shape[0]
    heads = queries.shape[1]
    block = min(512, count)
    steps = count // block
    scale_dot = 1.0 / math.sqrt(HD)

    def one_block(carry, pieces):
        query_blk, grad_blk = pieces
        scores = (
            jnp.einsum("qhd,khd->hqk", query_blk, key_rows, preferred_element_type=jnp.float32)
            * scale_dot
        )
        expo = jnp.exp(scores)
        totals = jnp.sum(expo, axis=-1, keepdims=True)
        weights = expo / totals
        probs = weights.astype(jnp.bfloat16)
        attn_blk = jnp.einsum(
            "hqk,khd->qhd", probs, value_rows, preferred_element_type=jnp.float32
        ).astype(jnp.bfloat16)
        delta = jnp.sum(grad_blk.astype(jnp.float32) * attn_blk.astype(jnp.float32), axis=-1).T
        dprob = jnp.einsum("qhd,khd->hqk", grad_blk, value_rows, preferred_element_type=jnp.float32)
        dscore = (weights * (dprob - delta[:, :, None]) * scale_dot).astype(jnp.bfloat16)
        dquery = jnp.einsum("hqk,khd->qhd", dscore, key_rows, preferred_element_type=jnp.float32)
        dkey = carry[0] + jnp.einsum(
            "hqk,qhd->khd", dscore, query_blk, preferred_element_type=jnp.float32
        )
        dvalue = carry[1] + jnp.einsum(
            "hqk,qhd->khd", probs, grad_blk, preferred_element_type=jnp.float32
        )
        return ((dkey, dvalue), (attn_blk, dquery))

    zeros_kv = jnp.zeros(key_rows.shape, jnp.float32)
    (dkey, dvalue), (attn_all, dquery) = lax.scan(
        one_block,
        (zeros_kv, zeros_kv),
        (queries.reshape(steps, block, heads, HD), grads.reshape(steps, block, heads, HD)),
    )
    return (attn_all.reshape(count, heads, HD), dquery.reshape(count, heads, HD), dkey, dvalue)


def shards(tokens, timesteps, pxrd_mod, time_weight, conv_kernel, qkv_weight, out_weight, out_cot):
    w_qkv, w_out, w_time = (
        lax.all_gather(qkv_weight, "fsdp", axis=0, tiled=True),
        lax.all_gather(out_weight, "fsdp", axis=0, tiled=True),
        lax.all_gather(time_weight, "fsdp", axis=0, tiled=True),
    )
    plane_count = tokens.shape[1]
    side_y = tokens.shape[2]
    side_x = tokens.shape[3]
    width_model = tokens.shape[4]
    row_count = plane_count * side_y * side_x
    inner_width = H * HD
    seq_count = lax.axis_size("seq")
    head_groups = min(H, seq_count)
    per_device = H // head_groups
    row_split = seq_count // head_groups
    part_rows = row_count // row_split
    group_width = per_device * HD
    padded = padded_2(tokens, (("seq", 1),), 1)[0]
    mixed = depthwise(padded, conv_kernel, plane_count)
    resid = (
        (tokens[0].astype(jnp.float32) + mixed).astype(jnp.bfloat16).reshape(row_count, width_model)
    )
    modul = modulation(timesteps, pxrd_mod, w_time)
    shift_row = modul[0, 0]
    scale_row = modul[0, 1]
    gate_row = modul[0, 2]
    resid_f = resid.astype(jnp.float32)
    normed = modulate(resid_f, shift_row, scale_row).astype(jnp.bfloat16)
    projected = jnp.dot(normed, w_qkv, preferred_element_type=jnp.float32)
    query_f, key_f, value_f = head_norms(projected)
    cotangent = out_cot[0].reshape(row_count, width_model).astype(jnp.float32)
    gated = (gate_row * cotangent).astype(jnp.bfloat16)
    grad_attn = lax.dot_general(
        gated, w_out, (((1,), (1,)), ((), ())), preferred_element_type=jnp.float32
    ).astype(jnp.bfloat16)

    def to_heads(token_rows):
        shaped = token_rows.reshape(row_split, part_rows, head_groups, group_width)
        return shaped.transpose(2, 0, 1, 3).reshape(seq_count, part_rows, group_width)

    def from_heads(head_rows):
        shaped = head_rows.reshape(head_groups, row_split, part_rows, group_width)
        return shaped.transpose(1, 2, 0, 3).reshape(row_count, inner_width)

    query_heads, grad_heads = (
        lax.all_to_all(
            to_heads(query_f.astype(jnp.bfloat16)), "seq", split_axis=0, concat_axis=0, tiled=True
        ),
        lax.all_to_all(to_heads(grad_attn), "seq", split_axis=0, concat_axis=0, tiled=True),
    )
    query_count = seq_count * part_rows
    query_heads = query_heads.reshape(query_count, per_device, HD)
    grad_heads = grad_heads.reshape(query_count, per_device, HD)
    stacked = jnp.stack(
        [
            key_f.astype(jnp.bfloat16).reshape(row_count, head_groups, group_width),
            value_f.astype(jnp.bfloat16).reshape(row_count, head_groups, group_width),
        ],
        axis=2,
    )
    by_group = stacked.transpose(1, 0, 2, 3).reshape(head_groups, row_count, 2 * group_width)
    copies = jnp.broadcast_to(
        by_group[:, None], (head_groups, row_split, row_count, 2 * group_width)
    )
    arrived = lax.all_to_all(
        copies.reshape(seq_count, row_count, 2 * group_width),
        "seq",
        split_axis=0,
        concat_axis=0,
        tiled=True,
    )
    key_value = arrived.reshape(seq_count * row_count, 2, per_device, HD)
    attn_heads, dquery, dkey, dvalue = attend_both(
        query_heads, grad_heads, key_value[:, 0], key_value[:, 1]
    )
    attn_tok = from_heads(
        lax.all_to_all(
            attn_heads.reshape(seq_count, part_rows, group_width),
            "seq",
            split_axis=0,
            concat_axis=0,
            tiled=True,
        )
    )
    projected_out = jnp.dot(attn_tok, w_out, preferred_element_type=jnp.float32)
    out_rows = (resid_f + gate_row * projected_out).astype(jnp.bfloat16)
    dquery_tok = from_heads(
        lax.all_to_all(
            dquery.reshape(seq_count, part_rows, group_width),
            "seq",
            split_axis=0,
            concat_axis=0,
            tiled=True,
        )
    )
    grads_kv = jnp.stack([dkey, dvalue], axis=1)
    returned = lax.all_to_all(
        grads_kv.reshape(seq_count, row_count, 2 * group_width).astype(jnp.bfloat16),
        "seq",
        split_axis=0,
        concat_axis=0,
        tiled=True,
    ).astype(jnp.float32)
    summed = jnp.sum(returned.reshape(head_groups, row_split, row_count, 2 * group_width), axis=1)
    grads_tok = (
        summed.reshape(head_groups, row_count, 2, group_width)
        .transpose(2, 1, 0, 3)
        .reshape(2, row_count, inner_width)
    )
    _, pullback = jax.vjp(head_norms, projected)
    (grad_projected,) = pullback((dquery_tok, grads_tok[0], grads_tok[1]))
    grad_proj_b = grad_projected.astype(jnp.bfloat16)
    grad_normed = lax.dot_general(
        grad_proj_b, w_qkv, (((1,), (1,)), ((), ())), preferred_element_type=jnp.float32
    )
    _, pull_norm = jax.vjp(lambda stream: modulate(stream, shift_row, scale_row), resid_f)
    (grad_stream,) = pull_norm(grad_normed)
    grad_resid = (
        (cotangent + grad_stream)
        .astype(jnp.bfloat16)
        .reshape(1, plane_count, side_y, side_x, width_model)
    )
    grad_padded = padded_2(grad_resid, (("seq", 1),), 1)[0]
    grad_tokens = (
        grad_resid[0].astype(jnp.float32) + depthwise(grad_padded, conv_kernel[::-1], plane_count)
    ).astype(jnp.bfloat16)
    local_terms = kernel_terms(padded, grad_resid[0], plane_count)
    norm_factor = 1.0 / math.sqrt(
        lax.axis_size("dp") * lax.axis_size("fsdp") * seq_count * row_count
    )
    grad_kernel = lax.psum(local_terms, ("seq", "dp", "fsdp")) * norm_factor
    return (out_rows.reshape(tokens.shape), grad_tokens.reshape(tokens.shape), grad_kernel)


def as_f32(value):
    return value.astype(jnp.float32)


def row_shift(value, step, inner):
    rows = value.shape[0]
    moved = pltpu.roll(value, step % rows, axis=0)
    place = lax.rem(lax.broadcasted_iota(jnp.int32, value.shape, 0), inner)
    return jnp.where(place == (0 if step == 1 else inner - 1), 0.0, moved)


def slab_shift(value, step, inner):
    if step == 0:
        return value
    empty = jnp.zeros((inner, value.shape[1]), value.dtype)
    if step == 1:
        return jnp.concatenate([empty, value[:-inner]], axis=0)
    return jnp.concatenate([value[inner:], empty], axis=0)


def conv_lanes(planes, taps, flipped, inner):
    by_x = []
    for tap_x in range(3):
        total = None
        for tap_y in range(3):
            part = None
            for tap_z, plane in planes.items():
                index = 9 * tap_z + 3 * tap_y + tap_x
                index = 26 - index if flipped else index
                term = taps[index : index + 1] * plane
                part = term if part is None else part + term
            part = slab_shift(part, 1 - tap_y, inner)
            total = part if total is None else total + part
        by_x.append(total)
    return by_x[1] + row_shift(by_x[0], 1, inner) + row_shift(by_x[2], -1, inner)


def sided(odd, near, far, body):
    pl.when(odd)(lambda: body(near, far))
    pl.when(jnp.logical_not(odd))(lambda: body(far, near))


def head_mean(value):
    width = value.shape[1]
    left = lax.broadcasted_iota(jnp.int32, (width, width), 0) // HD
    right = lax.broadcasted_iota(jnp.int32, (width, width), 1) // HD
    same = jnp.where(left == right, 1.0, 0.0).astype(jnp.bfloat16)
    high = value.astype(jnp.bfloat16)
    low = (value - as_f32(high)).astype(jnp.bfloat16)
    total = jnp.dot(high, same, preferred_element_type=jnp.float32)
    total = total + jnp.dot(low, same, preferred_element_type=jnp.float32)
    return total * (1.0 / HD)


def nt_dot(left, right):
    return lax.dot_general(
        left, right, (((1,), (1,)), ((), ())), preferred_element_type=jnp.float32
    )


def tn_dot(left, right):
    return lax.dot_general(
        left, right, (((0,), (0,)), ((), ())), preferred_element_type=jnp.float32
    )


def nn_dot(left, right):
    return jnp.dot(left, right, preferred_element_type=jnp.float32)


def front_body(slots, ids, feats, *rest):
    fetched = rest[:6]
    mod, wo_oth, sends = rest[6], rest[7], rest[8 : 8 + slots]
    by_group, wt_own, wt_oth, pxrd, wo_own, cot, arrive = rest[8 + slots :]
    held = (wt_own, wt_oth, pxrd, wo_own, wo_oth, cot)
    me, half = ids[0], ids[1]
    width = cot.shape[1]
    copies = [
        pltpu.make_async_copy(source, place, arrive.at[i])
        for i, (source, place) in enumerate(zip(fetched, held))
    ]
    for copy in copies:
        copy.start()
    for copy in copies[:3]:
        copy.wait()
    projected = nn_dot(feats[0], wt_own[...]) + nn_dot(feats[1], wt_oth[...])
    for row in range(3):
        cols = slice(row * width, (row + 1) * width)
        mod[row : row + 1, :] = projected[0:1, cols] + pxrd[row]
    for copy in copies[3:]:
        copy.wait()
    gated = (mod[2:3, :] * as_f32(cot[...])).astype(jnp.bfloat16)
    lanes = sends[0].shape[1]
    per_half = wo_own.shape[0] // lanes
    for weight, part in ((wo_own, half), (wo_oth, 1 - half)):
        grads = nt_dot(gated, weight[...]).astype(jnp.bfloat16)
        for j in range(per_half):
            by_group[part * per_half + j] = grads[:, j * lanes : (j + 1) * lanes]
    for k in range(slots):
        sends[k][...] = by_group[lax.bitwise_xor(me, gap_of(half, k))]


def own_conv_body(inner, tok_far, taps_far, out, tok, taps, arrive):
    @pl.when(lax.axis_index("fsdp") == 0)
    def work():
        copies = [
            pltpu.make_async_copy(tok_far, tok, arrive.at[0]),
            pltpu.make_async_copy(taps_far, taps, arrive.at[1]),
        ]
        for copy in copies:
            copy.start()
        for copy in copies:
            copy.wait()
        for start in range(0, tok.shape[1], 128):
            cols = slice(start, start + 128)
            plane = as_f32(tok[:, cols])
            out[:, cols] = plane + conv_lanes({1: plane}, taps[:, cols], False, inner)


def mix_body(slots, inner, ids, centre, tok, near, far, taps, mod, w_own, w_oth, *rest):
    resid, sections = rest[0], rest[1]
    sends = rest[2 : 2 + slots]
    normed, by_group, sums_ref = rest[2 + slots :]
    me, half = ids[0], ids[1]
    rows, width = tok.shape
    step = 128

    def all_planes(has_centre, before, after):
        sums = jnp.zeros((rows, step), jnp.float32)
        for start in range(0, width, step):
            cols = slice(start, start + step)
            planes = {0: as_f32(before[:, cols]), 2: as_f32(after[:, cols])}
            if has_centre:
                total = centre[:, cols]
            else:
                planes[1] = as_f32(tok[:, cols])
                total = planes[1]
            rounded = total + conv_lanes(planes, taps[:, cols], False, inner)
            rounded = rounded.astype(jnp.bfloat16)
            resid[:, cols] = rounded
            sums = sums + as_f32(rounded)
        sums_ref[...] = sums

    for has_centre in (True, False):

        @pl.when((half == 0) == has_centre)
        def work():
            sided(lax.rem(me, 2) == 1, near, far, functools.partial(all_planes, has_centre))

    sums = sums_ref[...]
    mean = jnp.sum(sums, axis=1, keepdims=True) * (1.0 / width)
    squares = jnp.zeros((rows, step), jnp.float32)
    for start in range(0, width, step):
        centre = as_f32(resid[:, start : start + step]) - mean
        squares = squares + centre * centre
    spread = jnp.sum(squares, axis=1, keepdims=True) * (1.0 / width)
    inverse = lax.rsqrt(spread + 1e-06)
    per_half = width // 2
    for start in range(0, width, step):
        cols = slice(start, start + step)
        centre = as_f32(resid[:, cols]) - mean
        value = centre * inverse * (1.0 + mod[1:2, cols]) + mod[0:1, cols]
        inside = start % per_half
        normed[start // per_half, :, inside : inside + step] = value.astype(jnp.bfloat16)
    projected = nn_dot(normed[half], w_own[...]) + nn_dot(normed[1 - half], w_oth[...])
    lanes = sends[0].shape[1] // 3
    inner_width = H * HD
    sections[...] = projected[:, : 2 * inner_width]
    for group in range(slots):
        for part in range(3):
            block = projected[:, part * inner_width + group * lanes :][:, :lanes]
            if part < 2:
                block = block * lax.rsqrt(head_mean(block * block) + 1e-06)
            by_group[group, :, part * lanes : (part + 1) * lanes] = block.astype(jnp.bfloat16)
    for k in range(slots):
        sends[k][...] = by_group[lax.bitwise_xor(me, gap_of(half, k))]


def attend_body(slots, *refs):
    qkv_in, grads_in = refs[:slots], refs[slots : 2 * slots]
    backs, attns = refs[2 * slots : 3 * slots], refs[3 * slots : 4 * slots]
    weights, probs, dscore = refs[4 * slots :]
    rows, lanes = grads_in[0].shape
    heads = lanes // HD
    count = slots * rows
    scale = 1.0 / math.sqrt(HD)
    step = 64
    zero = jnp.zeros((count, lanes), jnp.bfloat16)
    owner = lax.broadcasted_iota(jnp.int32, (count, lanes), 1) // HD
    masks = [owner == head for head in range(heads)]
    query = jnp.concatenate([ref[:, :lanes] for ref in qkv_in], axis=0)
    key = jnp.concatenate([ref[:, lanes : 2 * lanes] for ref in qkv_in], axis=0)
    value = jnp.concatenate([ref[:, 2 * lanes :] for ref in qkv_in], axis=0)
    grad = jnp.concatenate([ref[...] for ref in grads_in], axis=0)
    scaled = query * jnp.asarray(scale, jnp.bfloat16)
    for head in range(heads):
        weights[head] = nt_dot(jnp.where(masks[head], scaled, zero), key)
    for head in range(heads):
        for start in range(0, count, step):
            span = slice(start, start + step)
            expo = jnp.exp(weights[head, span, :])
            expo = expo * (1.0 / jnp.sum(expo, axis=1, keepdims=True))
            weights[head, span, :] = expo
            probs[span, head * count : (head + 1) * count] = expo.astype(jnp.bfloat16)
    values = jnp.concatenate([jnp.where(mask, value, zero) for mask in masks], axis=0)
    keys = jnp.concatenate([jnp.where(mask, key, zero) for mask in masks], axis=0)
    attn = nn_dot(probs[...], values).astype(jnp.bfloat16)
    for k in range(slots):
        attns[k][...] = attn[k * rows : (k + 1) * rows]
    product = as_f32(attn) * as_f32(grad)
    for head in range(heads):
        delta = jnp.sum(jnp.where(masks[head], product, 0.0), axis=1, keepdims=True)
        dprob = nt_dot(jnp.where(masks[head], grad, zero), value)
        for start in range(0, count, step):
            span = slice(start, start + step)
            part = weights[head, span, :] * (dprob[span] - delta[span])
            dscore[span, head * count : (head + 1) * count] = part.astype(jnp.bfloat16)
    dquery = nn_dot(dscore[...], keys) * scale
    dkeys, dvalues = None, None
    for head in range(heads):
        span = slice(head * count, (head + 1) * count)
        dkey = jnp.where(masks[head], tn_dot(dscore[:, span], scaled), 0.0)
        dvalue = jnp.where(masks[head], tn_dot(probs[:, span], grad), 0.0)
        dkeys = dkey if dkeys is None else dkeys + dkey
        dvalues = dvalue if dvalues is None else dvalues + dvalue
    for k in range(slots):
        span = slice(k * rows, (k + 1) * rows)
        for part, found in enumerate((dquery, dkeys, dvalues)):
            backs[k][:, part * lanes : (part + 1) * lanes] = found[span].astype(jnp.bfloat16)


def tail_body(slots, inner, ids, *refs):
    backs = refs[:slots]
    sections, resid, cot, mod, w_own, w_oth, tok, near_far, far_far = refs[slots : slots + 9]
    dresid, terms, by_group, dproj, dnormed, partial, near, far, arrive = refs[slots + 9 :]
    me, half = ids[0], ids[1]
    copies = [
        pltpu.make_async_copy(near_far, near, arrive.at[0]),
        pltpu.make_async_copy(far_far, far, arrive.at[1]),
    ]
    for copy in copies:
        copy.start()
    rows, width = resid.shape
    lanes = by_group.shape[3]
    inner_width = H * HD
    for k in range(slots):
        group = lax.bitwise_xor(me, gap_of(half, k))
        for part in range(3):
            by_group[group, part] = backs[k][:, part * lanes : (part + 1) * lanes]
    for group in range(slots):
        for part in range(3):
            start = part * inner_width + group * lanes
            grad = by_group[group, part]
            if part < 2:
                grad = as_f32(grad)
                block = sections[:, start : start + lanes]
                inverse = lax.rsqrt(head_mean(block * block) + 1e-06)
                unit = block * inverse
                grad = (inverse * (grad - unit * head_mean(grad * unit))).astype(jnp.bfloat16)
            dproj[:, start : start + lanes] = grad
    dnormed[half] = nt_dot(dproj[...], w_own[...])
    dnormed[1 - half] = nt_dot(dproj[...], w_oth[...])
    step = 128
    per_half = width // 2
    total = jnp.zeros((rows, step), jnp.float32)
    for start in range(0, width, step):
        total = total + as_f32(resid[:, start : start + step])
    mean = jnp.sum(total, axis=1, keepdims=True) * (1.0 / width)
    total = jnp.zeros((rows, step), jnp.float32)
    for start in range(0, width, step):
        centre = as_f32(resid[:, start : start + step]) - mean
        total = total + centre * centre
    inverse = lax.rsqrt(jnp.sum(total, axis=1, keepdims=True) * (1.0 / width) + 1e-06)
    plain = jnp.zeros((rows, step), jnp.float32)
    crossed = jnp.zeros((rows, step), jnp.float32)
    for start in range(0, width, step):
        cols = slice(start, start + step)
        inside = start % per_half
        grad = dnormed[start // per_half, :, inside : inside + step] * (1.0 + mod[1:2, cols])
        unit = (as_f32(resid[:, cols]) - mean) * inverse
        plain = plain + grad
        crossed = crossed + grad * unit
    plain = jnp.sum(plain, axis=1, keepdims=True) * (1.0 / width)
    crossed = jnp.sum(crossed, axis=1, keepdims=True) * (1.0 / width)
    for start in range(0, width, step):
        cols = slice(start, start + step)
        inside = start % per_half
        grad = dnormed[start // per_half, :, inside : inside + step] * (1.0 + mod[1:2, cols])
        unit = (as_f32(resid[:, cols]) - mean) * inverse
        stream = as_f32(cot[:, cols]) + inverse * (grad - plain - unit * crossed)
        dresid[:, cols] = stream.astype(jnp.bfloat16)
    for copy in copies:
        copy.wait()
    outer = functools.partial(tap_terms, inner, dresid, tok, partial)
    sided(lax.rem(me, 2) == 1, near, far, outer)
    count = terms.shape[0]
    total = partial[pl.ds(0, count, stride=8), :]
    for i in range(1, 8):
        total = total + partial[pl.ds(i, count, stride=8), :]
    terms[...] = total.astype(terms.dtype)


def tap_terms(inner, dresid, tok, partial, before, after):
    rows, width = dresid.shape
    step = 128
    for start in range(0, width, step):
        cols = slice(start, start + step)
        grad = as_f32(dresid[:, cols])
        moved = [row_shift(grad, -1, inner), grad, row_shift(grad, 1, inner)]
        base = 27 * (start // step)
        for tap_z, ref in enumerate((before, tok, after)):
            plane = as_f32(ref[:, cols])
            for tap_y in range(3):
                low, high = max(0, 1 - tap_y), max(0, tap_y - 1)
                for tap_x in range(3):
                    prod = (
                        plane[high * inner : rows - low * inner]
                        * moved[tap_x][low * inner : rows - high * inner]
                    )
                    row = 8 * (base + 9 * tap_z + 3 * tap_y + tap_x)
                    partial[row : row + 8, :] = jnp.sum(prod.reshape(-1, 8, step), axis=0)


def out_body(slots, ids, *refs):
    attns = refs[:slots]
    resid, mod, wo_own, wo_oth, out, by_group = refs[slots:]
    me, half = ids[0], ids[1]
    lanes = attns[0].shape[1]
    per_half = wo_own.shape[0] // lanes
    for k in range(slots):
        by_group[lax.bitwise_xor(me, gap_of(half, k))] = attns[k][...]
    total = None
    for weight, part in ((wo_own, half), (wo_oth, 1 - half)):
        for j in range(per_half):
            term = nn_dot(by_group[part * per_half + j], weight[j * lanes : (j + 1) * lanes, :])
            total = term if total is None else total + term
    out[...] = (as_f32(resid[...]) + mod[2:3, :] * total).astype(jnp.bfloat16)


def back_conv_body(inner, ids, grad, near, far, taps, out):
    width = grad.shape[1]
    step = 128

    def all_planes(before, after):
        for start in range(0, width, step):
            cols = slice(start, start + step)
            planes = {i: as_f32(ref[:, cols]) for i, ref in enumerate((before, grad, after))}
            mixed = conv_lanes(planes, taps[:, cols], True, inner)
            out[:, cols] = (planes[1] + mixed).astype(jnp.bfloat16)

    sided(lax.rem(ids[0], 2) == 1, near, far, all_planes)


def tree_sum(values):
    while len(values) > 1:
        values = [values[i] + values[i + 1] for i in range(0, len(values), 2)]
    return values[0]


def sum_body(*refs):
    out = refs[-1]
    out[...] = tree_sum([as_f32(ref[...]) for ref in refs[:-1]]).astype(out.dtype)


def final_body(factor, left, right, out):
    total = (left[...] + right[...]) * factor
    lanes = total.shape[1]
    for block in range(out.shape[1] // lanes):
        out[:, block * lanes : (block + 1) * lanes] = total[27 * block : 27 * (block + 1)]


def call(body, name, outs, args, scratch=(), flops=0, scalars=False, far_args=(), vmem=16):
    whole = pl.BlockSpec(memory_space=pltpu.VMEM)
    specs = [whole] * len(args)
    if scalars:
        specs[0] = pl.BlockSpec(memory_space=pltpu.SMEM)
    for i in far_args:
        specs[i] = pl.BlockSpec(memory_space=pltpu.HBM)
    sizes = [math.prod(a.shape) * a.dtype.itemsize for a in list(args) + list(outs)]
    args = [
        pltpu.with_memory_space_constraint(a, pltpu.HBM) if i in far_args else a
        for i, a in enumerate(args)
    ]
    return pl.pallas_call(
        body,
        out_shape=tuple(outs),
        in_specs=specs,
        out_specs=(whole,) * len(outs),
        scratch_shapes=list(scratch),
        compiler_params=pltpu.CompilerParams(vmem_limit_bytes=vmem * 2**20),
        cost_estimate=pl.CostEstimate(flops=flops, bytes_accessed=sum(sizes), transcendentals=0),
        name=name,
    )(*args)


def swapped(value, axis, distance):
    count = lax.axis_size(axis)
    return lax.ppermute(value, axis, [(i, i ^ distance) for i in range(count)])


ORDERS = ((0, 1, 3, 2), (0, 2, 3, 1))


def gap_of(half, k):
    return jnp.where(half == 0, ORDERS[0][k], ORDERS[1][k])


def exchanged(pieces):
    seqs, cores = lax.axis_size("seq"), lax.axis_size("fsdp")
    received = [pieces[0]]
    for k in range(1, len(pieces)):
        pairs = [
            (cores * z + core, cores * (z ^ ORDERS[core][k]) + core)
            for z in range(seqs)
            for core in range(cores)
        ]
        received.append(lax.ppermute(pieces[k], ("seq", "fsdp"), pairs))
    return received


def neighbours(value):
    count = lax.axis_size("seq")
    near = swapped(value, "seq", 1)
    middle = [(i, i + 1) for i in range(1, count - 1, 2)]
    return near, lax.ppermute(value, "seq", middle + [(j, i) for i, j in middle])


def slab_shards(
    tokens, timesteps, pxrd_mod, time_weight, conv_kernel, qkv_weight, out_weight, out_cot
):
    bf16, f32 = jnp.bfloat16, jnp.float32
    side_y, inner, width = tokens.shape[2:]
    rows = side_y * inner
    slots = lax.axis_size("seq")
    lanes = H * HD // slots
    me = lax.axis_index("seq")
    half = lax.axis_index("fsdp")
    ids = jnp.stack([me, half]).astype(jnp.int32)
    tok = tokens.reshape(rows, width)
    cot = out_cot.reshape(rows, width)
    shape = jax.ShapeDtypeStruct

    wo_oth = swapped(out_weight, "fsdp", 1)
    wt_oth = swapped(time_weight, "fsdp", 1)
    (centre,) = call(
        functools.partial(own_conv_body, inner),
        "own_conv",
        [shape((rows, width), f32)],
        (tok, conv_kernel),
        [
            pltpu.VMEM((rows, width), bf16),
            pltpu.VMEM(conv_kernel.shape, f32),
            pltpu.SemaphoreType.DMA((2,)),
        ],
        far_args=(0, 1),
    )
    tok_sent, centre = lax.optimization_barrier((tok, centre))
    near, far = neighbours(pltpu.with_memory_space_constraint(tok_sent, pltpu.HBM))
    wq_oth = swapped(qkv_weight, "fsdp", 1)

    freq = 2 * time_weight.shape[0]
    feats = time_features(timesteps, freq).reshape(2, freq // 2)
    own = lax.dynamic_slice_in_dim(feats, half, 1, axis=0)
    oth = lax.dynamic_slice_in_dim(feats, 1 - half, 1, axis=0)
    feats = jnp.broadcast_to(jnp.stack([own, oth]), (2, 8, freq // 2))
    pxrd_rows = pxrd_mod.transpose(1, 0, 2)
    front = call(
        functools.partial(front_body, slots),
        "front",
        [shape((3, width), f32), shape(out_weight.shape, bf16)]
        + [shape((rows, lanes), bf16)] * slots,
        (ids, feats, time_weight, wt_oth, pxrd_rows, out_weight, wo_oth, cot),
        [pltpu.VMEM((slots, rows, lanes), bf16)]
        + [pltpu.VMEM(time_weight.shape, bf16)] * 2
        + [pltpu.VMEM(pxrd_rows.shape, f32)]
        + [pltpu.VMEM(out_weight.shape, bf16)]
        + [pltpu.VMEM((rows, width), bf16), pltpu.SemaphoreType.DMA((6,))],
        far_args=range(2, 8),
        flops=2 * rows * width * H * HD,
        scalars=True,
    )
    mod, wo_held = front[:2]
    grads_in = exchanged(front[2:])

    mixed = call(
        functools.partial(mix_body, slots, inner),
        "mix",
        [shape((rows, width), bf16), shape((rows, 2 * H * HD), f32)]
        + [shape((rows, 3 * lanes), bf16)] * slots,
        (ids, centre, tok, near, far, conv_kernel, mod, qkv_weight, wq_oth),
        [
            pltpu.VMEM((2, rows, width // 2), bf16),
            pltpu.VMEM((slots, rows, 3 * lanes), bf16),
            pltpu.VMEM((rows, 128), f32),
        ],
        flops=2 * rows * width * 3 * H * HD,
        scalars=True,
    )
    resid, sections = mixed[:2]
    sends, grads_in = lax.optimization_barrier((mixed[2:], grads_in))
    qkv_in = exchanged(sends)
    count = slots * rows
    attended = call(
        functools.partial(attend_body, slots),
        "attend",
        [shape((rows, 3 * lanes), bf16)] * slots + [shape((rows, lanes), bf16)] * slots,
        (*qkv_in, *grads_in),
        [
            pltpu.VMEM((lanes // HD, count, count), f32),
            pltpu.VMEM((count, lanes // HD * count), bf16),
            pltpu.VMEM((count, lanes // HD * count), bf16),
        ],
        flops=12 * count * count * lanes,
    )
    backs = exchanged(attended[:slots])
    attns = exchanged(attended[slots:])
    dresid, terms = call(
        functools.partial(tail_body, slots, inner),
        "tail",
        [shape((rows, width), bf16), shape((27 * width // 128, 128), bf16)],
        (ids, *backs, sections, resid, cot, mod, qkv_weight, wq_oth, tok, near, far),
        [
            pltpu.VMEM((slots, 3, rows, lanes), bf16),
            pltpu.VMEM((rows, 3 * H * HD), bf16),
            pltpu.VMEM((2, rows, width // 2), f32),
            pltpu.VMEM((8 * 27 * width // 128, 128), f32),
            pltpu.VMEM((rows, width), bf16),
            pltpu.VMEM((rows, width), bf16),
            pltpu.SemaphoreType.DMA((2,)),
        ],
        flops=2 * rows * width * 3 * H * HD,
        scalars=True,
        far_args=(slots + 8, slots + 9),
    )
    dresid, attns = lax.optimization_barrier((dresid, attns))
    (out,) = call(
        functools.partial(out_body, slots),
        "out",
        [shape((rows, width), bf16)],
        (ids, *attns, resid, mod, out_weight, wo_held),
        [pltpu.VMEM((slots, rows, lanes), bf16)],
        flops=2 * rows * width * H * HD,
        scalars=True,
    )
    grad_near, grad_far = neighbours(dresid)
    other = swapped(terms, "dp", 1)
    other, out = lax.optimization_barrier((other, out))
    (terms,) = call(sum_body, "add_dp", [shape(terms.shape, bf16)], (terms, other))
    (token_grad,) = call(
        functools.partial(back_conv_body, inner),
        "back_conv",
        [shape((rows, width), bf16)],
        (ids, dresid, grad_near, grad_far, conv_kernel),
        scalars=True,
    )
    factor = 1.0 / math.sqrt(lax.axis_size("dp") * lax.axis_size("fsdp") * slots * rows)
    pieces = exchanged([terms] * slots)
    pieces[-1], token_grad = lax.optimization_barrier((pieces[-1], token_grad))
    (summed,) = call(sum_body, "add_seq", [shape(terms.shape, f32)], pieces)
    (kernel_grad,) = call(
        functools.partial(final_body, factor),
        "final",
        [shape((27, width), f32)],
        (summed, swapped(summed, "fsdp", 1)),
    )
    return out.reshape(tokens.shape), token_grad.reshape(tokens.shape), kernel_grad


def solution(mesh):
    count = mesh.shape["seq"]

    def pick(*args):
        tokens, time_weight = args[0], args[3]
        lanes = H * HD // count
        fits = (
            count == 4
            and tokens.shape[0] == 1
            and tokens.shape[1] == 1
            and tokens.shape[3] % 16 == 0
            and lanes % 128 == 0
            and mesh.shape["dp"] == 2
            and mesh.shape["fsdp"] == 2
        )
        return slab_shards(*args) if fits else shards(*args)

    placed = (
        P(("groups", "dp", "fsdp"), "seq", None, None, None),
        P(("groups", "dp", "fsdp")),
        P(("groups", "dp", "fsdp"), None, None),
        P("fsdp", None),
        P(),
        P("fsdp", None),
        P("fsdp", None),
        P(("groups", "dp", "fsdp"), "seq", None, None, None),
    )
    return jax.shard_map(
        pick,
        mesh=mesh,
        in_specs=placed,
        out_specs=(
            P(("groups", "dp", "fsdp"), "seq", None, None, None),
            P(("groups", "dp", "fsdp"), "seq", None, None, None),
            P("groups", None),
        ),
        check_vma=False,
    )
```

```python
import functools
import math

import jax
import jax.numpy as jnp
from jax import lax
from jax.experimental import pallas as pl
from jax.experimental.pallas import tpu as pltpu
from jax.sharding import PartitionSpec as P

H = 8
HD = 64


def padded_2(value, sides, width):
    for axis, dim in sides:
        count, length = (lax.axis_size(axis), value.shape[dim])
        up = [(i, (i + 1) % count) for i in range(count - 1)]
        down = [(j, i) for i, j in up]
        last = lax.slice_in_dim(value, length - width, length, axis=dim)
        leading = lax.slice_in_dim(value, 0, width, axis=dim)
        before = lax.ppermute(last, axis, up)
        after = lax.ppermute(leading, axis, down)
        value = jnp.concatenate([before, value, after], axis=dim)
    return value


def time_features(steps_int, freq_width):
    half_width = freq_width // 2
    freq_index = jnp.arange(half_width).astype(jnp.float32)
    frequency = jnp.exp(freq_index * (-math.log(10000.0) / half_width))
    angles = steps_int.astype(jnp.float32)[:, None] * frequency[None, :]
    return jnp.concatenate([jnp.cos(angles), jnp.sin(angles)], axis=1).astype(jnp.bfloat16)


def modulation(steps_int, pxrd_mod, time_weight):
    features = time_features(steps_int, time_weight.shape[0])
    projected = jnp.dot(features, time_weight, preferred_element_type=jnp.float32)
    return projected.reshape(steps_int.shape[0], 3, time_weight.shape[1] // 3) + pxrd_mod


def depthwise(padded_z, kernel_taps, plane_count):
    framed = jnp.pad(padded_z, ((0, 0), (1, 1), (1, 1), (0, 0)))
    side_y = framed.shape[1] - 2
    side_x = framed.shape[2] - 2
    result = jnp.zeros((plane_count, side_y, side_x, framed.shape[3]), jnp.float32)
    for tap_z in range(3):
        for tap_y in range(3):
            for tap_x in range(3):
                window = framed[
                    tap_z : tap_z + plane_count, tap_y : tap_y + side_y, tap_x : tap_x + side_x
                ]
                result = result + kernel_taps[9 * tap_z + 3 * tap_y + tap_x] * window.astype(
                    jnp.float32
                )
    return result


def kernel_terms(padded_z, upstream, plane_count):
    framed = jnp.pad(padded_z, ((0, 0), (1, 1), (1, 1), (0, 0)))
    side_y = framed.shape[1] - 2
    side_x = framed.shape[2] - 2
    upstream_f = upstream.astype(jnp.float32)
    collected = []
    for tap_z in range(3):
        for tap_y in range(3):
            for tap_x in range(3):
                window = framed[
                    tap_z : tap_z + plane_count, tap_y : tap_y + side_y, tap_x : tap_x + side_x
                ]
                collected.append(jnp.sum(window.astype(jnp.float32) * upstream_f, axis=(0, 1, 2)))
    return jnp.stack(collected)


def modulate(stream, shift_row, scale_row):
    centre = stream - jnp.mean(stream, axis=-1, keepdims=True)
    spread = jnp.mean(centre * centre, axis=-1, keepdims=True)
    return centre * lax.rsqrt(spread + 1e-06) * (1.0 + scale_row) + shift_row


def head_norms(projected):
    row_count = projected.shape[0]
    sections = projected.reshape(row_count, 3, H, HD)
    query_key = sections[:, :2]
    normed = query_key * lax.rsqrt(jnp.mean(query_key * query_key, axis=-1, keepdims=True) + 1e-06)
    return (
        normed[:, 0].reshape(row_count, H * HD),
        normed[:, 1].reshape(row_count, H * HD),
        sections[:, 2].reshape(row_count, H * HD),
    )


def attend_both(queries, grads, key_rows, value_rows):
    count = queries.shape[0]
    heads = queries.shape[1]
    block = min(512, count)
    steps = count // block
    scale_dot = 1.0 / math.sqrt(HD)

    def one_block(carry, pieces):
        query_blk, grad_blk = pieces
        scores = (
            jnp.einsum("qhd,khd->hqk", query_blk, key_rows, preferred_element_type=jnp.float32)
            * scale_dot
        )
        expo = jnp.exp(scores)
        totals = jnp.sum(expo, axis=-1, keepdims=True)
        weights = expo / totals
        probs = weights.astype(jnp.bfloat16)
        attn_blk = jnp.einsum(
            "hqk,khd->qhd", probs, value_rows, preferred_element_type=jnp.float32
        ).astype(jnp.bfloat16)
        delta = jnp.sum(grad_blk.astype(jnp.float32) * attn_blk.astype(jnp.float32), axis=-1).T
        dprob = jnp.einsum("qhd,khd->hqk", grad_blk, value_rows, preferred_element_type=jnp.float32)
        dscore = (weights * (dprob - delta[:, :, None]) * scale_dot).astype(jnp.bfloat16)
        dquery = jnp.einsum("hqk,khd->qhd", dscore, key_rows, preferred_element_type=jnp.float32)
        dkey = carry[0] + jnp.einsum(
            "hqk,qhd->khd", dscore, query_blk, preferred_element_type=jnp.float32
        )
        dvalue = carry[1] + jnp.einsum(
            "hqk,qhd->khd", probs, grad_blk, preferred_element_type=jnp.float32
        )
        return ((dkey, dvalue), (attn_blk, dquery))

    zeros_kv = jnp.zeros(key_rows.shape, jnp.float32)
    (dkey, dvalue), (attn_all, dquery) = lax.scan(
        one_block,
        (zeros_kv, zeros_kv),
        (queries.reshape(steps, block, heads, HD), grads.reshape(steps, block, heads, HD)),
    )
    return (attn_all.reshape(count, heads, HD), dquery.reshape(count, heads, HD), dkey, dvalue)


def shards(tokens, timesteps, pxrd_mod, time_weight, conv_kernel, qkv_weight, out_weight, out_cot):
    w_qkv, w_out, w_time = (
        lax.all_gather(qkv_weight, "fsdp", axis=0, tiled=True),
        lax.all_gather(out_weight, "fsdp", axis=0, tiled=True),
        lax.all_gather(time_weight, "fsdp", axis=0, tiled=True),
    )
    plane_count = tokens.shape[1]
    side_y = tokens.shape[2]
    side_x = tokens.shape[3]
    width_model = tokens.shape[4]
    row_count = plane_count * side_y * side_x
    inner_width = H * HD
    seq_count = lax.axis_size("seq")
    head_groups = min(H, seq_count)
    per_device = H // head_groups
    row_split = seq_count // head_groups
    part_rows = row_count // row_split
    group_width = per_device * HD
    padded = padded_2(tokens, (("seq", 1),), 1)[0]
    mixed = depthwise(padded, conv_kernel, plane_count)
    resid = (
        (tokens[0].astype(jnp.float32) + mixed).astype(jnp.bfloat16).reshape(row_count, width_model)
    )
    modul = modulation(timesteps, pxrd_mod, w_time)
    shift_row = modul[0, 0]
    scale_row = modul[0, 1]
    gate_row = modul[0, 2]
    resid_f = resid.astype(jnp.float32)
    normed = modulate(resid_f, shift_row, scale_row).astype(jnp.bfloat16)
    projected = jnp.dot(normed, w_qkv, preferred_element_type=jnp.float32)
    query_f, key_f, value_f = head_norms(projected)
    cotangent = out_cot[0].reshape(row_count, width_model).astype(jnp.float32)
    gated = (gate_row * cotangent).astype(jnp.bfloat16)
    grad_attn = lax.dot_general(
        gated, w_out, (((1,), (1,)), ((), ())), preferred_element_type=jnp.float32
    ).astype(jnp.bfloat16)

    def to_heads(token_rows):
        shaped = token_rows.reshape(row_split, part_rows, head_groups, group_width)
        return shaped.transpose(2, 0, 1, 3).reshape(seq_count, part_rows, group_width)

    def from_heads(head_rows):
        shaped = head_rows.reshape(head_groups, row_split, part_rows, group_width)
        return shaped.transpose(1, 2, 0, 3).reshape(row_count, inner_width)

    query_heads, grad_heads = (
        lax.all_to_all(
            to_heads(query_f.astype(jnp.bfloat16)), "seq", split_axis=0, concat_axis=0, tiled=True
        ),
        lax.all_to_all(to_heads(grad_attn), "seq", split_axis=0, concat_axis=0, tiled=True),
    )
    query_count = seq_count * part_rows
    query_heads = query_heads.reshape(query_count, per_device, HD)
    grad_heads = grad_heads.reshape(query_count, per_device, HD)
    stacked = jnp.stack(
        [
            key_f.astype(jnp.bfloat16).reshape(row_count, head_groups, group_width),
            value_f.astype(jnp.bfloat16).reshape(row_count, head_groups, group_width),
        ],
        axis=2,
    )
    by_group = stacked.transpose(1, 0, 2, 3).reshape(head_groups, row_count, 2 * group_width)
    copies = jnp.broadcast_to(
        by_group[:, None], (head_groups, row_split, row_count, 2 * group_width)
    )
    arrived = lax.all_to_all(
        copies.reshape(seq_count, row_count, 2 * group_width),
        "seq",
        split_axis=0,
        concat_axis=0,
        tiled=True,
    )
    key_value = arrived.reshape(seq_count * row_count, 2, per_device, HD)
    attn_heads, dquery, dkey, dvalue = attend_both(
        query_heads, grad_heads, key_value[:, 0], key_value[:, 1]
    )
    attn_tok = from_heads(
        lax.all_to_all(
            attn_heads.reshape(seq_count, part_rows, group_width),
            "seq",
            split_axis=0,
            concat_axis=0,
            tiled=True,
        )
    )
    projected_out = jnp.dot(attn_tok, w_out, preferred_element_type=jnp.float32)
    out_rows = (resid_f + gate_row * projected_out).astype(jnp.bfloat16)
    dquery_tok = from_heads(
        lax.all_to_all(
            dquery.reshape(seq_count, part_rows, group_width),
            "seq",
            split_axis=0,
            concat_axis=0,
            tiled=True,
        )
    )
    grads_kv = jnp.stack([dkey, dvalue], axis=1)
    returned = lax.all_to_all(
        grads_kv.reshape(seq_count, row_count, 2 * group_width).astype(jnp.bfloat16),
        "seq",
        split_axis=0,
        concat_axis=0,
        tiled=True,
    ).astype(jnp.float32)
    summed = jnp.sum(returned.reshape(head_groups, row_split, row_count, 2 * group_width), axis=1)
    grads_tok = (
        summed.reshape(head_groups, row_count, 2, group_width)
        .transpose(2, 1, 0, 3)
        .reshape(2, row_count, inner_width)
    )
    _, pullback = jax.vjp(head_norms, projected)
    (grad_projected,) = pullback((dquery_tok, grads_tok[0], grads_tok[1]))
    grad_proj_b = grad_projected.astype(jnp.bfloat16)
    grad_normed = lax.dot_general(
        grad_proj_b, w_qkv, (((1,), (1,)), ((), ())), preferred_element_type=jnp.float32
    )
    _, pull_norm = jax.vjp(lambda stream: modulate(stream, shift_row, scale_row), resid_f)
    (grad_stream,) = pull_norm(grad_normed)
    grad_resid = (
        (cotangent + grad_stream)
        .astype(jnp.bfloat16)
        .reshape(1, plane_count, side_y, side_x, width_model)
    )
    grad_padded = padded_2(grad_resid, (("seq", 1),), 1)[0]
    grad_tokens = (
        grad_resid[0].astype(jnp.float32) + depthwise(grad_padded, conv_kernel[::-1], plane_count)
    ).astype(jnp.bfloat16)
    local_terms = kernel_terms(padded, grad_resid[0], plane_count)
    norm_factor = 1.0 / math.sqrt(
        lax.axis_size("dp") * lax.axis_size("fsdp") * seq_count * row_count
    )
    grad_kernel = lax.psum(local_terms, ("seq", "dp", "fsdp")) * norm_factor
    return (out_rows.reshape(tokens.shape), grad_tokens.reshape(tokens.shape), grad_kernel)


def as_f32(value):
    return value.astype(jnp.float32)


def row_shift(value, step, inner):
    rows = value.shape[0]
    moved = pltpu.roll(value, step % rows, axis=0)
    place = lax.rem(lax.broadcasted_iota(jnp.int32, value.shape, 0), inner)
    return jnp.where(place == (0 if step == 1 else inner - 1), 0.0, moved)


def slab_shift(value, step, inner):
    if step == 0:
        return value
    empty = jnp.zeros((inner, value.shape[1]), value.dtype)
    if step == 1:
        return jnp.concatenate([empty, value[:-inner]], axis=0)
    return jnp.concatenate([value[inner:], empty], axis=0)


def conv_lanes(planes, taps, flipped, inner):
    by_x = []
    for tap_x in range(3):
        total = None
        for tap_y in range(3):
            part = None
            for tap_z, plane in planes.items():
                index = 9 * tap_z + 3 * tap_y + tap_x
                index = 26 - index if flipped else index
                term = taps[index : index + 1] * plane
                part = term if part is None else part + term
            part = slab_shift(part, 1 - tap_y, inner)
            total = part if total is None else total + part
        by_x.append(total)
    return by_x[1] + row_shift(by_x[0], 1, inner) + row_shift(by_x[2], -1, inner)


def sided(odd, near, far, body):
    pl.when(odd)(lambda: body(near, far))
    pl.when(jnp.logical_not(odd))(lambda: body(far, near))


def head_mean(value):
    width = value.shape[1]
    left = lax.broadcasted_iota(jnp.int32, (width, width), 0) // HD
    right = lax.broadcasted_iota(jnp.int32, (width, width), 1) // HD
    same = jnp.where(left == right, 1.0, 0.0).astype(jnp.bfloat16)
    high = value.astype(jnp.bfloat16)
    low = (value - as_f32(high)).astype(jnp.bfloat16)
    total = jnp.dot(high, same, preferred_element_type=jnp.float32)
    total = total + jnp.dot(low, same, preferred_element_type=jnp.float32)
    return total * (1.0 / HD)


def nt_dot(left, right):
    return lax.dot_general(
        left, right, (((1,), (1,)), ((), ())), preferred_element_type=jnp.float32
    )


def tn_dot(left, right):
    return lax.dot_general(
        left, right, (((0,), (0,)), ((), ())), preferred_element_type=jnp.float32
    )


def nn_dot(left, right):
    return jnp.dot(left, right, preferred_element_type=jnp.float32)


def front_body(slots, ids, feats, *rest):
    fetched = rest[:6]
    mod, wo_oth, sends = rest[6], rest[7], rest[8 : 8 + slots]
    by_group, wt_own, wt_oth, pxrd, wo_own, cot, arrive = rest[8 + slots :]
    held = (wt_own, wt_oth, pxrd, wo_own, wo_oth, cot)
    me, half = ids[0], ids[1]
    width = cot.shape[1]
    copies = [
        pltpu.make_async_copy(source, place, arrive.at[i])
        for i, (source, place) in enumerate(zip(fetched, held))
    ]
    for copy in copies:
        copy.start()
    for copy in copies[:3]:
        copy.wait()
    projected = nn_dot(feats[0], wt_own[...]) + nn_dot(feats[1], wt_oth[...])
    for row in range(3):
        cols = slice(row * width, (row + 1) * width)
        mod[row : row + 1, :] = projected[0:1, cols] + pxrd[row]
    for copy in copies[3:]:
        copy.wait()
    gated = (mod[2:3, :] * as_f32(cot[...])).astype(jnp.bfloat16)
    lanes = sends[0].shape[1]
    per_half = wo_own.shape[0] // lanes
    for weight, part in ((wo_own, half), (wo_oth, 1 - half)):
        grads = nt_dot(gated, weight[...]).astype(jnp.bfloat16)
        for j in range(per_half):
            by_group[part * per_half + j] = grads[:, j * lanes : (j + 1) * lanes]
    for k in range(slots):
        sends[k][...] = by_group[lax.bitwise_xor(me, gap_of(half, k))]


def own_conv_body(inner, tok_far, taps_far, out, tok, taps, arrive):
    @pl.when(lax.axis_index("fsdp") == 0)
    def work():
        copies = [
            pltpu.make_async_copy(tok_far, tok, arrive.at[0]),
            pltpu.make_async_copy(taps_far, taps, arrive.at[1]),
        ]
        for copy in copies:
            copy.start()
        for copy in copies:
            copy.wait()
        for start in range(0, tok.shape[1], 128):
            cols = slice(start, start + 128)
            plane = as_f32(tok[:, cols])
            out[:, cols] = plane + conv_lanes({1: plane}, taps[:, cols], False, inner)


def mix_body(slots, inner, ids, centre, tok, near, far, taps, mod, w_own, w_oth, *rest):
    resid, sections = rest[0], rest[1]
    sends = rest[2 : 2 + slots]
    normed, by_group, sums_ref = rest[2 + slots :]
    me, half = ids[0], ids[1]
    rows, width = tok.shape
    step = 128

    def all_planes(has_centre, before, after):
        sums = jnp.zeros((rows, step), jnp.float32)
        for start in range(0, width, step):
            cols = slice(start, start + step)
            planes = {0: as_f32(before[:, cols]), 2: as_f32(after[:, cols])}
            if has_centre:
                total = centre[:, cols]
            else:
                planes[1] = as_f32(tok[:, cols])
                total = planes[1]
            rounded = total + conv_lanes(planes, taps[:, cols], False, inner)
            rounded = rounded.astype(jnp.bfloat16)
            resid[:, cols] = rounded
            sums = sums + as_f32(rounded)
        sums_ref[...] = sums

    for has_centre in (True, False):

        @pl.when((half == 0) == has_centre)
        def work():
            sided(lax.rem(me, 2) == 1, near, far, functools.partial(all_planes, has_centre))

    sums = sums_ref[...]
    mean = jnp.sum(sums, axis=1, keepdims=True) * (1.0 / width)
    squares = jnp.zeros((rows, step), jnp.float32)
    for start in range(0, width, step):
        centre = as_f32(resid[:, start : start + step]) - mean
        squares = squares + centre * centre
    spread = jnp.sum(squares, axis=1, keepdims=True) * (1.0 / width)
    inverse = lax.rsqrt(spread + 1e-06)
    per_half = width // 2
    for start in range(0, width, step):
        cols = slice(start, start + step)
        centre = as_f32(resid[:, cols]) - mean
        value = centre * inverse * (1.0 + mod[1:2, cols]) + mod[0:1, cols]
        inside = start % per_half
        normed[start // per_half, :, inside : inside + step] = value.astype(jnp.bfloat16)
    projected = nn_dot(normed[half], w_own[...]) + nn_dot(normed[1 - half], w_oth[...])
    lanes = sends[0].shape[1] // 3
    inner_width = H * HD
    sections[...] = projected[:, : 2 * inner_width]
    for group in range(slots):
        for part in range(3):
            block = projected[:, part * inner_width + group * lanes :][:, :lanes]
            if part < 2:
                block = block * lax.rsqrt(head_mean(block * block) + 1e-06)
            by_group[group, :, part * lanes : (part + 1) * lanes] = block.astype(jnp.bfloat16)
    for k in range(slots):
        sends[k][...] = by_group[lax.bitwise_xor(me, gap_of(half, k))]


def attend_body(slots, *refs):
    qkv_in, grads_in = refs[:slots], refs[slots : 2 * slots]
    backs, attns = refs[2 * slots : 3 * slots], refs[3 * slots : 4 * slots]
    weights, probs, dscore = refs[4 * slots :]
    rows, lanes = grads_in[0].shape
    heads = lanes // HD
    count = slots * rows
    scale = 1.0 / math.sqrt(HD)
    step = 64
    zero = jnp.zeros((count, lanes), jnp.bfloat16)
    owner = lax.broadcasted_iota(jnp.int32, (count, lanes), 1) // HD
    masks = [owner == head for head in range(heads)]
    query = jnp.concatenate([ref[:, :lanes] for ref in qkv_in], axis=0)
    key = jnp.concatenate([ref[:, lanes : 2 * lanes] for ref in qkv_in], axis=0)
    value = jnp.concatenate([ref[:, 2 * lanes :] for ref in qkv_in], axis=0)
    grad = jnp.concatenate([ref[...] for ref in grads_in], axis=0)
    scaled = query * jnp.asarray(scale, jnp.bfloat16)
    for head in range(heads):
        weights[head] = nt_dot(jnp.where(masks[head], scaled, zero), key)
    for head in range(heads):
        for start in range(0, count, step):
            span = slice(start, start + step)
            expo = jnp.exp(weights[head, span, :])
            expo = expo * (1.0 / jnp.sum(expo, axis=1, keepdims=True))
            weights[head, span, :] = expo
            probs[span, head * count : (head + 1) * count] = expo.astype(jnp.bfloat16)
    values = jnp.concatenate([jnp.where(mask, value, zero) for mask in masks], axis=0)
    keys = jnp.concatenate([jnp.where(mask, key, zero) for mask in masks], axis=0)
    attn = nn_dot(probs[...], values).astype(jnp.bfloat16)
    for k in range(slots):
        attns[k][...] = attn[k * rows : (k + 1) * rows]
    product = as_f32(attn) * as_f32(grad)
    for head in range(heads):
        delta = jnp.sum(jnp.where(masks[head], product, 0.0), axis=1, keepdims=True)
        dprob = nt_dot(jnp.where(masks[head], grad, zero), value)
        for start in range(0, count, step):
            span = slice(start, start + step)
            part = weights[head, span, :] * (dprob[span] - delta[span])
            dscore[span, head * count : (head + 1) * count] = part.astype(jnp.bfloat16)
    dquery = nn_dot(dscore[...], keys) * scale
    dkeys, dvalues = None, None
    for head in range(heads):
        span = slice(head * count, (head + 1) * count)
        dkey = jnp.where(masks[head], tn_dot(dscore[:, span], scaled), 0.0)
        dvalue = jnp.where(masks[head], tn_dot(probs[:, span], grad), 0.0)
        dkeys = dkey if dkeys is None else dkeys + dkey
        dvalues = dvalue if dvalues is None else dvalues + dvalue
    for k in range(slots):
        span = slice(k * rows, (k + 1) * rows)
        for part, found in enumerate((dquery, dkeys, dvalues)):
            backs[k][:, part * lanes : (part + 1) * lanes] = found[span].astype(jnp.bfloat16)


def tail_body(slots, inner, ids, *refs):
    backs = refs[:slots]
    sections, resid, cot, mod, w_own, w_oth, tok, near_far, far_far = refs[slots : slots + 9]
    dresid, terms, by_group, dproj, dnormed, partial, near, far, arrive = refs[slots + 9 :]
    me, half = ids[0], ids[1]
    copies = [
        pltpu.make_async_copy(near_far, near, arrive.at[0]),
        pltpu.make_async_copy(far_far, far, arrive.at[1]),
    ]
    for copy in copies:
        copy.start()
    rows, width = resid.shape
    lanes = by_group.shape[3]
    inner_width = H * HD
    for k in range(slots):
        group = lax.bitwise_xor(me, gap_of(half, k))
        for part in range(3):
            by_group[group, part] = backs[k][:, part * lanes : (part + 1) * lanes]
    for group in range(slots):
        for part in range(3):
            start = part * inner_width + group * lanes
            grad = by_group[group, part]
            if part < 2:
                grad = as_f32(grad)
                block = sections[:, start : start + lanes]
                inverse = lax.rsqrt(head_mean(block * block) + 1e-06)
                unit = block * inverse
                grad = (inverse * (grad - unit * head_mean(grad * unit))).astype(jnp.bfloat16)
            dproj[:, start : start + lanes] = grad
    dnormed[half] = nt_dot(dproj[...], w_own[...])
    dnormed[1 - half] = nt_dot(dproj[...], w_oth[...])
    step = 128
    per_half = width // 2
    total = jnp.zeros((rows, step), jnp.float32)
    for start in range(0, width, step):
        total = total + as_f32(resid[:, start : start + step])
    mean = jnp.sum(total, axis=1, keepdims=True) * (1.0 / width)
    total = jnp.zeros((rows, step), jnp.float32)
    for start in range(0, width, step):
        centre = as_f32(resid[:, start : start + step]) - mean
        total = total + centre * centre
    inverse = lax.rsqrt(jnp.sum(total, axis=1, keepdims=True) * (1.0 / width) + 1e-06)
    plain = jnp.zeros((rows, step), jnp.float32)
    crossed = jnp.zeros((rows, step), jnp.float32)
    for start in range(0, width, step):
        cols = slice(start, start + step)
        inside = start % per_half
        grad = dnormed[start // per_half, :, inside : inside + step] * (1.0 + mod[1:2, cols])
        unit = (as_f32(resid[:, cols]) - mean) * inverse
        plain = plain + grad
        crossed = crossed + grad * unit
    plain = jnp.sum(plain, axis=1, keepdims=True) * (1.0 / width)
    crossed = jnp.sum(crossed, axis=1, keepdims=True) * (1.0 / width)
    for start in range(0, width, step):
        cols = slice(start, start + step)
        inside = start % per_half
        grad = dnormed[start // per_half, :, inside : inside + step] * (1.0 + mod[1:2, cols])
        unit = (as_f32(resid[:, cols]) - mean) * inverse
        stream = as_f32(cot[:, cols]) + inverse * (grad - plain - unit * crossed)
        dresid[:, cols] = stream.astype(jnp.bfloat16)
    for copy in copies:
        copy.wait()
    outer = functools.partial(tap_terms, inner, dresid, tok, partial)
    sided(lax.rem(me, 2) == 1, near, far, outer)
    count = terms.shape[0]
    total = partial[pl.ds(0, count, stride=8), :]
    for i in range(1, 8):
        total = total + partial[pl.ds(i, count, stride=8), :]
    terms[...] = total.astype(terms.dtype)


def tap_terms(inner, dresid, tok, partial, before, after):
    rows, width = dresid.shape
    step = 128
    for start in range(0, width, step):
        cols = slice(start, start + step)
        grad = as_f32(dresid[:, cols])
        moved = [row_shift(grad, -1, inner), grad, row_shift(grad, 1, inner)]
        base = 27 * (start // step)
        for tap_z, ref in enumerate((before, tok, after)):
            plane = as_f32(ref[:, cols])
            for tap_y in range(3):
                low, high = max(0, 1 - tap_y), max(0, tap_y - 1)
                for tap_x in range(3):
                    prod = (
                        plane[high * inner : rows - low * inner]
                        * moved[tap_x][low * inner : rows - high * inner]
                    )
                    row = 8 * (base + 9 * tap_z + 3 * tap_y + tap_x)
                    partial[row : row + 8, :] = jnp.sum(prod.reshape(-1, 8, step), axis=0)


def out_body(slots, ids, *refs):
    attns = refs[:slots]
    resid, mod, wo_own, wo_oth, out, by_group = refs[slots:]
    me, half = ids[0], ids[1]
    lanes = attns[0].shape[1]
    per_half = wo_own.shape[0] // lanes
    for k in range(slots):
        by_group[lax.bitwise_xor(me, gap_of(half, k))] = attns[k][...]
    total = None
    for weight, part in ((wo_own, half), (wo_oth, 1 - half)):
        for j in range(per_half):
            term = nn_dot(by_group[part * per_half + j], weight[j * lanes : (j + 1) * lanes, :])
            total = term if total is None else total + term
    out[...] = (as_f32(resid[...]) + mod[2:3, :] * total).astype(jnp.bfloat16)


def back_conv_body(inner, ids, grad, near, far, taps, out):
    width = grad.shape[1]
    step = 128

    def all_planes(before, after):
        for start in range(0, width, step):
            cols = slice(start, start + step)
            planes = {i: as_f32(ref[:, cols]) for i, ref in enumerate((before, grad, after))}
            mixed = conv_lanes(planes, taps[:, cols], True, inner)
            out[:, cols] = (planes[1] + mixed).astype(jnp.bfloat16)

    sided(lax.rem(ids[0], 2) == 1, near, far, all_planes)


def tree_sum(values):
    while len(values) > 1:
        values = [values[i] + values[i + 1] for i in range(0, len(values), 2)]
    return values[0]


def sum_body(*refs):
    out = refs[-1]
    out[...] = tree_sum([as_f32(ref[...]) for ref in refs[:-1]]).astype(out.dtype)


def final_body(factor, left, right, out):
    total = (left[...] + right[...]) * factor
    lanes = total.shape[1]
    for block in range(out.shape[1] // lanes):
        out[:, block * lanes : (block + 1) * lanes] = total[27 * block : 27 * (block + 1)]


def call(body, name, outs, args, scratch=(), flops=0, scalars=False, far_args=(), vmem=16):
    whole = pl.BlockSpec(memory_space=pltpu.VMEM)
    specs = [whole] * len(args)
    if scalars:
        specs[0] = pl.BlockSpec(memory_space=pltpu.SMEM)
    for i in far_args:
        specs[i] = pl.BlockSpec(memory_space=pltpu.HBM)
    sizes = [math.prod(a.shape) * a.dtype.itemsize for a in list(args) + list(outs)]
    args = [
        pltpu.with_memory_space_constraint(a, pltpu.HBM) if i in far_args else a
        for i, a in enumerate(args)
    ]
    return pl.pallas_call(
        body,
        out_shape=tuple(outs),
        in_specs=specs,
        out_specs=(whole,) * len(outs),
        scratch_shapes=list(scratch),
        compiler_params=pltpu.CompilerParams(vmem_limit_bytes=vmem * 2**20),
        cost_estimate=pl.CostEstimate(flops=flops, bytes_accessed=sum(sizes), transcendentals=0),
        name=name,
    )(*args)


def swapped(value, axis, distance):
    count = lax.axis_size(axis)
    return lax.ppermute(value, axis, [(i, i ^ distance) for i in range(count)])


ORDERS = ((0, 1, 3, 2), (0, 2, 3, 1))


def gap_of(half, k):
    return jnp.where(half == 0, ORDERS[0][k], ORDERS[1][k])


def exchanged(pieces):
    seqs, cores = lax.axis_size("seq"), lax.axis_size("fsdp")
    received = [pieces[0]]
    for k in range(1, len(pieces)):
        pairs = [
            (cores * z + core, cores * (z ^ ORDERS[core][k]) + core)
            for z in range(seqs)
            for core in range(cores)
        ]
        received.append(lax.ppermute(pieces[k], ("seq", "fsdp"), pairs))
    return received


def neighbours(value):
    count = lax.axis_size("seq")
    near = swapped(value, "seq", 1)
    middle = [(i, i + 1) for i in range(1, count - 1, 2)]
    return near, lax.ppermute(value, "seq", middle + [(j, i) for i, j in middle])


def slab_shards(
    tokens, timesteps, pxrd_mod, time_weight, conv_kernel, qkv_weight, out_weight, out_cot
):
    bf16, f32 = jnp.bfloat16, jnp.float32
    side_y, inner, width = tokens.shape[2:]
    rows = side_y * inner
    slots = lax.axis_size("seq")
    lanes = H * HD // slots
    me = lax.axis_index("seq")
    half = lax.axis_index("fsdp")
    ids = jnp.stack([me, half]).astype(jnp.int32)
    tok = tokens.reshape(rows, width)
    cot = out_cot.reshape(rows, width)
    shape = jax.ShapeDtypeStruct

    wo_oth = swapped(out_weight, "fsdp", 1)
    wt_oth = swapped(time_weight, "fsdp", 1)
    (centre,) = call(
        functools.partial(own_conv_body, inner),
        "own_conv",
        [shape((rows, width), f32)],
        (tok, conv_kernel),
        [
            pltpu.VMEM((rows, width), bf16),
            pltpu.VMEM(conv_kernel.shape, f32),
            pltpu.SemaphoreType.DMA((2,)),
        ],
        far_args=(0, 1),
    )
    tok_sent, centre = lax.optimization_barrier((tok, centre))
    near, far = neighbours(pltpu.with_memory_space_constraint(tok_sent, pltpu.HBM))
    wq_oth = swapped(qkv_weight, "fsdp", 1)

    freq = 2 * time_weight.shape[0]
    feats = time_features(timesteps, freq).reshape(2, freq // 2)
    own = lax.dynamic_slice_in_dim(feats, half, 1, axis=0)
    oth = lax.dynamic_slice_in_dim(feats, 1 - half, 1, axis=0)
    feats = jnp.broadcast_to(jnp.stack([own, oth]), (2, 8, freq // 2))
    pxrd_rows = pxrd_mod.transpose(1, 0, 2)
    front = call(
        functools.partial(front_body, slots),
        "front",
        [shape((3, width), f32), shape(out_weight.shape, bf16)]
        + [shape((rows, lanes), bf16)] * slots,
        (ids, feats, time_weight, wt_oth, pxrd_rows, out_weight, wo_oth, cot),
        [pltpu.VMEM((slots, rows, lanes), bf16)]
        + [pltpu.VMEM(time_weight.shape, bf16)] * 2
        + [pltpu.VMEM(pxrd_rows.shape, f32)]
        + [pltpu.VMEM(out_weight.shape, bf16)]
        + [pltpu.VMEM((rows, width), bf16), pltpu.SemaphoreType.DMA((6,))],
        far_args=range(2, 8),
        flops=2 * rows * width * H * HD,
        scalars=True,
    )
    mod, wo_held = front[:2]
    grads_in = exchanged(front[2:])

    mixed = call(
        functools.partial(mix_body, slots, inner),
        "mix",
        [shape((rows, width), bf16), shape((rows, 2 * H * HD), f32)]
        + [shape((rows, 3 * lanes), bf16)] * slots,
        (ids, centre, tok, near, far, conv_kernel, mod, qkv_weight, wq_oth),
        [
            pltpu.VMEM((2, rows, width // 2), bf16),
            pltpu.VMEM((slots, rows, 3 * lanes), bf16),
            pltpu.VMEM((rows, 128), f32),
        ],
        flops=2 * rows * width * 3 * H * HD,
        scalars=True,
    )
    resid, sections = mixed[:2]
    sends, grads_in = lax.optimization_barrier((mixed[2:], grads_in))
    qkv_in = exchanged(sends)
    count = slots * rows
    attended = call(
        functools.partial(attend_body, slots),
        "attend",
        [shape((rows, 3 * lanes), bf16)] * slots + [shape((rows, lanes), bf16)] * slots,
        (*qkv_in, *grads_in),
        [
            pltpu.VMEM((lanes // HD, count, count), f32),
            pltpu.VMEM((count, lanes // HD * count), bf16),
            pltpu.VMEM((count, lanes // HD * count), bf16),
        ],
        flops=12 * count * count * lanes,
    )
    backs = exchanged(attended[:slots])
    attns = exchanged(attended[slots:])
    dresid, terms = call(
        functools.partial(tail_body, slots, inner),
        "tail",
        [shape((rows, width), bf16), shape((27 * width // 128, 128), bf16)],
        (ids, *backs, sections, resid, cot, mod, qkv_weight, wq_oth, tok, near, far),
        [
            pltpu.VMEM((slots, 3, rows, lanes), bf16),
            pltpu.VMEM((rows, 3 * H * HD), bf16),
            pltpu.VMEM((2, rows, width // 2), f32),
            pltpu.VMEM((8 * 27 * width // 128, 128), f32),
            pltpu.VMEM((rows, width), bf16),
            pltpu.VMEM((rows, width), bf16),
            pltpu.SemaphoreType.DMA((2,)),
        ],
        flops=2 * rows * width * 3 * H * HD,
        scalars=True,
        far_args=(slots + 8, slots + 9),
    )
    dresid, attns = lax.optimization_barrier((dresid, attns))
    (out,) = call(
        functools.partial(out_body, slots),
        "out",
        [shape((rows, width), bf16)],
        (ids, *attns, resid, mod, out_weight, wo_held),
        [pltpu.VMEM((slots, rows, lanes), bf16)],
        flops=2 * rows * width * H * HD,
        scalars=True,
    )
    grad_near, grad_far = neighbours(dresid)
    other = swapped(terms, "dp", 1)
    (terms,) = call(sum_body, "add_dp", [shape(terms.shape, bf16)], (terms, other))
    (token_grad,) = call(
        functools.partial(back_conv_body, inner),
        "back_conv",
        [shape((rows, width), bf16)],
        (ids, dresid, grad_near, grad_far, conv_kernel),
        scalars=True,
    )
    factor = 1.0 / math.sqrt(lax.axis_size("dp") * lax.axis_size("fsdp") * slots * rows)
    pieces = exchanged([terms] * slots)
    pieces[-1], token_grad, out = lax.optimization_barrier((pieces[-1], token_grad, out))
    (summed,) = call(sum_body, "add_seq", [shape(terms.shape, f32)], pieces)
    (kernel_grad,) = call(
        functools.partial(final_body, factor),
        "final",
        [shape((27, width), f32)],
        (summed, swapped(summed, "fsdp", 1)),
    )
    return out.reshape(tokens.shape), token_grad.reshape(tokens.shape), kernel_grad


def solution(mesh):
    count = mesh.shape["seq"]

    def pick(*args):
        tokens, time_weight = args[0], args[3]
        lanes = H * HD // count
        fits = (
            count == 4
            and tokens.shape[0] == 1
            and tokens.shape[1] == 1
            and tokens.shape[3] % 16 == 0
            and lanes % 128 == 0
            and mesh.shape["dp"] == 2
            and mesh.shape["fsdp"] == 2
        )
        return slab_shards(*args) if fits else shards(*args)

    placed = (
        P(("groups", "dp", "fsdp"), "seq", None, None, None),
        P(("groups", "dp", "fsdp")),
        P(("groups", "dp", "fsdp"), None, None),
        P("fsdp", None),
        P(),
        P("fsdp", None),
        P("fsdp", None),
        P(("groups", "dp", "fsdp"), "seq", None, None, None),
    )
    return jax.shard_map(
        pick,
        mesh=mesh,
        in_specs=placed,
        out_specs=(
            P(("groups", "dp", "fsdp"), "seq", None, None, None),
            P(("groups", "dp", "fsdp"), "seq", None, None, None),
            P("groups", None),
        ),
        check_vma=False,
    )
```
